32 devices in a mesh: space: 8 (over y, x, core), dp: 4 (over z).
Axes of the slice: x: 2, y: 2, z: 4, core: 2. Of those that a mesh axis runs over, the one named last changes fastest.
Arguments:
- features: bfloat16 [8, 48, 72, 2048], P('dp', 'space'), may hold values from -6 to 6
- pointwise: bfloat16 [2, 2048, 256], P(None, 'dp'), may hold values from -0.125 to 0.125
- depthwise: bfloat16 [2, 9, 2048], P(None, None, 'dp'), may hold values from -2 to 2
- cotangent: bfloat16 [8, 48, 72, 512], P('dp', 'space'), may hold values from -6 to 6
Outputs:
- branches_out: bfloat16 [8, 48, 72, 512], P('dp', 'space')
- feature_grad: bfloat16 [8, 48, 72, 2048], P('dp', 'space')
- pointwise_grad: float32 [2, 2048, 256], P(None, 'dp')
- depthwise_grad: float32 [2, 9, 2048], P(None, None, 'dp')
The draws below stay inside these ranges and needn't reach their ends.
All inputs are finite; a program needn't handle non-finite values.
Results may differ from the reference program's by a relative error of at most 0.014.
Values may be sent and summed in bfloat16 or wider, within the bound.
No kernel may reach another device: no remote copies, remote signals or barrier semaphores. Data moves between devices by JAX's collectives and lax.ppermute only.
A program may use at most 64 MiB of HBM per device.

```python
import jax
import jax.numpy as jnp
from jax import lax

C = 2048
CO = 256
H = 48
W = 72
RATE_A = 12
RATE_B = 24
IMG_DEV = 2
IMAGES = 8
N_SPACE = 8
N_DP = 4


def raised(array, own_key, source, target, blocks, factor):
    owner, partner = [(jnp.arange(array.shape[axis_at]) // (array.shape[axis_at] // blocks)).reshape([-1 if axis == axis_at else 1 for axis in range(array.ndim)]) for axis_at in (source, target)]
    chosen = jax.random.permutation(own_key, blocks)[partner]
    strong = (owner == chosen) | (owner == (partner + blocks // 2) % blocks)
    return jnp.where(strong, factor * array, array)


def steps_of(rng, dims, pieces, smallest, top_value):
    level, own = 1.0, jax.random.fold_in(rng, 6)
    for dim, parts in pieces:
        draws = jnp.exp(jax.random.uniform(jax.random.fold_in(own, dim), (parts,), jnp.float32, smallest / len(pieces), top_value / len(pieces)))
        level = level * jnp.repeat(draws, dims[dim] // parts).reshape([-1 if axis == dim else 1 for axis in range(len(dims))])
    return level


def bell_draw(rng, extent, deviation, reach, pieces=(), held_as=jnp.bfloat16):
    gain = steps_of(rng, extent, pieces, -0.22, 0.18) if pieces else 1.0
    drawn = jax.random.normal(rng, extent, jnp.float32) * deviation * gain
    return jnp.minimum(jnp.maximum(drawn, -reach), reach).astype(held_as)


def bell_draw_with(stream_key, shape, deviation, bound, pieces, heavy, held_as=jnp.bfloat16):
    array = deviation * jax.random.normal(stream_key, shape, jnp.float32)
    if pieces:
        array = array * steps_of(stream_key, shape, pieces, -0.22, 0.18)
    return jnp.clip(raised(array, jax.random.fold_in(stream_key, 3), *heavy), -bound, bound).astype(held_as)


def setup_inputs(seed: int = 0) -> dict:
    key_of = jax.random.split(jax.random.key(seed), 5)
    features = bell_draw_with(key_of[0], (IMAGES, H, W, C), 1.0, 6.0, ((0, 4), (1, 8)), (0, 3, 4, 2.0))
    pointwise = bell_draw(key_of[1], (2, C, CO), C ** -0.5, 0.125, ((1, 4),))
    depthwise = bell_draw(key_of[2], (2, 9, C), 0.33, 2.0, ((2, 4),))
    cotangent = bell_draw(key_of[3], (IMAGES, H, W, 2 * CO), 1.0, 6.0, ((0, 4), (1, 8)))
    return dict(features=features, pointwise=pointwise, depthwise=depthwise, cotangent=cotangent)


def shifted(field, rate, up, side):
    padded = jnp.pad(field, ((0, 0), (rate, rate), (rate, rate), (0, 0)))
    row_start = rate + up * rate
    col_start = rate + side * rate
    return padded[:, row_start:row_start + H, col_start:col_start + W, :]

def group_pass(feat_group, cot_group, pointwise, depthwise):
    rows_dev = H // N_SPACE
    outputs = []
    grad_total = jnp.zeros(feat_group.shape, jnp.float32)
    w_parts = []
    k_parts = []
    for branch, rate in enumerate((RATE_A, RATE_B)):
        dsum = jnp.zeros(feat_group.shape, jnp.float32)
        for up in (-1, 0, 1):
            for side in (-1, 0, 1):
                tap = (up + 1) * 3 + (side + 1)
                dsum = dsum + shifted(feat_group, rate, up, side).astype(jnp.float32) * depthwise[branch, tap].astype(jnp.float32)
        dconv = dsum.astype(jnp.bfloat16)
        flat = dconv.reshape(-1, C)
        pre = jnp.dot(flat, pointwise[branch], preferred_element_type=jnp.float32)
        sig = jax.nn.sigmoid(pre)
        outputs.append((pre * sig).reshape(IMG_DEV, H, W, CO).astype(jnp.bfloat16))
        cot_part = cot_group[..., branch * CO:(branch + 1) * CO].reshape(-1, CO).astype(jnp.float32)
        gpre = (cot_part * sig * (1.0 + pre * (1.0 - sig))).astype(jnp.bfloat16)
        gdconv = lax.dot_general(gpre, pointwise[branch], (((1,), (1,)), ((), ())), preferred_element_type=jnp.float32).astype(jnp.bfloat16)
        gdconv = gdconv.reshape(feat_group.shape)
        blocks_d = dconv.reshape(IMG_DEV, N_SPACE, rows_dev, W, C).astype(jnp.float32)
        blocks_g = gpre.reshape(IMG_DEV, N_SPACE, rows_dev, W, CO).astype(jnp.float32)
        wblock = jnp.einsum('asrwc,asrwo->sco', blocks_d, blocks_g)
        w_parts.append(lax.optimization_barrier(jnp.sum(wblock.astype(jnp.bfloat16).astype(jnp.float32), axis=0)))
        gd_blocks = gdconv.reshape(IMG_DEV, N_SPACE, rows_dev, W, C).astype(jnp.float32)
        tap_rows = []
        for up in (-1, 0, 1):
            for side in (-1, 0, 1):
                tap = (up + 1) * 3 + (side + 1)
                src = shifted(feat_group, rate, up, side).reshape(IMG_DEV, N_SPACE, rows_dev, W, C).astype(jnp.float32)
                kblock = lax.optimization_barrier(jnp.sum(src * gd_blocks, axis=(0, 2, 3)))
                tap_rows.append(lax.optimization_barrier(jnp.sum(kblock.astype(jnp.bfloat16).astype(jnp.float32), axis=0)))
                grad_total = grad_total + shifted(gdconv, rate, -up, -side).astype(jnp.float32) * depthwise[branch, tap].astype(jnp.float32)
        k_parts.append(jnp.stack(tap_rows))
    joined = jnp.concatenate(outputs, axis=-1)
    return (joined, grad_total.astype(jnp.bfloat16), jnp.stack(w_parts), jnp.stack(k_parts))

def reference(features, pointwise, depthwise, cotangent):
    feat_groups = features.reshape(N_DP, IMG_DEV, H, W, C)
    cot_groups = cotangent.reshape(N_DP, IMG_DEV, H, W, 2 * CO)

    def one_group(pair):
        return group_pass(pair[0], pair[1], pointwise, depthwise)
    joined, grads, w_sums, k_sums = lax.map(one_group, (feat_groups, cot_groups))
    factor = 1.0 / jnp.sqrt(jnp.float32(IMG_DEV * N_DP * H * W))
    branches_out = joined.reshape(IMG_DEV * N_DP, H, W, 2 * CO)
    feature_grad = grads.reshape(IMG_DEV * N_DP, H, W, C)
    pointwise_grad = lax.optimization_barrier(jnp.sum(w_sums, axis=0)) * factor
    depthwise_grad = lax.optimization_barrier(jnp.sum(k_sums, axis=0)) * factor
    return (branches_out, feature_grad, pointwise_grad, depthwise_grad)
```

```python
import functools
import math

import jax
import jax.numpy as jnp
from jax import lax
from jax.experimental import pallas as pl
from jax.experimental.pallas import tpu as pltpu
from jax.sharding import PartitionSpec as P

RATES = (12, 24)
SIDES = (-1, 0, 1)
F32 = jnp.float32
BF16 = jnp.bfloat16
TAP_ROWS = 32


def shift(value, axis, steps):
    count = lax.axis_size(axis)
    first, last = max(0, -steps), min(count, count - steps)
    return lax.ppermute(value, axis, [(i, i + steps) for i in range(first, last)])


def cycle(value, axis, steps):
    count = lax.axis_size(axis)
    return lax.ppermute(value, axis, [(i, (i + steps) % count) for i in range(count)])


def swap(value, axis, mask):
    count = lax.axis_size(axis)
    return lax.ppermute(value, axis, [(i, i ^ mask) for i in range(count)])


def to_slabs(field, grain):
    n, rows, width, ch = field.shape
    parts = field.reshape(n, rows, width // grain, grain, ch)
    return parts.transpose(2, 0, 1, 3, 4).reshape(-1, ch)


def from_slabs(flat, shape, grain):
    n, rows, width, ch = shape
    parts = flat.reshape(width // grain, n, rows, grain, ch)
    return parts.transpose(1, 2, 0, 3, 4).reshape(shape)


def span(slabs, move):
    return max(0, -move), min(slabs, slabs - move)


def forward_kernel(terms, centre, slabs, idx_ref, x_ref, k_ref, w_ref, *refs):
    outs, acc = refs[: len(terms)], refs[len(terms)]
    step = pl.program_id(0)
    size = x_ref.shape[0] // slabs

    @pl.when(step == 0)
    def _():
        acc[...] = jnp.zeros_like(acc)

    for t, (branch, _, reach) in enumerate(terms):
        taps = [k_ref[0, 3 * t + i : 3 * t + i + 1, :] for i in range(3)]
        weight = w_ref[0, branch]
        pieces = []
        for q in range(slabs):
            total = None
            for i, side in enumerate(SIDES):
                src = q + side * reach
                if 0 <= src < slabs:
                    term = x_ref[src * size : (src + 1) * size, :].astype(F32) * taps[i]
                    total = term if total is None else total + term
            pieces.append(total.astype(BF16))
        field = jnp.concatenate(pieces, axis=0)
        acc[t] += jnp.dot(field, weight, preferred_element_type=F32)

    @pl.when(step == pl.num_programs(0) - 1)
    def _():
        for t in range(len(terms)):
            outs[t][...] = acc[t].astype(outs[t].dtype)


def forward(terms, slabs, idx, x, k, w):
    cells, channels = x.shape
    blocks, _, own, co = w.shape
    dtypes = [F32 if u == 0 else BF16 for _, u, _ in terms]
    return pl.pallas_call(
        functools.partial(forward_kernel, terms, None, slabs),
        grid_spec=pltpu.PrefetchScalarGridSpec(
            num_scalar_prefetch=1,
            grid=(blocks,),
            in_specs=[
                pl.BlockSpec((cells, own), lambda d, s: (0, s[3 + d])),
                pl.BlockSpec((1, k.shape[1], own), lambda d, s: (d, 0, 0)),
                pl.BlockSpec((1, 2, own, co), lambda d, s: (d, 0, 0, 0)),
            ],
            out_specs=[pl.BlockSpec((cells, co), lambda d, s: (0, 0)) for _ in terms],
            scratch_shapes=[pltpu.VMEM((len(terms), cells, co), F32)],
        ),
        out_shape=[jax.ShapeDtypeStruct((cells, co), dt) for dt in dtypes],
        compiler_params=pltpu.CompilerParams(vmem_limit_bytes=60 << 20),
        cost_estimate=pl.CostEstimate(
            flops=2 * len(terms) * cells * channels * co,
            bytes_accessed=2 * cells * channels + 2 * 2 * channels * co,
            transcendentals=0,
        ),
        name="forward_terms",
    )(idx, x, k, w)


def columns_of(terms, slabs, size, g_refs, gi):
    co = g_refs[0].shape[1]
    cells = slabs * size
    for t, (_, _, reach) in enumerate(terms):
        for i, side in enumerate(SIDES):
            lanes = slice((3 * t + i) * co, (3 * t + i + 1) * co)
            lo, hi = span(slabs, -side * reach)
            if lo > 0:
                gi[0 : lo * size, lanes] = jnp.zeros((lo * size, co), BF16)
            if hi * size < gi.shape[0]:
                gi[hi * size :, lanes] = jnp.zeros((gi.shape[0] - hi * size, co), BF16)
            a = lo - side * reach
            gi[lo * size : hi * size, lanes] = g_refs[t][a * size : (a + hi - lo) * size, :]
    del cells


def weight_kernel(terms, slabs, size, halves, quarters, last, idx_ref, xt_ref, kc_ref, w_ref, *refs):
    n = len(terms)
    g_refs = refs[:n]
    refs = refs[n:]
    if last:
        before_w, before_k, out_ref, gi, wacc, kacc = refs
    else:
        out_w, out_k, gi, wacc, kacc = refs
    own, co = w_ref.shape[2], w_ref.shape[3]

    @pl.when(pl.program_id(0) == 0)
    def _():
        columns_of(terms, slabs, size, g_refs, gi)

    if last:
        wacc[...] = before_w[0]
        kacc[...] = before_k[0]
    else:
        wacc[...] = jnp.zeros_like(wacc)
        kacc[...] = jnp.zeros_like(kacc)
    upper = idx_ref[2] > 0
    for t, (branch, u, _) in enumerate(terms):
        for i in range(3):
            col = 3 * t + i
            part = jnp.dot(
                xt_ref[...], gi[:, col * co : (col + 1) * co], preferred_element_type=F32
            )
            wacc[branch] += part * kc_ref[0, :, col : col + 1]
            total = jnp.sum(part * w_ref[0, branch].astype(F32), axis=1, keepdims=True)
            row = branch * 9 + i
            if u is None:
                kacc[:, row : row + 1] = jnp.where(upper, 0.0, total)
                kacc[:, row + 6 : row + 7] = jnp.where(upper, total, 0.0)
            else:
                at = row + 3 * (u + 1)
                kacc[:, at : at + 1] = total
    if not last:
        out_w[0] = wacc[...]
        out_k[0] = kacc[...]
        return
    taps = kacc[...].T
    part_c = own // halves
    piece = part_c // quarters
    rows = TAP_ROWS // quarters
    for h in range(halves):
        for q in range(quarters):
            at_h = h ^ idx_ref[0] if halves > 1 else 0
            at_q = q ^ idx_ref[1] if quarters > 1 else 0
            base = h * part_c + q * piece
            for branch in range(2):
                out_ref[0, at_h, at_q, branch * piece : (branch + 1) * piece, :] = wacc[
                    branch, base : base + piece, :
                ].astype(BF16)
            block = taps[q * rows : (q + 1) * rows, h * part_c : (h + 1) * part_c]
            if part_c < co:
                block = jnp.concatenate([block, jnp.zeros((rows, co - part_c), F32)], axis=1)
            out_ref[0, at_h, at_q, 2 * piece :, :] = block.astype(BF16)


def weight_grads(terms, slabs, size, halves, quarters, idx, xt, kc, w, gs, before=None):
    blocks, _, own, co = w.shape
    padded = xt.shape[1]
    last = before is not None
    in_specs = [
        pl.BlockSpec((own, padded), lambda d, s: (s[3 + d], 0)),
        pl.BlockSpec((1,) + kc.shape[1:], lambda d, s: (d, 0, 0)),
        pl.BlockSpec((1, 2, own, co), lambda d, s: (d, 0, 0, 0)),
    ] + [pl.BlockSpec(g.shape, lambda d, s: (0, 0)) for g in gs]
    args = [xt, kc, w, *gs]
    wide = [
        pl.BlockSpec((1, 2, own, co), lambda d, s: (d, 0, 0, 0)),
        pl.BlockSpec((1, own, 128), lambda d, s: (d, 0, 0)),
    ]
    if last:
        rows = (2 * (own // halves) + TAP_ROWS) // quarters
        in_specs += wide
        args += list(before)
        out_specs = pl.BlockSpec((1, halves, quarters, rows, co), lambda d, s: (d, 0, 0, 0, 0))
        out_shape = jax.ShapeDtypeStruct((blocks, halves, quarters, rows, co), BF16)
    else:
        out_specs = wide
        out_shape = [
            jax.ShapeDtypeStruct((blocks, 2, own, co), F32),
            jax.ShapeDtypeStruct((blocks, own, 128), F32),
        ]
    return pl.pallas_call(
        functools.partial(weight_kernel, terms, slabs, size, halves, quarters, last),
        grid_spec=pltpu.PrefetchScalarGridSpec(
            num_scalar_prefetch=1,
            grid=(blocks,),
            in_specs=in_specs,
            out_specs=out_specs,
            scratch_shapes=[
                pltpu.VMEM((padded, 3 * len(terms) * co), BF16),
                pltpu.VMEM((2, own, co), F32),
                pltpu.VMEM((own, 128), F32),
            ],
        ),
        out_shape=out_shape,
        compiler_params=pltpu.CompilerParams(vmem_limit_bytes=60 << 20),
        cost_estimate=pl.CostEstimate(
            flops=6 * len(terms) * padded * own * blocks * co,
            bytes_accessed=2 * own * blocks * padded + 8 * own * blocks * co,
            transcendentals=0,
        ),
        name="weight_terms_last" if last else "weight_terms",
    )(idx, *args)


def feature_kernel(terms, slabs, size, last, idx_ref, k_ref, wt_ref, *refs):
    n = len(terms)
    g_refs = refs[:n]
    refs = refs[n:]
    if last:
        before, out_ref, gi, kw = refs
    else:
        out_ref, gi, kw = refs
    co = wt_ref.shape[2]

    @pl.when(pl.program_id(0) == 0)
    def _():
        columns_of(terms, slabs, size, g_refs, gi)

    for t, (branch, _, _) in enumerate(terms):
        weight = wt_ref[0, branch].astype(F32)
        for i in range(3):
            col = 3 * t + i
            kw[col * co : (col + 1) * co, :] = (weight * k_ref[0, col : col + 1, :]).astype(BF16)

    def chunk(q, carry):
        rows = pl.ds(q * size, size)
        part = jnp.dot(gi[rows, :], kw[...], preferred_element_type=F32)
        if last:
            part = part + before[rows, :]
        out_ref[rows, :] = part.astype(out_ref.dtype)
        return carry

    lax.fori_loop(0, slabs, chunk, 0)


def feature_grads(terms, slabs, size, idx, k, wt, gs, before=None):
    blocks, _, co, own = wt.shape
    cells = slabs * size
    last = before is not None
    block = pl.BlockSpec((cells, own), lambda d, s: (0, s[3 + d]))
    in_specs = [
        pl.BlockSpec((1,) + k.shape[1:], lambda d, s: (d, 0, 0)),
        pl.BlockSpec((1, 2, co, own), lambda d, s: (d, 0, 0, 0)),
    ] + [pl.BlockSpec(g.shape, lambda d, s: (0, 0)) for g in gs]
    args = [k, wt, *gs]
    if last:
        in_specs.append(block)
        args.append(before)
    return pl.pallas_call(
        functools.partial(feature_kernel, terms, slabs, size, last),
        grid_spec=pltpu.PrefetchScalarGridSpec(
            num_scalar_prefetch=1,
            grid=(blocks,),
            in_specs=in_specs,
            out_specs=block,
            scratch_shapes=[
                pltpu.VMEM((cells, 3 * len(terms) * co), BF16),
                pltpu.VMEM((3 * len(terms) * co, own), BF16),
            ],
        ),
        out_shape=jax.ShapeDtypeStruct((cells, own * blocks), BF16 if last else F32),
        compiler_params=pltpu.CompilerParams(vmem_limit_bytes=60 << 20),
        cost_estimate=pl.CostEstimate(
            flops=6 * len(terms) * cells * own * blocks * co,
            bytes_accessed=6 * own * blocks * cells,
            transcendentals=0,
        ),
        name="feature_terms_last" if last else "feature_terms",
    )(idx, *args)


def finish_kernel(factor, idx_ref, in_ref, w_ref, k_ref):
    piece = w_ref.shape[3]
    for branch in range(2):
        rows = in_ref[0, 0, branch * piece : (branch + 1) * piece, :]
        w_ref[branch, 0, 0] = rows.astype(F32) * factor
    k_ref[...] = in_ref[0, 0, 2 * piece :, : k_ref.shape[1]].astype(F32) * factor


def finish(idx, pieces, own, factor):
    halves, quarters, rows, co = pieces.shape
    part_c = own // halves
    piece = part_c // quarters

    def place(h, q, s):
        return (h ^ s[0] if halves > 1 else h, q ^ s[1] if quarters > 1 else q, 0, 0)

    w, k = pl.pallas_call(
        functools.partial(finish_kernel, factor),
        grid_spec=pltpu.PrefetchScalarGridSpec(
            num_scalar_prefetch=1,
            grid=(halves, quarters),
            in_specs=[pl.BlockSpec((1, 1, rows, co), place)],
            out_specs=[
                pl.BlockSpec((2, 1, 1, piece, co), lambda h, q, s: (0, h, q, 0, 0)),
                pl.BlockSpec((TAP_ROWS // quarters, part_c), lambda h, q, s: (q, h)),
            ],
        ),
        out_shape=[
            jax.ShapeDtypeStruct((2, halves, quarters, piece, co), F32),
            jax.ShapeDtypeStruct((TAP_ROWS, own), F32),
        ],
        name="finish_grads",
    )(idx, pieces)
    return w.reshape(2, own, co), k[:18].reshape(2, 9, own)


def body(features, pointwise, depthwise, cotangent):
    n, rows, width, channels = features.shape
    own, co = pointwise.shape[1:]
    space, dp = lax.axis_size("space"), lax.axis_size("dp")
    me, row = lax.axis_index("space"), lax.axis_index("dp")
    chips = space // 2
    halves = 2 if space % 2 == 0 and own % 256 == 0 else 1
    part_c = own // halves
    even = chips & (chips - 1) == 0 and TAP_ROWS % (8 * chips) == 0 and part_c % (16 * chips) == 0
    quarters = chips if halves == 2 and even else 1
    core, chip = me % 2, me // 2

    grain = math.gcd(*RATES)
    slabs, size = width // grain, n * rows * grain
    cells = slabs * size

    terms, moves = [], []
    for branch, rate in enumerate(RATES):
        offset, reach = rate // rows, rate // grain
        terms.append((branch, 0, reach))
        moves.append(0)
        if 2 * offset == space:
            terms.append((branch, None, reach))
            moves.append(offset)
        elif offset < space:
            for u in (-1, 1):
                terms.append((branch, u, reach))
                moves.append(u * offset)
    middle = [t for t, m in enumerate(moves) if m == 0]
    outer = [t for t, m in enumerate(moves) if m != 0]
    half_way = next((moves[t] for t in outer if terms[t][1] is None), space)
    upper = (me >= half_way).astype(jnp.int32)

    def send(value, t, direction):
        if terms[t][1] is None:
            return cycle(value, "space", moves[t])
        return shift(value, "space", direction * moves[t])

    idx = jnp.concatenate(
        [
            jnp.stack([core, chip, upper]).astype(jnp.int32),
            (row + dp - jnp.arange(dp)).astype(jnp.int32) % dp,
        ]
    )

    taps = depthwise.reshape(18, own)
    k_all = [taps] + [cycle(taps, "dp", d) for d in range(1, dp)]
    if halves == 2:
        mine = lax.dynamic_slice_in_dim(pointwise, core * part_c, part_c, axis=1)
        mine = jnp.stack([mine] + [cycle(mine, "dp", d) for d in range(1, dp)])
        other = swap(mine, "space", 1)
        low = jnp.where(core == 0, mine, other)
        high = jnp.where(core == 0, other, mine)
        w = jnp.concatenate([low, high], axis=2)
    else:
        w = jnp.stack([pointwise] + [cycle(pointwise, "dp", d) for d in range(1, dp)])
    wt = w.transpose(0, 1, 3, 2)

    k_rows = jnp.stack(k_all).astype(F32)
    k_terms = []
    for branch, u, _ in terms:
        at = branch * 9
        if u is None:
            k_terms.append(
                jnp.where(upper > 0, k_rows[:, at + 6 : at + 9], k_rows[:, at : at + 3])
            )
        else:
            k_terms.append(k_rows[:, at + 3 * (u + 1) : at + 3 * (u + 1) + 3])

    def tap_rows(chosen):
        joined = jnp.concatenate([k_terms[t] for t in chosen], axis=1)
        return jnp.pad(joined, ((0, 0), (0, -joined.shape[1] % 8), (0, 0)))

    k_fwd = tap_rows(range(len(terms)))
    k_mid, k_out = tap_rows(middle), tap_rows(outer)
    kc_mid, kc_out = k_mid.transpose(0, 2, 1), k_out.transpose(0, 2, 1)

    x = to_slabs(features, grain)
    xt = jnp.pad(x.T, ((0, 0), (0, -cells % 128)))
    cot = to_slabs(cotangent, grain)

    parts = forward(terms, slabs, idx, x, k_fwd, w)
    received = {t: send(parts[t], t, -1) for t in outer}

    outputs, gs = [], [None] * len(terms)
    for t in middle:
        branch = terms[t][0]
        pre = parts[t]
        for o in outer:
            if terms[o][0] == branch:
                pre = pre + received[o].astype(F32)
        sig = jax.nn.sigmoid(pre)
        outputs.append((pre * sig).astype(BF16))
        cot_part = cot[:, branch * co : (branch + 1) * co].astype(F32)
        gs[t] = (cot_part * sig * (1.0 + pre * (1.0 - sig))).astype(BF16)
        for o in outer:
            if terms[o][0] == branch:
                gs[o] = send(gs[t], o, 1)
    branches_out = from_slabs(jnp.concatenate(outputs, axis=-1), cotangent.shape, grain)

    pick = lambda values, chosen: [values[t] for t in chosen]
    mid_terms, out_terms = pick(terms, middle), pick(terms, outer)
    first = weight_grads(
        mid_terms, slabs, size, halves, quarters, idx, xt, kc_mid, w, pick(gs, middle)
    )
    f_first = feature_grads(mid_terms, slabs, size, idx, k_mid, wt, pick(gs, middle))
    grads = weight_grads(
        out_terms, slabs, size, halves, quarters, idx, xt, kc_out, w, pick(gs, outer), first
    )
    f_last = feature_grads(out_terms, slabs, size, idx, k_out, wt, pick(gs, outer), f_first)
    feature_grad = from_slabs(f_last, features.shape, grain)

    factor = 1.0 / math.sqrt(dp * n * space * rows * width)
    if halves == 2:
        kept = grads[:, 0].astype(F32) + swap(grads[:, 1], "space", 1).astype(F32)
        kept = kept.astype(BF16)
    else:
        kept = grads[:, 0]
    if quarters > 1:
        total = kept[:, 0].astype(F32)
        for e in range(1, quarters):
            total = total + swap(kept[:, e], "space", 2 * e).astype(F32)
        total = total.astype(BF16)
    else:
        total = kept[:, 0]
    mine = total[0].astype(F32)
    for d in range(1, dp):
        mine = mine + cycle(total[d], "dp", -d).astype(F32)
    if quarters > 1:
        mine = mine.astype(BF16)
        block = jnp.stack([mine] + [swap(mine, "space", 2 * e) for e in range(1, quarters)])
    else:
        peers = [[i for i in range(space) if i % halves == c] for c in range(halves)]
        block = lax.psum(mine, "space", axis_index_groups=peers)[None]
    block = jnp.stack([block, swap(block, "space", 1)]) if halves == 2 else block[None]
    pointwise_grad, depthwise_grad = finish(idx, block, own, factor)
    return branches_out, feature_grad, pointwise_grad, depthwise_grad


def solution(mesh):
    return jax.shard_map(
        body,
        mesh=mesh,
        in_specs=(
            P("dp", "space", None, None),
            P(None, "dp", None),
            P(None, None, "dp"),
            P("dp", "space", None, None),
        ),
        out_specs=(
            P("dp", "space", None, None),
            P("dp", "space", None, None),
            P(None, "dp", None),
            P(None, None, "dp"),
        ),
        check_vma=False,
    )
```

```python
import functools
import math

import jax
import jax.numpy as jnp
from jax import lax
from jax.experimental import pallas as pl
from jax.experimental.pallas import tpu as pltpu
from jax.sharding import PartitionSpec as P

RATES = (12, 24)
SIDES = (-1, 0, 1)
F32 = jnp.float32
BF16 = jnp.bfloat16
TAP_ROWS = 32


def shift(value, axis, steps):
    count = lax.axis_size(axis)
    first, last = max(0, -steps), min(count, count - steps)
    return lax.ppermute(value, axis, [(i, i + steps) for i in range(first, last)])


def cycle(value, axis, steps):
    count = lax.axis_size(axis)
    return lax.ppermute(value, axis, [(i, (i + steps) % count) for i in range(count)])


def swap(value, axis, mask):
    count = lax.axis_size(axis)
    return lax.ppermute(value, axis, [(i, i ^ mask) for i in range(count)])


def to_slabs(field, grain):
    n, rows, width, ch = field.shape
    parts = field.reshape(n, rows, width // grain, grain, ch)
    return parts.transpose(2, 0, 1, 3, 4).reshape(-1, ch)


def from_slabs(flat, shape, grain):
    n, rows, width, ch = shape
    parts = flat.reshape(width // grain, n, rows, grain, ch)
    return parts.transpose(1, 2, 0, 3, 4).reshape(shape)


def span(slabs, q, side, reach):
    return 0 <= q + side * reach < slabs


def sums_kernel(terms, slabs, grain, x_ref, k_ref, xs_ref, *refs):
    outs, wide = refs[: len(terms)], refs[len(terms)]
    n, rows = x_ref.shape[:2]
    size = n * rows * grain
    for g in range(n * rows):
        line = x_ref[g // rows, g % rows].astype(F32)
        for q in range(slabs):
            at = q * size + g * grain
            wide[at : at + grain, :] = line[q * grain : (q + 1) * grain, :]
    xs_ref[...] = wide[...].astype(BF16)
    for t, (_, _, reach) in enumerate(terms):
        taps = [k_ref[0, 3 * t + i : 3 * t + i + 1, :] for i in range(3)]
        for q in range(slabs):
            total = None
            for i, side in enumerate(SIDES):
                if span(slabs, q, side, reach):
                    src = (q + side * reach) * size
                    term = wide[src : src + size, :] * taps[i]
                    total = term if total is None else total + term
            outs[t][q * size : (q + 1) * size, :] = total.astype(BF16)


def depthwise_sums(terms, slabs, grain, idx, x, k):
    n, rows, width, channels = x.shape
    cells, (blocks, _, own) = n * rows * width, k.shape
    flat = pl.BlockSpec((cells, own), lambda d, s: (0, s[3 + d]))
    kernel = functools.partial(sums_kernel, terms, slabs, grain)
    return pl.pallas_call(
        lambda s, *refs: kernel(*refs),
        grid_spec=pltpu.PrefetchScalarGridSpec(
            num_scalar_prefetch=1,
            grid=(blocks,),
            in_specs=[
                pl.BlockSpec((n, rows, width, own), lambda d, s: (0, 0, 0, s[3 + d])),
                pl.BlockSpec((1, k.shape[1], own), lambda d, s: (d, 0, 0)),
            ],
            out_specs=[flat] * (1 + len(terms)),
            scratch_shapes=[pltpu.VMEM((cells, own), F32)],
        ),
        out_shape=[jax.ShapeDtypeStruct((cells, channels), BF16)] * (1 + len(terms)),
        compiler_params=pltpu.CompilerParams(vmem_limit_bytes=60 << 20),
        cost_estimate=pl.CostEstimate(
            flops=6 * len(terms) * cells * channels,
            bytes_accessed=2 * (2 + len(terms)) * cells * channels,
            transcendentals=0,
        ),
        name="depthwise_sums",
    )(idx, x, k)


def forward_kernel(branches, w_ref, *refs):
    n = len(branches)
    ins, outs, acc = refs[:n], refs[n : 2 * n], refs[2 * n]
    step = pl.program_id(0)

    @pl.when(step == 0)
    def _():
        acc[...] = jnp.zeros_like(acc)

    for t, branch in enumerate(branches):
        acc[t] += jnp.dot(ins[t][...], w_ref[0, branch], preferred_element_type=F32)

    @pl.when(step == pl.num_programs(0) - 1)
    def _():
        for t in range(n):
            outs[t][...] = acc[t].astype(outs[t].dtype)


def forward(branches, dtype, idx, sums, w):
    cells, channels = sums[0].shape
    blocks, _, own, co = w.shape
    n = len(branches)
    kernel = functools.partial(forward_kernel, branches)
    return pl.pallas_call(
        lambda s, *refs: kernel(*refs),
        grid_spec=pltpu.PrefetchScalarGridSpec(
            num_scalar_prefetch=1,
            grid=(blocks,),
            in_specs=[pl.BlockSpec((1, 2, own, co), lambda d, s: (d, 0, 0, 0))]
            + [pl.BlockSpec((cells, own), lambda d, s: (0, s[3 + d]))] * n,
            out_specs=[pl.BlockSpec((cells, co), lambda d, s: (0, 0))] * n,
            scratch_shapes=[pltpu.VMEM((n, cells, co), F32)],
        ),
        out_shape=[jax.ShapeDtypeStruct((cells, co), dtype)] * n,
        compiler_params=pltpu.CompilerParams(vmem_limit_bytes=60 << 20),
        cost_estimate=pl.CostEstimate(
            flops=2 * n * cells * channels * co,
            bytes_accessed=2 * n * cells * channels + 4 * channels * co,
            transcendentals=0,
        ),
        name="forward_terms",
    )(idx, w, *sums)


def backward_kernel(terms, slabs, grain, halves, quarters, last, idx_ref, *refs):
    n = len(terms)
    x_ref, k_ref, w_ref, *refs = refs
    g_refs, d_refs, refs = refs[:n], refs[n : 2 * n], refs[2 * n :]
    if last:
        f_before, w_before, k_before, f_out, out_ref, gt, gd, kacc, wide = refs
    else:
        f_out, w_out, k_out, gt, gd, kacc = refs
    own, co = w_ref.shape[2:]
    cells = g_refs[0].shape[0]
    size = cells // slabs
    lanes = own // halves
    upper = idx_ref[2] > 0

    @pl.when(pl.program_id(0) == 0)
    def _():
        for t in range(n):
            gt[t] = g_refs[t][...].T

    kacc[...] = k_before[0] if last else jnp.zeros_like(kacc)
    for h in range(halves):
        cols = slice(h * lanes, (h + 1) * lanes)
        for t, (branch, _, _) in enumerate(terms):
            gd[h, t] = lax.dot_general(
                g_refs[t][...],
                w_ref[0, branch, cols, :],
                (((1,), (1,)), ((), ())),
                preferred_element_type=F32,
            )
        per = 2 * co // quarters
        seg = min(per, co)
        at_h = h ^ idx_ref[0] if halves > 1 else 0
        for branch in range(2):
            total = w_before[0, branch, :, cols] if last else None
            for t in range(n):
                if terms[t][0] == branch:
                    part = jnp.dot(gt[t], d_refs[t][:, cols], preferred_element_type=F32)
                    total = part if total is None else total + part
            if not last:
                w_out[0, branch, :, cols] = total
                continue
            for j in range(co // seg):
                q, off = divmod(branch * co + j * seg, per)
                at_q = q ^ idx_ref[1] if quarters > 1 else 0
                out_ref[0, at_h, at_q, off : off + seg, :] = total[
                    j * seg : (j + 1) * seg, :
                ].astype(BF16)
        sums = [None] * (3 * n)
        for q in range(slabs):
            here = slice(q * size, (q + 1) * size)
            xq = x_ref[here, cols].astype(F32)
            acc = f_before[here, cols] if last else None
            for t, (_, _, reach) in enumerate(terms):
                for i, side in enumerate(SIDES):
                    if not span(slabs, q, -side, reach):
                        continue
                    col = 3 * t + i
                    src = (q - side * reach) * size
                    part = gd[h, t, src : src + size, :]
                    term = part * k_ref[0, col : col + 1, cols]
                    acc = term if acc is None else acc + term
                    prod = jnp.sum((xq * part).reshape(size // 8, 8, lanes), axis=0)
                    sums[col] = prod if sums[col] is None else sums[col] + prod
            if last:
                rows = f_out.shape[1]
                for g in range(f_out.shape[0] * rows):
                    wide[g, q * grain : (q + 1) * grain, cols] = acc[g * grain : (g + 1) * grain, :]
            else:
                f_out[here, cols] = acc
        for t, (branch, u, _) in enumerate(terms):
            for i in range(3):
                total = jnp.sum(sums[3 * t + i], axis=0, keepdims=True)
                row = branch * 9 + i
                if u is None:
                    kacc[row : row + 1, cols] = jnp.where(upper, 0.0, total)
                    kacc[row + 6 : row + 7, cols] = jnp.where(upper, total, 0.0)
                else:
                    row += 3 * (u + 1)
                    kacc[row : row + 1, cols] = total
        if last:
            taps = TAP_ROWS // quarters
            for q in range(quarters):
                at_q = q ^ idx_ref[1] if quarters > 1 else 0
                out_ref[0, at_h, at_q, per:, :] = kacc[q * taps : (q + 1) * taps, cols].astype(BF16)
    if last:
        for g in range(wide.shape[0]):
            f_out[g // f_out.shape[1], g % f_out.shape[1]] = wide[g].astype(BF16)
    else:
        k_out[0] = kacc[...]


def backward(terms, slabs, grain, halves, quarters, idx, shape, x, k, w, gs, ds, before=None):
    blocks, _, own, co = w.shape
    cells, channels = x.shape
    images, rows, width, _ = shape
    n = len(terms)
    last = before is not None
    flat = pl.BlockSpec((cells, own), lambda d, s: (0, s[3 + d]))
    part_w = pl.BlockSpec((1, 2, co, own), lambda d, s: (d, 0, 0, 0))
    part_k = pl.BlockSpec((1, TAP_ROWS, own), lambda d, s: (d, 0, 0))
    in_specs = [
        flat,
        pl.BlockSpec((1,) + k.shape[1:], lambda d, s: (d, 0, 0)),
        pl.BlockSpec((1, 2, own, co), lambda d, s: (d, 0, 0, 0)),
    ]
    in_specs += [pl.BlockSpec((cells, co), lambda d, s: (0, 0))] * n + [flat] * n
    scratch = [
        pltpu.VMEM((n, co, cells), BF16),
        pltpu.VMEM((halves, n, cells, own // halves), F32),
        pltpu.VMEM((TAP_ROWS, own), F32),
    ]
    if last:
        in_specs += [flat, part_w, part_k]
        piece = (2 * co + TAP_ROWS) // quarters
        packed = (halves, quarters, piece, own // halves)
        out_specs = [
            pl.BlockSpec((images, rows, width, own), lambda d, s: (0, 0, 0, s[3 + d])),
            pl.BlockSpec((1,) + packed, lambda d, s: (d, 0, 0, 0, 0)),
        ]
        out_shape = [
            jax.ShapeDtypeStruct(shape, BF16),
            jax.ShapeDtypeStruct((blocks,) + packed, BF16),
        ]
        scratch.append(pltpu.VMEM((images * rows, width, own), F32))
    else:
        out_specs = [flat, part_w, part_k]
        out_shape = [
            jax.ShapeDtypeStruct((cells, channels), F32),
            jax.ShapeDtypeStruct((blocks, 2, co, own), F32),
            jax.ShapeDtypeStruct((blocks, TAP_ROWS, own), F32),
        ]
    return pl.pallas_call(
        functools.partial(backward_kernel, terms, slabs, grain, halves, quarters, last),
        grid_spec=pltpu.PrefetchScalarGridSpec(
            num_scalar_prefetch=1,
            grid=(blocks,),
            in_specs=in_specs,
            out_specs=out_specs,
            scratch_shapes=scratch,
        ),
        out_shape=out_shape,
        compiler_params=pltpu.CompilerParams(vmem_limit_bytes=60 << 20),
        cost_estimate=pl.CostEstimate(
            flops=4 * n * cells * channels * co,
            bytes_accessed=(2 * n + 6) * cells * channels,
            transcendentals=0,
        ),
        name="backward_outer" if last else "backward_middle",
    )(idx, x, k, w, *gs, *ds, *(before or ()))


def finish_kernel(factor, halves, quarters, idx_ref, in_ref, w_ref, k_ref, wide):
    co = w_ref.shape[2]
    per, taps = 2 * co // quarters, TAP_ROWS // quarters
    lanes = in_ref.shape[3]
    for h in range(halves):
        at_h = h ^ idx_ref[0] if halves > 1 else 0
        for q in range(quarters):
            at_q = q ^ idx_ref[1] if quarters > 1 else 0
            block = in_ref[at_h, at_q].astype(F32) * factor
            cols = slice(h * lanes, (h + 1) * lanes)
            wide[q * per : (q + 1) * per, cols] = block[:per]
            k_ref[q * taps : (q + 1) * taps, cols] = block[per:]
    for branch in range(2):
        w_ref[branch] = wide[branch * co : (branch + 1) * co, :].T


def finish(idx, pieces, own, factor):
    halves, quarters, rows, _ = pieces.shape
    co = (rows * quarters - TAP_ROWS) // 2
    w, k = pl.pallas_call(
        functools.partial(finish_kernel, factor, halves, quarters),
        in_specs=[
            pl.BlockSpec(memory_space=pltpu.SMEM),
            pl.BlockSpec(memory_space=pltpu.VMEM),
        ],
        out_specs=[pl.BlockSpec(memory_space=pltpu.VMEM)] * 2,
        out_shape=[
            jax.ShapeDtypeStruct((2, own, co), F32),
            jax.ShapeDtypeStruct((TAP_ROWS, own), F32),
        ],
        scratch_shapes=[pltpu.VMEM((2 * co, own), F32)],
        name="finish_grads",
    )(idx, pieces)
    return w, k[:18].reshape(2, 9, own)


def body(features, pointwise, depthwise, cotangent):
    n, rows, width, channels = features.shape
    own, co = pointwise.shape[1:]
    space, dp = lax.axis_size("space"), lax.axis_size("dp")
    me, row = lax.axis_index("space"), lax.axis_index("dp")
    chips = space // 2
    halves = 2 if space % 2 == 0 and own % 256 == 0 else 1
    part_c = own // halves
    even = chips & (chips - 1) == 0 and TAP_ROWS % (8 * chips) == 0 and 2 * co % (16 * chips) == 0 and chips <= 2 * co
    quarters = chips if halves == 2 and even else 1
    core, chip = me % 2, me // 2

    grain = math.gcd(*RATES)
    slabs = width // grain

    terms, moves = [], []
    for branch, rate in enumerate(RATES):
        offset, reach = rate // rows, rate // grain
        terms.append((branch, 0, reach))
        moves.append(0)
        if 2 * offset == space:
            terms.append((branch, None, reach))
            moves.append(offset)
        elif offset < space:
            for u in (-1, 1):
                terms.append((branch, u, reach))
                moves.append(u * offset)
    middle = [t for t, m in enumerate(moves) if m == 0]
    outer = [t for t, m in enumerate(moves) if m != 0]
    half_way = next((moves[t] for t in outer if terms[t][1] is None), space)
    upper = (me >= half_way).astype(jnp.int32)

    def send(value, t, direction):
        if terms[t][1] is None:
            return cycle(value, "space", moves[t])
        return shift(value, "space", direction * moves[t])

    idx = jnp.concatenate(
        [
            jnp.stack([core, chip, upper]).astype(jnp.int32),
            (row + dp - jnp.arange(dp)).astype(jnp.int32) % dp,
        ]
    )

    taps = depthwise.reshape(18, own)
    k_all = [taps] + [cycle(taps, "dp", d) for d in range(1, dp)]
    if halves == 2:
        mine = lax.dynamic_slice_in_dim(pointwise, core * part_c, part_c, axis=1)
        mine = jnp.stack([mine] + [cycle(mine, "dp", d) for d in range(1, dp)])
        other = swap(mine, "space", 1)
        low = jnp.where(core == 0, mine, other)
        high = jnp.where(core == 0, other, mine)
        w = jnp.concatenate([low, high], axis=2)
    else:
        w = jnp.stack([pointwise] + [cycle(pointwise, "dp", d) for d in range(1, dp)])

    k_rows = jnp.stack(k_all).astype(F32)
    k_terms = []
    for branch, u, _ in terms:
        at = branch * 9
        if u is None:
            k_terms.append(
                jnp.where(upper > 0, k_rows[:, at + 6 : at + 9], k_rows[:, at : at + 3])
            )
        else:
            k_terms.append(k_rows[:, at + 3 * (u + 1) : at + 3 * (u + 1) + 3])

    def tap_rows(chosen):
        joined = jnp.concatenate([k_terms[t] for t in chosen], axis=1)
        return jnp.pad(joined, ((0, 0), (0, -joined.shape[1] % 8), (0, 0)))

    k_fwd = tap_rows(range(len(terms)))
    k_mid, k_out = tap_rows(middle), tap_rows(outer)
    x, *sums = depthwise_sums(terms, slabs, grain, idx, features, k_fwd)
    cot = to_slabs(cotangent, grain)

    pick = lambda values, chosen: [values[t] for t in chosen]
    parts = [None] * len(terms)
    for chosen, dtype in ((outer, BF16), (middle, F32)):
        branches = [terms[t][0] for t in chosen]
        for t, part in zip(chosen, forward(branches, dtype, idx, pick(sums, chosen), w)):
            parts[t] = part
    received = {t: send(parts[t], t, -1) for t in outer}

    outputs, gs = [], [None] * len(terms)
    for t in middle:
        branch = terms[t][0]
        pre = parts[t]
        for o in outer:
            if terms[o][0] == branch:
                pre = pre + received[o].astype(F32)
        sig = jax.nn.sigmoid(pre)
        outputs.append((pre * sig).astype(BF16))
        cot_part = cot[:, branch * co : (branch + 1) * co].astype(F32)
        gs[t] = (cot_part * sig * (1.0 + pre * (1.0 - sig))).astype(BF16)
        for o in outer:
            if terms[o][0] == branch:
                gs[o] = send(gs[t], o, 1)
    branches_out = from_slabs(jnp.concatenate(outputs, axis=-1), cotangent.shape, grain)

    mid_terms, out_terms = pick(terms, middle), pick(terms, outer)
    common = (slabs, grain, halves, quarters, idx, features.shape, x)
    first = backward(mid_terms, *common, k_mid, w, pick(gs, middle), pick(sums, middle))
    feature_grad, grads = backward(
        out_terms, *common, k_out, w, pick(gs, outer), pick(sums, outer), first
    )

    factor = 1.0 / math.sqrt(dp * n * space * rows * width)
    if halves == 2:
        kept = grads[:, 0].astype(F32) + swap(grads[:, 1], "space", 1).astype(F32)
        kept = kept.astype(BF16)
    else:
        kept = grads[:, 0]
    if quarters > 1:
        total = kept[:, 0].astype(F32)
        for e in range(1, quarters):
            total = total + swap(kept[:, e], "space", 2 * e).astype(F32)
        total = total.astype(BF16)
    else:
        total = kept[:, 0]
    mine = total[0].astype(F32)
    for d in range(1, dp):
        mine = mine + cycle(total[d], "dp", -d).astype(F32)
    if quarters > 1:
        mine = mine.astype(BF16)
        block = jnp.stack([mine] + [swap(mine, "space", 2 * e) for e in range(1, quarters)])
    else:
        peers = [[i for i in range(space) if i % halves == c] for c in range(halves)]
        block = lax.psum(mine, "space", axis_index_groups=peers)[None]
    block = jnp.stack([block, swap(block, "space", 1)]) if halves == 2 else block[None]
    pointwise_grad, depthwise_grad = finish(idx, block, own, factor)
    return branches_out, feature_grad, pointwise_grad, depthwise_grad


def solution(mesh):
    return jax.shard_map(
        body,
        mesh=mesh,
        in_specs=(
            P("dp", "space", None, None),
            P(None, "dp", None),
            P(None, None, "dp"),
            P("dp", "space", None, None),
        ),
        out_specs=(
            P("dp", "space", None, None),
            P("dp", "space", None, None),
            P(None, "dp", None),
            P(None, None, "dp"),
        ),
        check_vma=False,
    )
```

```python
import functools
import math

import jax
import jax.numpy as jnp
from jax import lax
from jax.experimental import pallas as pl
from jax.experimental.pallas import tpu as pltpu
from jax.sharding import PartitionSpec as P

RATES = (12, 24)
SIDES = (-1, 0, 1)
F32 = jnp.float32
BF16 = jnp.bfloat16
TAP_ROWS = 32


def shift(value, axis, steps):
    count = lax.axis_size(axis)
    first, last = max(0, -steps), min(count, count - steps)
    return lax.ppermute(value, axis, [(i, i + steps) for i in range(first, last)])


def cycle(value, axis, steps):
    count = lax.axis_size(axis)
    return lax.ppermute(value, axis, [(i, (i + steps) % count) for i in range(count)])


def swap(value, axis, mask):
    count = lax.axis_size(axis)
    return lax.ppermute(value, axis, [(i, i ^ mask) for i in range(count)])


def to_slabs(field, grain):
    n, rows, width, ch = field.shape
    parts = field.reshape(n, rows, width // grain, grain, ch)
    return parts.transpose(2, 0, 1, 3, 4).reshape(-1, ch)


def from_slabs(flat, shape, grain):
    n, rows, width, ch = shape
    parts = flat.reshape(width // grain, n, rows, grain, ch)
    return parts.transpose(1, 2, 0, 3, 4).reshape(shape)


def span(slabs, q, side, reach):
    return 0 <= q + side * reach < slabs


def sums_kernel(terms, slabs, grain, x_ref, k_ref, xs_ref, *refs):
    outs, wide = refs[: len(terms)], refs[len(terms)]
    n, rows = x_ref.shape[:2]
    size = n * rows * grain
    for g in range(n * rows):
        line = x_ref[g // rows, g % rows].astype(F32)
        for q in range(slabs):
            at = q * size + g * grain
            wide[at : at + grain, :] = line[q * grain : (q + 1) * grain, :]
    xs_ref[...] = wide[...].astype(BF16)
    for t, (_, _, reach) in enumerate(terms):
        taps = [k_ref[0, 3 * t + i : 3 * t + i + 1, :] for i in range(3)]
        for q in range(slabs):
            total = None
            for i, side in enumerate(SIDES):
                if span(slabs, q, side, reach):
                    src = (q + side * reach) * size
                    term = wide[src : src + size, :] * taps[i]
                    total = term if total is None else total + term
            outs[t][q * size : (q + 1) * size, :] = total.astype(BF16)


def depthwise_sums(terms, slabs, grain, idx, x, k):
    n, rows, width, channels = x.shape
    cells, (blocks, _, own) = n * rows * width, k.shape
    flat = pl.BlockSpec((cells, own), lambda d, s: (0, d))
    kernel = functools.partial(sums_kernel, terms, slabs, grain)
    return pl.pallas_call(
        lambda s, *refs: kernel(*refs),
        grid_spec=pltpu.PrefetchScalarGridSpec(
            num_scalar_prefetch=1,
            grid=(blocks,),
            in_specs=[
                pl.BlockSpec((n, rows, width, own), lambda d, s: (0, 0, 0, s[3 + d])),
                pl.BlockSpec((1, k.shape[1], own), lambda d, s: (d, 0, 0)),
            ],
            out_specs=[flat] * (1 + len(terms)),
            scratch_shapes=[pltpu.VMEM((cells, own), F32)],
        ),
        out_shape=[jax.ShapeDtypeStruct((cells, channels), BF16)] * (1 + len(terms)),
        compiler_params=pltpu.CompilerParams(vmem_limit_bytes=60 << 20),
        cost_estimate=pl.CostEstimate(
            flops=6 * len(terms) * cells * channels,
            bytes_accessed=2 * (2 + len(terms)) * cells * channels,
            transcendentals=0,
        ),
        name="depthwise_sums",
    )(idx, x, k)


def forward_kernel(branches, w_ref, *refs):
    n = len(branches)
    for t, branch in enumerate(branches):
        part = jnp.dot(refs[t][...], w_ref[branch], preferred_element_type=F32)
        refs[n + t][...] = part.astype(refs[n + t].dtype)


def forward(branches, dtype, sums, w):
    cells, channels = sums[0].shape
    co = w.shape[2]
    n = len(branches)
    steps = 2 if cells % 32 == 0 else 1
    rows = cells // steps
    return pl.pallas_call(
        functools.partial(forward_kernel, branches),
        grid=(steps,),
        in_specs=[pl.BlockSpec(w.shape, lambda i: (0, 0, 0))]
        + [pl.BlockSpec((rows, channels), lambda i: (i, 0))] * n,
        out_specs=[pl.BlockSpec((rows, co), lambda i: (i, 0))] * n,
        out_shape=[jax.ShapeDtypeStruct((cells, co), dtype)] * n,
        compiler_params=pltpu.CompilerParams(vmem_limit_bytes=60 << 20),
        cost_estimate=pl.CostEstimate(
            flops=2 * n * cells * channels * co,
            bytes_accessed=2 * n * cells * channels + 4 * channels * co,
            transcendentals=0,
        ),
        name="forward_terms",
    )(w, *sums)


def backward_kernel(terms, slabs, grain, halves, quarters, last, idx_ref, *refs):
    n = len(terms)
    x_ref, k_ref, w_ref, *refs = refs
    g_refs, d_refs, refs = refs[:n], refs[n : 2 * n], refs[2 * n :]
    if last:
        f_before, w_before, k_before, f_out, *outs, gt, gd, kacc, wide = refs
    else:
        f_out, w_out, k_out, gt, gd, kacc = refs
    own, co = w_ref.shape[1:]
    cells = g_refs[0].shape[0]
    size = cells // slabs
    lanes = own // halves
    upper = idx_ref[2] > 0
    per, seg = 2 * co // quarters, min(2 * co // quarters, co)

    def packed(h, q, rows, value):
        at_q = q ^ idx_ref[1] if quarters > 1 else 0
        if halves == 1:
            outs[0][at_q, 0, rows, :] = value.astype(BF16)
            return
        keep = idx_ref[0] == h

        @pl.when(keep)
        def _():
            outs[0][at_q, 0, rows, :] = value.astype(BF16)

        @pl.when(jnp.logical_not(keep))
        def _():
            outs[1][at_q, 0, rows, :] = value.astype(BF16)

    @pl.when(pl.program_id(0) == 0)
    def _():
        for t in range(n):
            gt[t] = g_refs[t][...].T

    kacc[...] = k_before[0] if last else jnp.zeros_like(kacc)
    for t, (branch, _, _) in enumerate(terms):
        gd[t] = lax.dot_general(
            g_refs[t][...], w_ref[branch], (((1,), (1,)), ((), ())), preferred_element_type=F32
        )
    for branch in range(2):
        total = w_before[0, branch] if last else None
        for t in range(n):
            if terms[t][0] == branch:
                part = jnp.dot(gt[t], d_refs[t][...], preferred_element_type=F32)
                total = part if total is None else total + part
        if not last:
            w_out[0, branch] = total
            continue
        for j in range(co // seg):
            q, off = divmod(branch * co + j * seg, per)
            for h in range(halves):
                block = total[j * seg : (j + 1) * seg, h * lanes : (h + 1) * lanes]
                packed(h, q, slice(off, off + seg), block)
    for h in range(halves):
        cols = slice(h * lanes, (h + 1) * lanes)
        sums = [None] * (3 * n)
        for q in range(slabs):
            here = slice(q * size, (q + 1) * size)
            xq = x_ref[here, cols].astype(F32)
            acc = f_before[here, cols] if last else None
            for t, (_, _, reach) in enumerate(terms):
                for i, side in enumerate(SIDES):
                    if not span(slabs, q, -side, reach):
                        continue
                    col = 3 * t + i
                    src = (q - side * reach) * size
                    part = gd[t, src : src + size, cols]
                    term = part * k_ref[0, col : col + 1, cols]
                    acc = term if acc is None else acc + term
                    prod = jnp.sum((xq * part).reshape(size // 8, 8, lanes), axis=0)
                    sums[col] = prod if sums[col] is None else sums[col] + prod
            if last:
                rows = f_out.shape[1]
                for g in range(f_out.shape[0] * rows):
                    wide[g, q * grain : (q + 1) * grain, cols] = acc[g * grain : (g + 1) * grain, :]
            else:
                f_out[here, cols] = acc
        for t, (branch, u, _) in enumerate(terms):
            for i in range(3):
                total = jnp.sum(sums[3 * t + i], axis=0, keepdims=True)
                row = branch * 9 + i
                if u is None:
                    kacc[row : row + 1, cols] = jnp.where(upper, 0.0, total)
                    kacc[row + 6 : row + 7, cols] = jnp.where(upper, total, 0.0)
                else:
                    row += 3 * (u + 1)
                    kacc[row : row + 1, cols] = total
        if last:
            taps = TAP_ROWS // quarters
            for q in range(quarters):
                packed(h, q, slice(per, None), kacc[q * taps : (q + 1) * taps, cols])
    if last:
        for g in range(wide.shape[0]):
            f_out[g // f_out.shape[1], g % f_out.shape[1]] = wide[g].astype(BF16)
    else:
        k_out[0] = kacc[...]


def backward(terms, slabs, grain, halves, quarters, idx, shape, x, k, w, gs, ds, before=None):
    blocks, _, own = k.shape
    co = w.shape[2]
    cells, channels = x.shape
    images, rows, width, _ = shape
    n = len(terms)
    last = before is not None
    flat = pl.BlockSpec((cells, own), lambda d, s: (0, d))
    part_w = pl.BlockSpec((1, 2, co, own), lambda d, s: (d, 0, 0, 0))
    part_k = pl.BlockSpec((1, TAP_ROWS, own), lambda d, s: (d, 0, 0))
    in_specs = [
        flat,
        pl.BlockSpec((1,) + k.shape[1:], lambda d, s: (d, 0, 0)),
        pl.BlockSpec((2, own, co), lambda d, s: (0, d, 0)),
    ]
    in_specs += [pl.BlockSpec((cells, co), lambda d, s: (0, 0))] * n + [flat] * n
    scratch = [
        pltpu.VMEM((n, co, cells), BF16),
        pltpu.VMEM((n, cells, own), F32),
        pltpu.VMEM((TAP_ROWS, own), F32),
    ]
    if last:
        in_specs += [flat, part_w, part_k]
        piece = (2 * co + TAP_ROWS) // quarters
        packed = (quarters, blocks, piece, own // halves)
        out_specs = [
            pl.BlockSpec((images, rows, width, own), lambda d, s: (0, 0, 0, s[3 + d])),
        ]
        out_specs += [
            pl.BlockSpec((quarters, 1) + packed[2:], lambda d, s: (0, d, 0, 0))
        ] * halves
        out_shape = [
            jax.ShapeDtypeStruct(shape, BF16),
        ] + [jax.ShapeDtypeStruct(packed, BF16)] * halves
        scratch.append(pltpu.VMEM((images * rows, width, own), F32))
    else:
        out_specs = [flat, part_w, part_k]
        out_shape = [
            jax.ShapeDtypeStruct((cells, channels), F32),
            jax.ShapeDtypeStruct((blocks, 2, co, own), F32),
            jax.ShapeDtypeStruct((blocks, TAP_ROWS, own), F32),
        ]
    return pl.pallas_call(
        functools.partial(backward_kernel, terms, slabs, grain, halves, quarters, last),
        grid_spec=pltpu.PrefetchScalarGridSpec(
            num_scalar_prefetch=1,
            grid=(blocks,),
            in_specs=in_specs,
            out_specs=out_specs,
            scratch_shapes=scratch,
        ),
        out_shape=out_shape,
        compiler_params=pltpu.CompilerParams(vmem_limit_bytes=60 << 20),
        cost_estimate=pl.CostEstimate(
            flops=4 * n * cells * channels * co,
            bytes_accessed=(2 * n + 6) * cells * channels,
            transcendentals=0,
        ),
        name="backward_outer" if last else "backward_middle",
    )(idx, x, k, w, *gs, *ds, *(before or ()))


def finish_kernel(factor, halves, quarters, idx_ref, in_ref, w_ref, k_ref, wide):
    co = w_ref.shape[2]
    per, taps = 2 * co // quarters, TAP_ROWS // quarters
    lanes = in_ref.shape[3]
    for h in range(halves):
        at_h = h ^ idx_ref[0] if halves > 1 else 0
        for q in range(quarters):
            at_q = q ^ idx_ref[1] if quarters > 1 else 0
            block = in_ref[at_h, at_q].astype(F32) * factor
            cols = slice(h * lanes, (h + 1) * lanes)
            wide[q * per : (q + 1) * per, cols] = block[:per]
            k_ref[q * taps : (q + 1) * taps, cols] = block[per:]
    for branch in range(2):
        w_ref[branch] = wide[branch * co : (branch + 1) * co, :].T


def finish(idx, pieces, own, factor):
    halves, quarters, rows, _ = pieces.shape
    co = (rows * quarters - TAP_ROWS) // 2
    w, k = pl.pallas_call(
        functools.partial(finish_kernel, factor, halves, quarters),
        in_specs=[
            pl.BlockSpec(memory_space=pltpu.SMEM),
            pl.BlockSpec(memory_space=pltpu.VMEM),
        ],
        out_specs=[pl.BlockSpec(memory_space=pltpu.VMEM)] * 2,
        out_shape=[
            jax.ShapeDtypeStruct((2, own, co), F32),
            jax.ShapeDtypeStruct((TAP_ROWS, own), F32),
        ],
        scratch_shapes=[pltpu.VMEM((2 * co, own), F32)],
        name="finish_grads",
    )(idx, pieces)
    return w, k[:18].reshape(2, 9, own)


def body(features, pointwise, depthwise, cotangent):
    n, rows, width, channels = features.shape
    own, co = pointwise.shape[1:]
    space, dp = lax.axis_size("space"), lax.axis_size("dp")
    me, row = lax.axis_index("space"), lax.axis_index("dp")
    chips = space // 2
    halves = 2 if space % 2 == 0 and own % 256 == 0 else 1
    part_c = own // halves
    even = chips & (chips - 1) == 0 and TAP_ROWS % (8 * chips) == 0 and 2 * co % (16 * chips) == 0 and chips <= 2 * co
    quarters = chips if halves == 2 and even else 1
    core, chip = me % 2, me // 2

    grain = math.gcd(*RATES)
    slabs = width // grain

    terms, moves = [], []
    for branch, rate in enumerate(RATES):
        offset, reach = rate // rows, rate // grain
        terms.append((branch, 0, reach))
        moves.append(0)
        if 2 * offset == space:
            terms.append((branch, None, reach))
            moves.append(offset)
        elif offset < space:
            for u in (-1, 1):
                terms.append((branch, u, reach))
                moves.append(u * offset)
    middle = [t for t, m in enumerate(moves) if m == 0]
    outer = [t for t, m in enumerate(moves) if m != 0]
    half_way = next((moves[t] for t in outer if terms[t][1] is None), space)
    upper = (me >= half_way).astype(jnp.int32)

    def send(value, t, direction):
        if terms[t][1] is None:
            return cycle(value, "space", moves[t])
        return shift(value, "space", direction * moves[t])

    idx = jnp.concatenate(
        [
            jnp.stack([core, chip, upper]).astype(jnp.int32),
            (row + dp - jnp.arange(dp)).astype(jnp.int32) % dp,
        ]
    )

    taps = depthwise.reshape(18, own)
    k_all = [taps] + [cycle(taps, "dp", d) for d in range(1, dp)]
    mine = pointwise
    if halves == 2:
        mine = lax.dynamic_slice_in_dim(pointwise, core * part_c, part_c, axis=1)
    mine = [mine] + [cycle(mine, "dp", d) for d in range(1, dp)]

    k_rows = jnp.stack(k_all).astype(F32)
    k_terms = []
    for branch, u, _ in terms:
        at = branch * 9
        if u is None:
            k_terms.append(
                jnp.where(upper > 0, k_rows[:, at + 6 : at + 9], k_rows[:, at : at + 3])
            )
        else:
            k_terms.append(k_rows[:, at + 3 * (u + 1) : at + 3 * (u + 1) + 3])

    def tap_rows(chosen):
        joined = jnp.concatenate([k_terms[t] for t in chosen], axis=1)
        return jnp.pad(joined, ((0, 0), (0, -joined.shape[1] % 8), (0, 0)))

    k_fwd = tap_rows(range(len(terms)))
    k_mid, k_out = tap_rows(middle), tap_rows(outer)
    x, *sums = depthwise_sums(terms, slabs, grain, idx, features, k_fwd)
    x, sums, mine = lax.optimization_barrier((x, sums, mine))
    if halves == 2:
        mine = jnp.stack(mine, axis=1)
        other = swap(mine, "space", 1)
        low = jnp.where(core == 0, mine, other)
        high = jnp.where(core == 0, other, mine)
        w = jnp.concatenate([low, high], axis=2).reshape(2, channels, co)
    else:
        w = jnp.concatenate(mine, axis=1)
    cot = to_slabs(cotangent, grain)

    pick = lambda values, chosen: [values[t] for t in chosen]
    parts = [None] * len(terms)
    for chosen, dtype in ((outer, BF16), (middle, F32)):
        branches = [terms[t][0] for t in chosen]
        for t, part in zip(chosen, forward(branches, dtype, pick(sums, chosen), w)):
            parts[t] = part
    received = {t: send(parts[t], t, -1) for t in outer}

    outputs, gs = [], [None] * len(terms)
    for t in middle:
        branch = terms[t][0]
        pre = parts[t]
        for o in outer:
            if terms[o][0] == branch:
                pre = pre + received[o].astype(F32)
        sig = jax.nn.sigmoid(pre)
        outputs.append((pre * sig).astype(BF16))
        cot_part = cot[:, branch * co : (branch + 1) * co].astype(F32)
        gs[t] = (cot_part * sig * (1.0 + pre * (1.0 - sig))).astype(BF16)
        for o in outer:
            if terms[o][0] == branch:
                gs[o] = send(gs[t], o, 1)
    branches_out = from_slabs(jnp.concatenate(outputs, axis=-1), cotangent.shape, grain)

    mid_terms, out_terms = pick(terms, middle), pick(terms, outer)
    common = (slabs, grain, halves, quarters, idx, features.shape, x)
    first = backward(mid_terms, *common, k_mid, w, pick(gs, middle), pick(sums, middle))
    feature_grad, *grads = backward(
        out_terms, *common, k_out, w, pick(gs, outer), pick(sums, outer), first
    )

    factor = 1.0 / math.sqrt(dp * n * space * rows * width)
    kept = grads[0]
    if halves == 2:
        kept = (kept.astype(F32) + swap(grads[1], "space", 1).astype(F32)).astype(BF16)
    total = kept[0]
    if quarters > 1:
        total = total.astype(F32)
        for e in range(1, quarters):
            total = total + swap(kept[e], "space", 2 * e).astype(F32)
        total = total.astype(BF16)
    mine = total[0].astype(F32)
    for d in range(1, dp):
        mine = mine + cycle(total[d], "dp", -d).astype(F32)
    if quarters > 1:
        mine = mine.astype(BF16)
        block = jnp.stack([mine] + [swap(mine, "space", 2 * e) for e in range(1, quarters)])
    else:
        peers = [[i for i in range(space) if i % halves == c] for c in range(halves)]
        block = lax.psum(mine, "space", axis_index_groups=peers)[None]
    block = jnp.stack([block, swap(block, "space", 1)]) if halves == 2 else block[None]
    pointwise_grad, depthwise_grad = finish(idx, block, own, factor)
    return branches_out, feature_grad, pointwise_grad, depthwise_grad


def solution(mesh):
    return jax.shard_map(
        body,
        mesh=mesh,
        in_specs=(
            P("dp", "space", None, None),
            P(None, "dp", None),
            P(None, None, "dp"),
            P("dp", "space", None, None),
        ),
        out_specs=(
            P("dp", "space", None, None),
            P("dp", "space", None, None),
            P(None, "dp", None),
            P(None, None, "dp"),
        ),
        check_vma=False,
    )
```

```python
import functools
import math

import jax
import jax.numpy as jnp
from jax import lax
from jax.experimental import pallas as pl
from jax.experimental.pallas import tpu as pltpu
from jax.sharding import PartitionSpec as P


RATES = (12, 24)
SIDES = (-1, 0, 1)
F32 = jnp.float32
BF16 = jnp.bfloat16
TAP_ROWS = 32


def shift(value, axis, steps):
    count = lax.axis_size(axis)
    first, last = max(0, -steps), min(count, count - steps)
    return lax.ppermute(value, axis, [(i, i + steps) for i in range(first, last)])


def cycle(value, axis, steps):
    count = lax.axis_size(axis)
    return lax.ppermute(value, axis, [(i, (i + steps) % count) for i in range(count)])


def swap(value, axis, mask):
    count = lax.axis_size(axis)
    return lax.ppermute(value, axis, [(i, i ^ mask) for i in range(count)])


def to_slabs(field, grain):
    n, rows, width, ch = field.shape
    parts = field.reshape(n, rows, width // grain, grain, ch)
    return parts.transpose(2, 0, 1, 3, 4).reshape(-1, ch)


def from_slabs(flat, shape, grain):
    n, rows, width, ch = shape
    parts = flat.reshape(width // grain, n, rows, grain, ch)
    return parts.transpose(1, 2, 0, 3, 4).reshape(shape)


def span(slabs, q, side, reach):
    return 0 <= q + side * reach < slabs


def sums_kernel(terms, slabs, grain, x_ref, k_ref, xs_ref, *refs):
    outs, wide = refs[: len(terms)], refs[len(terms)]
    n, rows = x_ref.shape[:2]
    size = n * rows * grain
    for g in range(n * rows):
        line = x_ref[g // rows, g % rows].astype(F32)
        for q in range(slabs):
            at = q * size + g * grain
            wide[at : at + grain, :] = line[q * grain : (q + 1) * grain, :]
    xs_ref[...] = wide[...].astype(BF16)
    for t, (_, _, reach) in enumerate(terms):
        taps = [k_ref[0, 3 * t + i : 3 * t + i + 1, :] for i in range(3)]
        for q in range(slabs):
            total = None
            for i, side in enumerate(SIDES):
                if span(slabs, q, side, reach):
                    src = (q + side * reach) * size
                    term = wide[src : src + size, :] * taps[i]
                    total = term if total is None else total + term
            outs[t][q * size : (q + 1) * size, :] = total.astype(BF16)


def depthwise_sums(terms, slabs, grain, idx, x, k):
    n, rows, width, channels = x.shape
    cells, (blocks, _, own) = n * rows * width, k.shape
    flat = pl.BlockSpec((cells, own), lambda d, s: (0, d))
    kernel = functools.partial(sums_kernel, terms, slabs, grain)
    return pl.pallas_call(
        lambda s, *refs: kernel(*refs),
        grid_spec=pltpu.PrefetchScalarGridSpec(
            num_scalar_prefetch=1,
            grid=(blocks,),
            in_specs=[
                pl.BlockSpec((n, rows, width, own), lambda d, s: (0, 0, 0, s[3 + d])),
                pl.BlockSpec((1, k.shape[1], own), lambda d, s: (d, 0, 0)),
            ],
            out_specs=[flat] * (1 + len(terms)),
            scratch_shapes=[pltpu.VMEM((cells, own), F32)],
        ),
        out_shape=[jax.ShapeDtypeStruct((cells, channels), BF16)] * (1 + len(terms)),
        compiler_params=pltpu.CompilerParams(vmem_limit_bytes=60 << 20),
        cost_estimate=pl.CostEstimate(
            flops=6 * len(terms) * cells * channels,
            bytes_accessed=2 * (2 + len(terms)) * cells * channels,
            transcendentals=0,
        ),
        name="depthwise_sums",
    )(idx, x, k)


def forward_kernel(branches, w_ref, *refs):
    n = len(branches)
    for t, branch in enumerate(branches):
        part = jnp.dot(refs[t][...], w_ref[branch], preferred_element_type=F32)
        refs[n + t][...] = part.astype(refs[n + t].dtype)


def forward(branches, dtypes, sums, w):
    cells, channels = sums[0].shape
    co = w.shape[2]
    n = len(branches)
    steps = 2 if cells % 32 == 0 else 1
    rows = cells // steps
    only = branches[0]
    if set(branches) == {only}:
        w_spec = pl.BlockSpec((1,) + w.shape[1:], lambda i: (only, 0, 0))
        branches = [0] * n
    else:
        w_spec = pl.BlockSpec(w.shape, lambda i: (0, 0, 0))
    return pl.pallas_call(
        functools.partial(forward_kernel, branches),
        grid=(steps,),
        in_specs=[w_spec] + [pl.BlockSpec((rows, channels), lambda i: (i, 0))] * n,
        out_specs=[pl.BlockSpec((rows, co), lambda i: (i, 0))] * n,
        out_shape=[jax.ShapeDtypeStruct((cells, co), dt) for dt in dtypes],
        compiler_params=pltpu.CompilerParams(vmem_limit_bytes=60 << 20),
        cost_estimate=pl.CostEstimate(
            flops=2 * n * cells * channels * co,
            bytes_accessed=2 * n * cells * channels + 2 * channels * co,
            transcendentals=0,
        ),
        name="forward_terms",
    )(w, *sums)


def back(g, weight):
    return lax.dot_general(g, weight, (((1,), (1,)), ((), ())), preferred_element_type=F32)


def weight_kernel(terms, slabs, halves, quarters, last, idx_ref, x_ref, w_ref, *refs):
    n = len(terms)
    g_refs, d_refs, refs = refs[:n], refs[n : 2 * n], refs[2 * n :]
    if last:
        w_before, k_before, *outs, gt, gd, kacc, pieces = refs
    else:
        w_out, k_out, gt, gd, kacc = refs
    own, co = w_ref.shape[1:]
    size = g_refs[0].shape[0] // slabs
    lanes = own // halves

    @pl.when(pl.program_id(0) == 0)
    def _():
        for t in range(n):
            gt[t] = g_refs[t][...].T

    for t in range(n):
        gd[t] = back(g_refs[t][...], w_ref[0])
    total = w_before[0] if last else None
    for t in range(n):
        part = jnp.dot(gt[t], d_refs[t][...], preferred_element_type=F32)
        total = part if total is None else total + part
    per = co // quarters
    if last:
        for h in range(halves):
            for q in range(quarters):
                block = total[q * per : (q + 1) * per, h * lanes : (h + 1) * lanes]
                pieces[h, q, :per, :] = block.astype(BF16)
    else:
        w_out[0] = total
    kacc[...] = k_before[0] if last else jnp.zeros_like(kacc)
    upper = idx_ref[2] > 0
    for h in range(halves):
        cols = slice(h * lanes, (h + 1) * lanes)
        sums = [None] * (3 * n)
        for q in range(slabs):
            xq = x_ref[q * size : (q + 1) * size, cols].astype(F32)
            for t, (_, _, reach) in enumerate(terms):
                for i, side in enumerate(SIDES):
                    if not span(slabs, q, -side, reach):
                        continue
                    src = (q - side * reach) * size
                    part = xq * gd[t, src : src + size, cols]
                    part = jnp.sum(part.reshape(size // 8, 8, lanes), axis=0)
                    at = 3 * t + i
                    sums[at] = part if sums[at] is None else sums[at] + part
        for t, (_, u, _) in enumerate(terms):
            for i in range(3):
                total = jnp.sum(sums[3 * t + i], axis=0, keepdims=True)
                if u is None:
                    kacc[i : i + 1, cols] = jnp.where(upper, 0.0, total)
                    kacc[i + 6 : i + 7, cols] = jnp.where(upper, total, 0.0)
                else:
                    row = 3 * (u + 1) + i
                    kacc[row : row + 1, cols] = total
    if not last:
        k_out[0] = kacc[...]
        return
    taps = TAP_ROWS // quarters
    for h in range(halves):
        for q in range(quarters):
            block = kacc[q * taps : (q + 1) * taps, h * lanes : (h + 1) * lanes]
            pieces[h, q, per:, :] = block.astype(BF16)
    for e in range(quarters):
        at = e ^ idx_ref[1] if quarters > 1 else 0
        if halves == 1:
            outs[0][e, 0] = pieces[0, at]
        else:
            outs[0][e, 0] = pieces[idx_ref[0], at]
            outs[1][e, 0] = pieces[1 - idx_ref[0], at]


def weight_grads(terms, slabs, halves, quarters, blocks, idx, x, w, gs, ds, before=None):
    cells, channels = x.shape
    own, co = channels // blocks, w.shape[2]
    n, branch = len(terms), terms[0][0]
    last = before is not None
    flat = pl.BlockSpec((cells, own), lambda d, s: (0, d))
    part_w = pl.BlockSpec((1, co, own), lambda d, s: (d, 0, 0))
    part_k = pl.BlockSpec((1, TAP_ROWS, own), lambda d, s: (d, 0, 0))
    in_specs = [flat, pl.BlockSpec((1, own, co), lambda d, s: (branch, d, 0))]
    in_specs += [pl.BlockSpec((cells, co), lambda d, s: (0, 0))] * n + [flat] * n
    scratch = [
        pltpu.VMEM((n, co, cells), BF16),
        pltpu.VMEM((n, cells, own), F32),
        pltpu.VMEM((TAP_ROWS, own), F32),
    ]
    if last:
        in_specs += [part_w, part_k]
        piece = ((co + TAP_ROWS) // quarters, own // halves)
        out_specs = [pl.BlockSpec((quarters, 1) + piece, lambda d, s: (0, d, 0, 0))] * halves
        out_shape = [jax.ShapeDtypeStruct((quarters, blocks) + piece, BF16)] * halves
        scratch.append(pltpu.VMEM((halves, quarters) + piece, BF16))
    else:
        out_specs = [part_w, part_k]
        out_shape = [
            jax.ShapeDtypeStruct((blocks, co, own), F32),
            jax.ShapeDtypeStruct((blocks, TAP_ROWS, own), F32),
        ]
    return pl.pallas_call(
        functools.partial(weight_kernel, terms, slabs, halves, quarters, last),
        grid_spec=pltpu.PrefetchScalarGridSpec(
            num_scalar_prefetch=1,
            grid=(blocks,),
            in_specs=in_specs,
            out_specs=out_specs,
            scratch_shapes=scratch,
        ),
        out_shape=out_shape,
        compiler_params=pltpu.CompilerParams(vmem_limit_bytes=60 << 20),
        cost_estimate=pl.CostEstimate(
            flops=4 * n * cells * channels * co,
            bytes_accessed=2 * (n + 1) * cells * channels + 6 * channels * co,
            transcendentals=0,
        ),
        name="weight_outer" if last else "weight_middle",
    )(idx, x, w, *gs, *ds, *(before or ()))


def feature_kernel(terms, slabs, grain, k_ref, w_ref, *refs):
    n = len(terms)
    g_refs, (out_ref, gd, wide) = refs[:n], refs[n:]
    size = g_refs[0].shape[0] // slabs
    own = w_ref.shape[1]
    for t, (branch, _, _) in enumerate(terms):
        gd[t] = back(g_refs[t][...], w_ref[branch])
    lanes = own // 2 if own % 256 == 0 else own
    for h in range(own // lanes):
        cols = slice(h * lanes, (h + 1) * lanes)
        for q in range(slabs):
            acc = None
            for t, (_, _, reach) in enumerate(terms):
                for i, side in enumerate(SIDES):
                    if not span(slabs, q, -side, reach):
                        continue
                    src = (q - side * reach) * size
                    term = gd[t, src : src + size, cols] * k_ref[0, 3 * t + i : 3 * t + i + 1, cols]
                    acc = term if acc is None else acc + term
            for g in range(wide.shape[0]):
                wide[g, q * grain : (q + 1) * grain, cols] = acc[g * grain : (g + 1) * grain, :]
    rows = out_ref.shape[1]
    for g in range(wide.shape[0]):
        out_ref[g // rows, g % rows] = wide[g].astype(BF16)


def feature_grads(terms, slabs, grain, idx, shape, k, w, gs):
    images, rows, width, channels = shape
    blocks, _, own = k.shape
    cells, co = gs[0].shape
    n = len(terms)
    kernel = functools.partial(feature_kernel, terms, slabs, grain)
    return pl.pallas_call(
        lambda s, *refs: kernel(*refs),
        grid_spec=pltpu.PrefetchScalarGridSpec(
            num_scalar_prefetch=1,
            grid=(blocks,),
            in_specs=[
                pl.BlockSpec((1,) + k.shape[1:], lambda d, s: (d, 0, 0)),
                pl.BlockSpec((2, own, co), lambda d, s: (0, d, 0)),
            ]
            + [pl.BlockSpec((cells, co), lambda d, s: (0, 0))] * n,
            out_specs=pl.BlockSpec((images, rows, width, own), lambda d, s: (0, 0, 0, s[3 + d])),
            scratch_shapes=[
                pltpu.VMEM((n, cells, own), F32),
                pltpu.VMEM((images * rows, width, own), F32),
            ],
        ),
        out_shape=jax.ShapeDtypeStruct(shape, BF16),
        compiler_params=pltpu.CompilerParams(vmem_limit_bytes=60 << 20),
        cost_estimate=pl.CostEstimate(
            flops=2 * n * cells * channels * co,
            bytes_accessed=4 * cells * channels,
            transcendentals=0,
        ),
        name="feature_grads",
    )(idx, k, w, *gs)


def finish_kernel(factor, halves, quarters, idx_ref, in_ref, w_ref, k_ref, wide, taps_of):
    co = w_ref.shape[2]
    per, taps = co // quarters, TAP_ROWS // quarters
    lanes = in_ref.shape[4]
    for branch in range(2):
        for h in range(halves):
            at_h = h ^ idx_ref[0] if halves > 1 else 0
            cols = slice(h * lanes, (h + 1) * lanes)
            for q in range(quarters):
                at_q = q ^ idx_ref[1] if quarters > 1 else 0
                block = in_ref[at_h, at_q, branch].astype(F32) * factor
                wide[q * per : (q + 1) * per, cols] = block[:per]
                taps_of[q * taps : (q + 1) * taps, cols] = block[per:]
        w_ref[branch] = wide[...].T
        k_ref[branch] = taps_of[: k_ref.shape[1], :]


def finish(idx, pieces, own, factor):
    halves, quarters, _, rows, _ = pieces.shape
    co = rows * quarters - TAP_ROWS
    return pl.pallas_call(
        functools.partial(finish_kernel, factor, halves, quarters),
        in_specs=[
            pl.BlockSpec(memory_space=pltpu.SMEM),
            pl.BlockSpec(memory_space=pltpu.VMEM),
        ],
        out_specs=[pl.BlockSpec(memory_space=pltpu.VMEM)] * 2,
        out_shape=[
            jax.ShapeDtypeStruct((2, own, co), F32),
            jax.ShapeDtypeStruct((2, 9, own), F32),
        ],
        scratch_shapes=[pltpu.VMEM((co, own), F32), pltpu.VMEM((TAP_ROWS, own), F32)],
        name="finish_grads",
    )(idx, pieces)


def pyramid(features, pointwise, depthwise, cotangent):
    n, rows, width, channels = features.shape
    own, co = pointwise.shape[1:]
    space, dp = lax.axis_size("space"), lax.axis_size("dp")
    me, row = lax.axis_index("space"), lax.axis_index("dp")
    chips = space // 2
    halves = 2 if space % 2 == 0 and own % 256 == 0 else 1
    part_c = own // halves
    even = chips & (chips - 1) == 0 and TAP_ROWS % (8 * chips) == 0 and co % (16 * chips) == 0
    quarters = chips if halves == 2 and even else 1
    core, chip = me % 2, me // 2

    grain = math.gcd(*RATES)
    slabs = width // grain

    terms, moves = [], []
    for branch, rate in enumerate(RATES):
        offset, reach = rate // rows, rate // grain
        terms.append((branch, 0, reach))
        moves.append(0)
        if 2 * offset == space:
            terms.append((branch, None, reach))
            moves.append(offset)
        elif offset < space:
            for u in (-1, 1):
                terms.append((branch, u, reach))
                moves.append(u * offset)
    middle = [t for t, m in enumerate(moves) if m == 0]
    outer = [t for t, m in enumerate(moves) if m != 0]
    half_way = next((moves[t] for t in outer if terms[t][1] is None), space)
    upper = (me >= half_way).astype(jnp.int32)

    def send(value, t, direction):
        if terms[t][1] is None:
            return cycle(value, "space", moves[t])
        return shift(value, "space", direction * moves[t])

    idx = jnp.concatenate(
        [
            jnp.stack([core, chip, upper]).astype(jnp.int32),
            (row + dp - jnp.arange(dp)).astype(jnp.int32) % dp,
        ]
    )

    taps = depthwise.reshape(18, own)
    k_all = [taps] + [cycle(taps, "dp", d) for d in range(1, dp)]
    mine = pointwise
    if halves == 2:
        mine = lax.dynamic_slice_in_dim(pointwise, core * part_c, part_c, axis=1)
    mine = [mine] + [cycle(mine, "dp", d) for d in range(1, dp)]

    k_rows = jnp.stack(k_all).astype(F32)
    k_terms = []
    for branch, u, _ in terms:
        at = branch * 9
        if u is None:
            k_terms.append(
                jnp.where(upper > 0, k_rows[:, at + 6 : at + 9], k_rows[:, at : at + 3])
            )
        else:
            k_terms.append(k_rows[:, at + 3 * (u + 1) : at + 3 * (u + 1) + 3])

    taps_all = jnp.concatenate(k_terms, axis=1)
    taps_all = jnp.pad(taps_all, ((0, 0), (0, -taps_all.shape[1] % 8), (0, 0)))

    x, *sums = depthwise_sums(terms, slabs, grain, idx, features, taps_all)
    x, sums, mine = lax.optimization_barrier((x, sums, mine))
    if halves == 2:
        mine = jnp.stack(mine, axis=1)
        other = swap(mine, "space", 1)
        low = jnp.where(core == 0, mine, other)
        high = jnp.where(core == 0, other, mine)
        w = jnp.concatenate([low, high], axis=2).reshape(2, channels, co)
    else:
        w = jnp.concatenate(mine, axis=1)

    held = lax.optimization_barrier
    pick = lambda values, chosen: [values[t] for t in chosen]
    mid = [[t for t in middle if terms[t][0] == b] for b in range(2)]
    out = [[t for t in outer if terms[t][0] == b] for b in range(2)]
    cot = to_slabs(cotangent, grain)

    order = (1, 0)
    parts, received, outputs, gs = [None] * len(terms), {}, [None] * 2, [None] * len(terms)
    for b in order:
        count = len(out[b])
        for t, part in zip(out[b], forward([b] * count, [BF16] * count, pick(sums, out[b]), w)):
            parts[t] = part
        received[b] = [send(parts[t], t, -1) for t in out[b]]
        if b == order[0]:
            _, sums = held((pick(parts, out[b]), sums))
    chosen = mid[1] + mid[0]
    centre = forward([terms[t][0] for t in chosen], [F32] * 2, pick(sums, chosen), w)
    for t, part in zip(chosen, centre):
        parts[t] = part

    common = (slabs, halves, quarters, dp, idx, x, w)
    first, grads, summed = [None] * 2, [None] * 2, [None] * 2
    for b in order:
        t = mid[b][0]
        if b == order[1]:
            received[b], first[order[0]] = held((received[b], first[order[0]]))
        pre = parts[t]
        for other in received[b]:
            pre = pre + other.astype(F32)
        sig = jax.nn.sigmoid(pre)
        outputs[b] = (pre * sig).astype(BF16)
        cot_part = cot[:, b * co : (b + 1) * co].astype(F32)
        gs[t] = (cot_part * sig * (1.0 + pre * (1.0 - sig))).astype(BF16)
        for o in out[b]:
            gs[o] = send(gs[t], o, 1)
        first[b] = weight_grads(pick(terms, mid[b]), *common, pick(gs, mid[b]), pick(sums, mid[b]))
    last_g = pick(gs, out[order[1]])
    for b in order:
        if b == order[0]:
            grad_g = pick(gs, out[b])
            grad_g, first[order[1]] = held((grad_g, first[order[1]]))
        else:
            grad_g = last_g
        grads[b] = weight_grads(pick(terms, out[b]), *common, grad_g, pick(sums, out[b]), first[b])
        kept = grads[b][0]
        if halves == 2:
            kept = (kept.astype(F32) + swap(grads[b][1], "space", 1).astype(F32)).astype(BF16)
        if b == order[0]:
            last_g, kept = held((last_g, kept))
        else:
            gs, kept = held((gs, kept))
        summed[b] = [kept[0]] + [swap(kept[e], "space", 2 * e) for e in range(1, quarters)]
    feature_grad = feature_grads(terms, slabs, grain, idx, features.shape, taps_all, w, gs)
    branches_out = from_slabs(jnp.concatenate(outputs, axis=-1), cotangent.shape, grain)

    factor = 1.0 / math.sqrt(dp * n * space * rows * width)
    total = jnp.stack([sum(p.astype(F32) for p in pieces) for pieces in summed], axis=1)
    total = total.astype(BF16)
    mine = total[0].astype(F32)
    for d in range(1, dp):
        mine = mine + cycle(total[d], "dp", -d).astype(F32)
    if quarters > 1:
        mine = mine.astype(BF16)
        block = jnp.stack([mine] + [swap(mine, "space", 2 * e) for e in range(1, quarters)])
    else:
        peers = [[i for i in range(space) if i % halves == c] for c in range(halves)]
        block = lax.psum(mine, "space", axis_index_groups=peers)[None]
    block = jnp.stack([block, swap(block, "space", 1)]) if halves == 2 else block[None]
    pointwise_grad, depthwise_grad = finish(idx, block, own, factor)
    return branches_out, feature_grad, pointwise_grad, depthwise_grad


def solution(mesh):
    return jax.shard_map(
        pyramid,
        mesh=mesh,
        in_specs=(
            P("dp", "space", None, None),
            P(None, "dp", None),
            P(None, None, "dp"),
            P("dp", "space", None, None),
        ),
        out_specs=(
            P("dp", "space", None, None),
            P("dp", "space", None, None),
            P(None, "dp", None),
            P(None, None, "dp"),
        ),
        check_vma=False,
    )
```

```python
import functools
import math

import jax
import jax.numpy as jnp
from jax import lax
from jax.experimental import pallas as pl
from jax.experimental.pallas import tpu as pltpu
from jax.sharding import PartitionSpec as P


RATES = (12, 24)
SIDES = (-1, 0, 1)
F32 = jnp.float32
BF16 = jnp.bfloat16
TAP_ROWS = 32
MIB = 1 << 20


def shift(value, axis, steps):
    count = lax.axis_size(axis)
    first, last = max(0, -steps), min(count, count - steps)
    return lax.ppermute(value, axis, [(i, i + steps) for i in range(first, last)])


def cycle(value, axis, steps):
    count = lax.axis_size(axis)
    return lax.ppermute(value, axis, [(i, (i + steps) % count) for i in range(count)])


def swap(value, axis, mask):
    count = lax.axis_size(axis)
    return lax.ppermute(value, axis, [(i, i ^ mask) for i in range(count)])


def span(slabs, q, side, reach):
    return 0 <= q + side * reach < slabs


WHOLE = pl.BlockSpec(memory_space=pltpu.VMEM)


def lanes_at(start, count):
    return pl.ds(start if isinstance(start, int) else pl.multiple_of(start, count), count)


def sums_kernel(terms, slabs, grain, halves, idx_ref, x_ref, k_ref, xs_ref, *refs):
    outs, wide = refs[: len(terms)], refs[len(terms)]
    n, rows = x_ref.shape[:2]
    size = n * rows * grain
    step, blocks = pl.program_id(0), pl.num_programs(0)
    lanes = x_ref.shape[3] // halves
    for g in range(n * rows):
        line = x_ref[g // rows, g % rows].astype(F32)
        for q in range(slabs):
            at = q * size + g * grain
            wide[at : at + grain, :] = line[q * grain : (q + 1) * grain, :]
    for h in range(halves):
        src = lanes_at((h ^ idx_ref[0]) * lanes if halves > 1 else 0, lanes)
        dst = lanes_at((h * blocks + step) * lanes, lanes)
        for q in range(slabs):
            here = slice(q * size, (q + 1) * size)
            xs_ref[here, dst] = wide[here, src].astype(BF16)
        for t, (_, _, reach) in enumerate(terms):
            taps = [k_ref[0, 3 * t + i : 3 * t + i + 1, src] for i in range(3)]
            for q in range(slabs):
                total = None
                for i, side in enumerate(SIDES):
                    if span(slabs, q, side, reach):
                        at = (q + side * reach) * size
                        term = wide[at : at + size, src] * taps[i]
                        total = term if total is None else total + term
                outs[t][q * size : (q + 1) * size, dst] = total.astype(BF16)


def depthwise_sums(terms, slabs, grain, halves, idx, x, k):
    n, rows, width, channels = x.shape
    cells, (blocks, _, own) = n * rows * width, k.shape
    return pl.pallas_call(
        functools.partial(sums_kernel, terms, slabs, grain, halves),
        grid_spec=pltpu.PrefetchScalarGridSpec(
            num_scalar_prefetch=1,
            grid=(blocks,),
            in_specs=[
                pl.BlockSpec((n, rows, width, own), lambda d, s: (0, 0, 0, s[3 + d])),
                pl.BlockSpec((1, k.shape[1], own), lambda d, s: (d, 0, 0)),
            ],
            out_specs=[WHOLE] * (1 + len(terms)),
            scratch_shapes=[pltpu.VMEM((cells, own), F32)],
        ),
        out_shape=[jax.ShapeDtypeStruct((cells, channels), BF16)] * (1 + len(terms)),
        compiler_params=pltpu.CompilerParams(vmem_limit_bytes=8 * MIB),
        cost_estimate=pl.CostEstimate(
            flops=6 * len(terms) * cells * channels,
            bytes_accessed=2 * (2 + len(terms)) * cells * channels,
            transcendentals=0,
        ),
        name="depthwise_sums",
    )(idx, x, k)


def forward_kernel(branches, parts, add, *refs):
    w_refs, refs = refs[: len(parts)], refs[len(parts) :]
    n = len(branches)
    for t, branch in enumerate(branches):
        total = refs[n + t][...] if add else None
        for w_ref, h in zip(w_refs, parts):
            depth = w_ref.shape[1]
            field = refs[t][:, h * depth : (h + 1) * depth]
            part = jnp.dot(field, w_ref[branch], preferred_element_type=F32)
            total = part if total is None else total + part
        out = refs[len(refs) - n + t]
        out[...] = total.astype(out.dtype)


def forward(branches, dtypes, sums, ws, before=None):
    cells = sums[0].shape[0]
    first = next(iter(ws.values()))
    depth, co = first.shape[1:]
    args = [*ws.values(), *sums, *(before or [])]
    return pl.pallas_call(
        functools.partial(forward_kernel, branches, tuple(ws), before is not None),
        in_specs=[WHOLE] * len(args),
        out_specs=[WHOLE] * len(sums),
        out_shape=[jax.ShapeDtypeStruct((cells, co), dt) for dt in dtypes],
        compiler_params=pltpu.CompilerParams(vmem_limit_bytes=8 * MIB),
        cost_estimate=pl.CostEstimate(
            flops=2 * len(sums) * cells * depth * len(ws) * co,
            bytes_accessed=2 * len(sums) * cells * depth * len(ws),
            transcendentals=0,
        ),
        name="forward_terms",
    )(*args)


def back(g, weight):
    return lax.dot_general(g, weight, (((1,), (1,)), ((), ())), preferred_element_type=F32)


def weight_kernel(terms, slabs, halves, quarters, last, branch, idx_ref, x_ref, w_ref, *refs):
    n = len(terms)
    g_refs, d_refs, refs = refs[:n], refs[n : 2 * n], refs[2 * n :]
    if last:
        w_before, k_before, *outs, gt, gd, kacc, pieces = refs
    else:
        w_out, k_out, gt, gd, kacc = refs
    step, blocks = pl.program_id(0), pl.num_programs(0)
    own, co = kacc.shape[1], w_ref.shape[2]
    size = g_refs[0].shape[0] // slabs
    lanes = own // halves
    block = lanes_at(step * own, own)

    @pl.when(step == 0)
    def _():
        for t in range(n):
            gt[t] = g_refs[t][...].T

    for t in range(n):
        gd[t] = back(g_refs[t][...], w_ref[branch, block, :])
    total = w_before[step] if last else None
    for t in range(n):
        part = jnp.dot(gt[t], d_refs[t][:, block], preferred_element_type=F32)
        total = part if total is None else total + part
    per = co // quarters
    if last:
        for h in range(halves):
            for q in range(quarters):
                rows = total[q * per : (q + 1) * per, h * lanes : (h + 1) * lanes]
                pieces[h, q, :per, :] = rows.astype(BF16)
    else:
        w_out[step] = total
    kacc[...] = k_before[step] if last else jnp.zeros_like(kacc)
    upper = idx_ref[2] > 0
    for h in range(halves):
        cols = slice(h * lanes, (h + 1) * lanes)
        there = lanes_at(step * own + h * lanes, lanes)
        sums = [None] * (3 * n)
        for q in range(slabs):
            xq = x_ref[q * size : (q + 1) * size, there].astype(F32)
            for t, (_, _, reach) in enumerate(terms):
                for i, side in enumerate(SIDES):
                    if not span(slabs, q, -side, reach):
                        continue
                    src = (q - side * reach) * size
                    part = xq * gd[t, src : src + size, cols]
                    part = jnp.sum(part.reshape(size // 8, 8, lanes), axis=0)
                    at = 3 * t + i
                    sums[at] = part if sums[at] is None else sums[at] + part
        for t, (_, u, _) in enumerate(terms):
            for i in range(3):
                total = jnp.sum(sums[3 * t + i], axis=0, keepdims=True)
                if u is None:
                    kacc[i : i + 1, cols] = jnp.where(upper, 0.0, total)
                    kacc[i + 6 : i + 7, cols] = jnp.where(upper, total, 0.0)
                else:
                    row = 3 * (u + 1) + i
                    kacc[row : row + 1, cols] = total
    if not last:
        k_out[step] = kacc[...]
        return
    taps = TAP_ROWS // quarters
    for h in range(halves):
        for q in range(quarters):
            rows = kacc[q * taps : (q + 1) * taps, h * lanes : (h + 1) * lanes]
            pieces[h, q, per:, :] = rows.astype(BF16)

    def put(out, which):
        for e in range(quarters):
            at = e ^ idx_ref[1] if quarters > 1 else 0
            for h in range(halves):
                out[e, (step - which * (blocks // halves)) * halves + h] = pieces[h, at]

    for which in range(halves):
        mine = step // (blocks // halves) == which
        pl.when(mine)(functools.partial(put, outs[which], which))


def weight_grads(terms, slabs, halves, quarters, blocks, idx, x, w, gs, ds, before=None):
    cells, channels = x.shape
    own, co = channels // blocks, w.shape[2]
    n, branch = len(terms), terms[0][0]
    last = before is not None
    args = [x, w, *gs, *ds, *(before or ())]
    scratch = [
        pltpu.VMEM((n, co, cells), BF16),
        pltpu.VMEM((n, cells, own), F32),
        pltpu.VMEM((TAP_ROWS, own), F32),
    ]
    if last:
        piece = ((co + TAP_ROWS) // quarters, own // halves)
        out_shape = [jax.ShapeDtypeStruct((quarters, blocks) + piece, BF16)] * halves
        scratch.append(pltpu.VMEM((halves, quarters) + piece, BF16))
    else:
        out_shape = [
            jax.ShapeDtypeStruct((blocks, co, own), F32),
            jax.ShapeDtypeStruct((blocks, TAP_ROWS, own), F32),
        ]
    return pl.pallas_call(
        functools.partial(weight_kernel, terms, slabs, halves, quarters, last, branch),
        grid_spec=pltpu.PrefetchScalarGridSpec(
            num_scalar_prefetch=1,
            grid=(blocks,),
            in_specs=[WHOLE] * len(args),
            out_specs=[WHOLE] * len(out_shape),
            scratch_shapes=scratch,
        ),
        out_shape=out_shape,
        compiler_params=pltpu.CompilerParams(vmem_limit_bytes=10 * MIB),
        cost_estimate=pl.CostEstimate(
            flops=4 * n * cells * channels * co,
            bytes_accessed=2 * (n + 1) * cells * channels,
            transcendentals=0,
        ),
        name="weight_outer" if last else "weight_middle",
    )(idx, *args)


def feature_kernel(terms, slabs, grain, halves, add, last, idx_ref, k_ref, w_ref, *refs):
    n = len(terms)
    g_refs, refs = refs[:n], refs[n:]
    before = refs[0] if add else None
    out_ref, gd, weight, *wide = refs[1:] if add else refs
    size = g_refs[0].shape[0] // slabs
    step, blocks = pl.program_id(0), pl.num_programs(0)
    own = weight.shape[1]
    lanes = own // halves
    for h in range(halves):
        at = ((h ^ idx_ref[0] if halves > 1 else 0) * blocks + step) * lanes
        weight[:, h * lanes : (h + 1) * lanes, :] = w_ref[:, lanes_at(at, lanes), :]
    for t, (branch, _, _, _) in enumerate(terms):
        gd[t] = back(g_refs[t][...], weight[branch])
    for h in range(halves):
        cols = slice(h * lanes, (h + 1) * lanes)
        for q in range(slabs):
            here = slice(q * size, (q + 1) * size)
            acc = before[step, here, cols] if add else None
            for t, (_, _, reach, row) in enumerate(terms):
                for i, side in enumerate(SIDES):
                    if not span(slabs, q, -side, reach):
                        continue
                    src = (q - side * reach) * size
                    term = gd[t, src : src + size, cols] * k_ref[0, row + i : row + i + 1, cols]
                    acc = term if acc is None else acc + term
            if not last:
                out_ref[step, here, cols] = acc
                continue
            for g in range(wide[0].shape[0]):
                wide[0][g, q * grain : (q + 1) * grain, cols] = acc[g * grain : (g + 1) * grain, :]
    if last:
        rows = out_ref.shape[1]
        for g in range(wide[0].shape[0]):
            out_ref[g // rows, g % rows] = wide[0][g].astype(BF16)


def feature_grads(terms, slabs, grain, halves, idx, shape, last, k, w, gs, before=None):
    images, rows, width, channels = shape
    blocks, _, own = k.shape
    cells, co = gs[0].shape
    n = len(terms)
    scratch = [pltpu.VMEM((n, cells, own), F32), pltpu.VMEM((2, own, co), BF16)]
    if last:
        out_spec = pl.BlockSpec((images, rows, width, own), lambda d, s: (0, 0, 0, s[3 + d]))
        out_shape = jax.ShapeDtypeStruct(shape, BF16)
        scratch.append(pltpu.VMEM((images * rows, width, own), F32))
    else:
        out_spec, out_shape = WHOLE, jax.ShapeDtypeStruct((blocks, cells, own), F32)
    args = [w, *gs] + ([] if before is None else [before])
    return pl.pallas_call(
        functools.partial(feature_kernel, terms, slabs, grain, halves, before is not None, last),
        grid_spec=pltpu.PrefetchScalarGridSpec(
            num_scalar_prefetch=1,
            grid=(blocks,),
            in_specs=[pl.BlockSpec((1,) + k.shape[1:], lambda d, s: (d, 0, 0))]
            + [WHOLE] * len(args),
            out_specs=out_spec,
            scratch_shapes=scratch,
        ),
        out_shape=out_shape,
        compiler_params=pltpu.CompilerParams(vmem_limit_bytes=14 * MIB),
        cost_estimate=pl.CostEstimate(
            flops=2 * n * cells * channels * co,
            bytes_accessed=4 * cells * channels,
            transcendentals=0,
        ),
        name="feature_last" if last else "feature_first",
    )(idx, k, *args)


def turn_kernel(slabs, grain, count, has_out, cot_ref, centre_ref, *refs):
    received, refs = refs[:count], refs[count + has_out :]
    g_ref, out_ref, flat, wide = refs
    n, rows = cot_ref.shape[:2]
    size = n * rows * grain
    for g in range(n * rows):
        line = cot_ref[g // rows, g % rows].astype(F32)
        for q in range(slabs):
            at = q * size + g * grain
            flat[at : at + grain, :] = line[q * grain : (q + 1) * grain, :]
    for q in range(slabs):
        here = slice(q * size, (q + 1) * size)
        pre = centre_ref[here, :]
        for ref in received:
            pre = pre + ref[here, :].astype(F32)
        sig = jax.nn.sigmoid(pre)
        g_ref[here, :] = (flat[here, :] * sig * (1.0 + pre * (1.0 - sig))).astype(BF16)
        out = pre * sig
        for g in range(n * rows):
            wide[g, q * grain : (q + 1) * grain, :] = out[g * grain : (g + 1) * grain, :]
    for g in range(n * rows):
        out_ref[g // rows, g % rows] = wide[g].astype(BF16)


def turn(slabs, grain, branch, cotangent, centre, received, outputs):
    n, rows, width, _ = cotangent.shape
    cells, co = centre.shape
    natural = pl.BlockSpec((n, rows, width, co), lambda i: (0, 0, 0, branch))
    has_out = outputs is not None
    args = [cotangent, centre, *received] + ([outputs] if has_out else [])
    specs = [natural] + [WHOLE] * (1 + len(received))
    return pl.pallas_call(
        functools.partial(turn_kernel, slabs, grain, len(received), has_out),
        grid=(1,),
        in_specs=specs + [pl.BlockSpec(memory_space=pl.ANY)] * has_out,
        out_specs=[WHOLE, natural],
        out_shape=[
            jax.ShapeDtypeStruct((cells, co), BF16),
            jax.ShapeDtypeStruct(cotangent.shape, BF16),
        ],
        scratch_shapes=[
            pltpu.VMEM((cells, co), F32),
            pltpu.VMEM((n * rows, width, co), F32),
        ],
        input_output_aliases={len(args) - 1: 1} if has_out else {},
        compiler_params=pltpu.CompilerParams(vmem_limit_bytes=8 * MIB),
        cost_estimate=pl.CostEstimate(
            flops=12 * cells * co, bytes_accessed=8 * cells * co, transcendentals=2 * cells * co
        ),
        name="turn",
    )(*args)


def finish_kernel(factor, halves, quarters, idx_ref, *refs):
    ins, (w_ref, k_ref, wide, taps_of) = refs[:halves], refs[halves:]
    co = w_ref.shape[2]
    per, taps = co // quarters, TAP_ROWS // quarters
    lanes = ins[0].shape[3]
    for branch in range(2):
        for q in range(quarters):
            at = q ^ idx_ref[1] if quarters > 1 else 0
            blocks = [ref[at, branch].astype(F32) * factor for ref in ins]
            if halves == 2:
                low = idx_ref[0] == 0
                blocks = [jnp.where(low, *blocks), jnp.where(low, *blocks[::-1])]
            for h, block in enumerate(blocks):
                cols = slice(h * lanes, (h + 1) * lanes)
                wide[q * per : (q + 1) * per, cols] = block[:per]
                taps_of[q * taps : (q + 1) * taps, cols] = block[per:]
        w_ref[branch] = wide[...].T
        for t in range(k_ref.shape[0]):
            k_ref[t, branch : branch + 1, :] = taps_of[t : t + 1, :]


def finish(idx, pieces, own, factor):
    halves = len(pieces)
    quarters, _, rows, _ = pieces[0].shape
    co = rows * quarters - TAP_ROWS
    w, k = pl.pallas_call(
        functools.partial(finish_kernel, factor, halves, quarters),
        in_specs=[pl.BlockSpec(memory_space=pltpu.SMEM)] + [WHOLE] * halves,
        out_specs=[WHOLE] * 2,
        out_shape=[
            jax.ShapeDtypeStruct((2, own, co), F32),
            jax.ShapeDtypeStruct((9, 2, own), F32),
        ],
        scratch_shapes=[pltpu.VMEM((co, own), F32), pltpu.VMEM((TAP_ROWS, own), F32)],
        name="finish_grads",
    )(idx, *pieces)
    return w, k.transpose(1, 0, 2)


def pyramid(features, pointwise, depthwise, cotangent):
    n, rows, width, _ = features.shape
    own, co = pointwise.shape[1:]
    space, dp = lax.axis_size("space"), lax.axis_size("dp")
    me, row = lax.axis_index("space"), lax.axis_index("dp")
    chips = space // 2
    halves = 2 if space % 2 == 0 and own % 256 == 0 and dp % 2 == 0 else 1
    part_c = own // halves
    even = chips & (chips - 1) == 0 and TAP_ROWS % (8 * chips) == 0 and co % (16 * chips) == 0
    quarters = chips if halves == 2 and even else 1
    core, chip = me % 2, me // 2

    grain = math.gcd(*RATES)
    slabs = width // grain

    terms, moves = [], []
    for branch, rate in enumerate(RATES):
        offset, reach = rate // rows, rate // grain
        terms.append((branch, 0, reach))
        moves.append(0)
        if 2 * offset == space:
            terms.append((branch, None, reach))
            moves.append(offset)
        elif offset < space:
            for u in (-1, 1):
                terms.append((branch, u, reach))
                moves.append(u * offset)
    middle = [t for t, m in enumerate(moves) if m == 0]
    outer = [t for t, m in enumerate(moves) if m != 0]
    half_way = next((moves[t] for t in outer if terms[t][1] is None), space)
    upper = (me >= half_way).astype(jnp.int32)

    def send(value, t, direction):
        if terms[t][1] is None:
            return cycle(value, "space", moves[t])
        return shift(value, "space", direction * moves[t])

    idx = jnp.concatenate(
        [
            jnp.stack([core, chip, upper]).astype(jnp.int32),
            (row + dp - jnp.arange(dp)).astype(jnp.int32) % dp,
        ]
    )

    taps = depthwise.transpose(1, 0, 2)
    k_all = [taps] + [cycle(taps, "dp", d) for d in range(1, dp)]
    mine = pointwise
    if halves == 2:
        mine = lax.dynamic_slice_in_dim(pointwise, core * part_c, part_c, axis=1)
    mine = [mine] + [cycle(mine, "dp", d) for d in range(1, dp)]

    k_rows = jnp.stack(k_all).astype(F32).transpose(0, 2, 1, 3).reshape(dp, 18, own)
    k_terms = []
    for branch, u, _ in terms:
        at = branch * 9
        if u is None:
            k_terms.append(
                jnp.where(upper > 0, k_rows[:, at + 6 : at + 9], k_rows[:, at : at + 3])
            )
        else:
            k_terms.append(k_rows[:, at + 3 * (u + 1) : at + 3 * (u + 1) + 3])

    taps_all = jnp.concatenate(k_terms, axis=1)
    taps_all = jnp.pad(taps_all, ((0, 0), (0, -taps_all.shape[1] % 8), (0, 0)))

    x, *sums = depthwise_sums(terms, slabs, grain, halves, idx, features, taps_all)
    x, sums, mine = lax.optimization_barrier((x, sums, mine))
    ws = {0: jnp.concatenate(mine, axis=1)}
    if halves == 2:
        ws[1] = swap(ws[0], "space", 1)
    w = jnp.concatenate(list(ws.values()), axis=1)

    held = lax.optimization_barrier
    pick = lambda values, chosen: [values[t] for t in chosen]
    mid = [[t for t in middle if terms[t][0] == b] for b in range(2)]
    out = [[t for t in outer if terms[t][0] == b] for b in range(2)]

    order = (1, 0)
    parts, received, outputs, gs = [None] * len(terms), {}, None, [None] * len(terms)
    early = out[order[0]] + out[order[1]]
    begun, rest = {t: None for t in early}, ws
    if halves == 2:
        some = forward([terms[t][0] for t in early], [F32] * len(early), pick(sums, early), {0: ws[0]})
        begun, rest = dict(zip(early, some)), {1: ws[1]}
    for b in order:
        count = len(out[b])
        before = [begun[t] for t in out[b]] if halves == 2 else None
        ready = forward([b] * count, [BF16] * count, pick(sums, out[b]), rest, before)
        for t, part in zip(out[b], ready):
            parts[t] = part
        received[b] = [send(parts[t], t, -1) for t in out[b]]
        if b == order[0]:
            _, sums = held((pick(parts, out[b]), sums))
    chosen = mid[1] + mid[0]
    centre = forward([terms[t][0] for t in chosen], [F32] * 2, pick(sums, chosen), ws)
    for t, part in zip(chosen, centre):
        parts[t] = part

    common = (slabs, halves, quarters, dp, idx, x, w)
    first, grads, summed = [None] * 2, [None] * 2, [None] * 2
    for b in order:
        t = mid[b][0]
        if b == order[1]:
            received[b], first[order[0]] = held((received[b], first[order[0]]))
        gs[t], outputs = turn(slabs, grain, b, cotangent, parts[t], received[b], outputs)
        for o in out[b]:
            gs[o] = send(gs[t], o, 1)
        first[b] = weight_grads(pick(terms, mid[b]), *common, pick(gs, mid[b]), pick(sums, mid[b]))
    last_g = pick(gs, out[order[1]])

    def feature_part(chosen, fields, last, before=None):
        rows_of = [terms[t] + (3 * t,) for t in chosen]
        return feature_grads(
            rows_of, slabs, grain, halves, idx, features.shape, last, taps_all, w,
            pick(fields, chosen), before,
        )

    for b in order:
        if b == order[0]:
            grad_g = pick(gs, out[b])
            grad_g, first[order[1]] = held((grad_g, first[order[1]]))
            for t, field in zip(out[b], grad_g):
                gs[t] = field
        else:
            grad_g = last_g
        grads[b] = weight_grads(pick(terms, out[b]), *common, grad_g, pick(sums, out[b]), first[b])
        kept = grads[b][0]
        if halves == 2:
            kept = (kept.astype(F32) + swap(grads[b][1], "space", 1).astype(F32)).astype(BF16)
        if b == order[0]:
            feature_grad = feature_part(mid[0] + mid[1] + out[b], gs, False)
            last_g, kept, feature_grad = held((last_g, kept, feature_grad))
        else:
            last_g, kept = held((last_g, kept))
            for t, field in zip(out[b], last_g):
                gs[t] = field
        summed[b] = [kept[0]] + [swap(kept[e], "space", 2 * e) for e in range(1, quarters)]
    feature_grad = feature_part(out[order[1]], gs, True, feature_grad)

    factor = 1.0 / math.sqrt(dp * n * space * rows * width)
    total = jnp.stack([sum(p.astype(F32) for p in pieces) for pieces in summed], axis=1)
    total = total.astype(BF16)
    mine = total[0].astype(F32)
    for d in range(1, dp):
        mine = mine + cycle(total[d], "dp", -d).astype(F32)
    if quarters > 1:
        mine = mine.astype(BF16)
        block = jnp.stack([mine] + [swap(mine, "space", 2 * e) for e in range(1, quarters)])
    else:
        peers = [[i for i in range(space) if i % halves == c] for c in range(halves)]
        block = lax.psum(mine, "space", axis_index_groups=peers)[None]
    block = [block, swap(block, "space", 1)] if halves == 2 else [block]
    pointwise_grad, depthwise_grad = finish(idx, block, own, factor)
    return outputs, feature_grad, pointwise_grad, depthwise_grad


def solution(mesh):
    return jax.shard_map(
        pyramid,
        mesh=mesh,
        in_specs=(
            P("dp", "space", None, None),
            P(None, "dp", None),
            P(None, None, "dp"),
            P("dp", "space", None, None),
        ),
        out_specs=(
            P("dp", "space", None, None),
            P("dp", "space", None, None),
            P(None, "dp", None),
            P(None, None, "dp"),
        ),
        check_vma=False,
    )
```

```python
import functools
import math

import jax
import jax.numpy as jnp
from jax import lax
from jax.experimental import pallas as pl
from jax.experimental.pallas import tpu as pltpu
from jax.sharding import PartitionSpec as P


RATES = (12, 24)
SIDES = (-1, 0, 1)
F32 = jnp.float32
BF16 = jnp.bfloat16
TAP_ROWS = 32
MIB = 1 << 20


def shift(value, axis, steps):
    count = lax.axis_size(axis)
    first, last = max(0, -steps), min(count, count - steps)
    return lax.ppermute(value, axis, [(i, i + steps) for i in range(first, last)])


def cycle(value, axis, steps):
    count = lax.axis_size(axis)
    return lax.ppermute(value, axis, [(i, (i + steps) % count) for i in range(count)])


def swap(value, axis, mask):
    count = lax.axis_size(axis)
    return lax.ppermute(value, axis, [(i, i ^ mask) for i in range(count)])


def span(slabs, q, side, reach):
    return 0 <= q + side * reach < slabs


WHOLE = pl.BlockSpec(memory_space=pltpu.VMEM)


def lanes_at(start, count):
    return pl.ds(start if isinstance(start, int) else pl.multiple_of(start, count), count)


def sums_kernel(terms, slabs, grain, halves, idx_ref, x_ref, k_ref, xs_ref, *refs):
    outs, wide = refs[: len(terms)], refs[len(terms)]
    n, rows = x_ref.shape[:2]
    size = n * rows * grain
    step, blocks = pl.program_id(0), pl.num_programs(0)
    lanes = x_ref.shape[3] // halves
    for g in range(n * rows):
        line = x_ref[g // rows, g % rows].astype(F32)
        for q in range(slabs):
            at = q * size + g * grain
            wide[at : at + grain, :] = line[q * grain : (q + 1) * grain, :]
    for h in range(halves):
        src = lanes_at((h ^ idx_ref[0]) * lanes if halves > 1 else 0, lanes)
        dst = lanes_at((h * blocks + step) * lanes, lanes)
        for q in range(slabs):
            here = slice(q * size, (q + 1) * size)
            xs_ref[here, dst] = wide[here, src].astype(BF16)
        for t, (_, _, reach) in enumerate(terms):
            taps = [k_ref[0, 3 * t + i : 3 * t + i + 1, src] for i in range(3)]
            for q in range(slabs):
                total = None
                for i, side in enumerate(SIDES):
                    if span(slabs, q, side, reach):
                        at = (q + side * reach) * size
                        term = wide[at : at + size, src] * taps[i]
                        total = term if total is None else total + term
                outs[t][q * size : (q + 1) * size, dst] = total.astype(BF16)


def depthwise_sums(terms, slabs, grain, halves, idx, x, k):
    n, rows, width, channels = x.shape
    cells, (blocks, _, own) = n * rows * width, k.shape
    return pl.pallas_call(
        functools.partial(sums_kernel, terms, slabs, grain, halves),
        grid_spec=pltpu.PrefetchScalarGridSpec(
            num_scalar_prefetch=1,
            grid=(blocks,),
            in_specs=[
                pl.BlockSpec((n, rows, width, own), lambda d, s: (0, 0, 0, s[3 + d])),
                pl.BlockSpec((1, k.shape[1], own), lambda d, s: (d, 0, 0)),
            ],
            out_specs=[WHOLE] * (1 + len(terms)),
            scratch_shapes=[pltpu.VMEM((cells, own), F32)],
        ),
        out_shape=[jax.ShapeDtypeStruct((cells, channels), BF16)] * (1 + len(terms)),
        compiler_params=pltpu.CompilerParams(vmem_limit_bytes=8 * MIB),
        cost_estimate=pl.CostEstimate(
            flops=6 * len(terms) * cells * channels,
            bytes_accessed=2 * (2 + len(terms)) * cells * channels,
            transcendentals=0,
        ),
        name="depthwise_sums",
    )(idx, x, k)


def forward_kernel(branches, parts, add, *refs):
    n = len(branches)
    count = len(parts) * len(set(branches))
    all_refs, refs = refs[:count], refs[count:]
    for t, branch in enumerate(branches):
        total = refs[n + t][...] if add else None
        at = sorted(set(branches)).index(branch) * len(parts)
        for w_ref, h in zip(all_refs[at : at + len(parts)], parts):
            depth = w_ref.shape[0]
            field = refs[t][:, h * depth : (h + 1) * depth]
            part = jnp.dot(field, w_ref[...], preferred_element_type=F32)
            total = part if total is None else total + part
        out = refs[len(refs) - n + t]
        out[...] = total.astype(out.dtype)


def forward(branches, dtypes, sums, ws, before=None):
    cells = sums[0].shape[0]
    used = [ws[h][b] for b in sorted(set(branches)) for h in ws]
    depth, co = used[0].shape
    args = [*used, *sums, *(before or [])]
    return pl.pallas_call(
        functools.partial(forward_kernel, branches, tuple(ws), before is not None),
        in_specs=[WHOLE] * len(args),
        out_specs=[WHOLE] * len(sums),
        out_shape=[jax.ShapeDtypeStruct((cells, co), dt) for dt in dtypes],
        compiler_params=pltpu.CompilerParams(vmem_limit_bytes=8 * MIB),
        cost_estimate=pl.CostEstimate(
            flops=2 * len(sums) * cells * depth * len(ws) * co,
            bytes_accessed=2 * len(sums) * cells * depth * len(ws),
            transcendentals=0,
        ),
        name="forward_terms",
    )(*args)


def back(g, weight):
    return lax.dot_general(g, weight, (((1,), (1,)), ((), ())), preferred_element_type=F32)


def weight_kernel(terms, slabs, halves, quarters, last, idx_ref, x_ref, w_ref, *refs):
    n = len(terms)
    g_refs, d_refs, refs = refs[:n], refs[n : 2 * n], refs[2 * n :]
    if last:
        w_before, k_before, *outs, gt, gd, kacc, pieces = refs
        outs = outs[-halves:]
    else:
        w_out, k_out, gt, gd, kacc = refs
    step, blocks = pl.program_id(0), pl.num_programs(0)
    own, co = kacc.shape[1], w_ref.shape[1]
    size = g_refs[0].shape[0] // slabs
    lanes = own // halves
    block = lanes_at(step * own, own)

    @pl.when(step == 0)
    def _():
        for t in range(n):
            gt[t] = g_refs[t][...].T

    for t in range(n):
        gd[t] = back(g_refs[t][...], w_ref[block, :])
    total = w_before[step] if last else None
    for t in range(n):
        part = jnp.dot(gt[t], d_refs[t][:, block], preferred_element_type=F32)
        total = part if total is None else total + part
    per = co // quarters
    if last:
        for h in range(halves):
            for q in range(quarters):
                rows = total[q * per : (q + 1) * per, h * lanes : (h + 1) * lanes]
                pieces[h, q, :per, :] = rows.astype(BF16)
    else:
        w_out[step] = total
    kacc[...] = k_before[step] if last else jnp.zeros_like(kacc)
    upper = idx_ref[2] > 0
    for h in range(halves):
        cols = slice(h * lanes, (h + 1) * lanes)
        there = lanes_at(step * own + h * lanes, lanes)
        sums = [None] * (3 * n)
        for q in range(slabs):
            xq = x_ref[q * size : (q + 1) * size, there].astype(F32)
            for t, (_, _, reach) in enumerate(terms):
                for i, side in enumerate(SIDES):
                    if not span(slabs, q, -side, reach):
                        continue
                    src = (q - side * reach) * size
                    part = xq * gd[t, src : src + size, cols]
                    part = jnp.sum(part.reshape(size // 8, 8, lanes), axis=0)
                    at = 3 * t + i
                    sums[at] = part if sums[at] is None else sums[at] + part
        for t, (_, u, _) in enumerate(terms):
            for i in range(3):
                total = jnp.sum(sums[3 * t + i], axis=0, keepdims=True)
                if u is None:
                    kacc[i : i + 1, cols] = jnp.where(upper, 0.0, total)
                    kacc[i + 6 : i + 7, cols] = jnp.where(upper, total, 0.0)
                else:
                    row = 3 * (u + 1) + i
                    kacc[row : row + 1, cols] = total
    if not last:
        k_out[step] = kacc[...]
        return
    taps = TAP_ROWS // quarters
    for h in range(halves):
        for q in range(quarters):
            rows = kacc[q * taps : (q + 1) * taps, h * lanes : (h + 1) * lanes]
            pieces[h, q, per:, :] = rows.astype(BF16)

    def put(out, which):
        for e in range(quarters):
            at = e ^ idx_ref[1] if quarters > 1 else 0
            for h in range(halves):
                out[e, (step - which * (blocks // halves)) * halves + h, terms[0][0]] = pieces[h, at]

    for which in range(halves):
        mine = step // (blocks // halves) == which
        pl.when(mine)(functools.partial(put, outs[which], which))


def weight_grads(terms, slabs, halves, quarters, blocks, idx, x, w, gs, ds, before=None, into=()):
    cells, channels = x.shape
    own, co = channels // blocks, w.shape[1]
    n = len(terms)
    last = before is not None
    args = [x, w, *gs, *ds, *(before or ()), *into]
    scratch = [
        pltpu.VMEM((n, co, cells), BF16),
        pltpu.VMEM((n, cells, own), F32),
        pltpu.VMEM((TAP_ROWS, own), F32),
    ]
    if last:
        piece = ((co + TAP_ROWS) // quarters, own // halves)
        out_shape = [jax.ShapeDtypeStruct((quarters, blocks, 2) + piece, BF16)] * halves
        scratch.append(pltpu.VMEM((halves, quarters) + piece, BF16))
    else:
        out_shape = [
            jax.ShapeDtypeStruct((blocks, co, own), F32),
            jax.ShapeDtypeStruct((blocks, TAP_ROWS, own), F32),
        ]
    return pl.pallas_call(
        functools.partial(weight_kernel, terms, slabs, halves, quarters, last),
        grid_spec=pltpu.PrefetchScalarGridSpec(
            num_scalar_prefetch=1,
            grid=(blocks,),
            in_specs=[WHOLE] * len(args),
            out_specs=[WHOLE] * len(out_shape),
            scratch_shapes=scratch,
        ),
        out_shape=out_shape,
        input_output_aliases={1 + len(args) - len(into) + i: i for i in range(len(into))},
        compiler_params=pltpu.CompilerParams(vmem_limit_bytes=10 * MIB),
        cost_estimate=pl.CostEstimate(
            flops=4 * n * cells * channels * co,
            bytes_accessed=2 * (n + 1) * cells * channels,
            transcendentals=0,
        ),
        name="weight_outer" if last else "weight_middle",
    )(idx, *args)


def feature_kernel(terms, slabs, grain, halves, idx_ref, k_ref, *refs):
    n = len(terms)
    w_refs, g_refs, (out_ref, gd, weight, wide) = refs[:2], refs[2 : 2 + n], refs[2 + n :]
    size = g_refs[0].shape[0] // slabs
    step, blocks = pl.program_id(0), pl.num_programs(0)
    own = weight.shape[1]
    lanes = own // halves
    for h in range(halves):
        at = ((h ^ idx_ref[0] if halves > 1 else 0) * blocks + step) * lanes
        for branch in range(2):
            rows = w_refs[branch][lanes_at(at, lanes), :]
            weight[branch, h * lanes : (h + 1) * lanes, :] = rows
    for t, (branch, _, _) in enumerate(terms):
        gd[t] = back(g_refs[t][...], weight[branch])
    for h in range(halves):
        cols = slice(h * lanes, (h + 1) * lanes)
        for q in range(slabs):
            acc = None
            for t, (_, _, reach) in enumerate(terms):
                for i, side in enumerate(SIDES):
                    if not span(slabs, q, -side, reach):
                        continue
                    src = (q - side * reach) * size
                    term = gd[t, src : src + size, cols] * k_ref[0, 3 * t + i : 3 * t + i + 1, cols]
                    acc = term if acc is None else acc + term
            for g in range(wide.shape[0]):
                wide[g, q * grain : (q + 1) * grain, cols] = acc[g * grain : (g + 1) * grain, :]
    rows = out_ref.shape[1]
    for g in range(wide.shape[0]):
        out_ref[g // rows, g % rows] = wide[g].astype(BF16)


def feature_grads(terms, slabs, grain, halves, idx, shape, k, w, gs):
    images, rows, width, channels = shape
    blocks, _, own = k.shape
    cells, co = gs[0].shape
    n = len(terms)
    args = [*w, *gs]
    return pl.pallas_call(
        functools.partial(feature_kernel, terms, slabs, grain, halves),
        grid_spec=pltpu.PrefetchScalarGridSpec(
            num_scalar_prefetch=1,
            grid=(blocks,),
            in_specs=[pl.BlockSpec((1,) + k.shape[1:], lambda d, s: (d, 0, 0))]
            + [WHOLE] * len(args),
            out_specs=pl.BlockSpec((images, rows, width, own), lambda d, s: (0, 0, 0, s[3 + d])),
            scratch_shapes=[
                pltpu.VMEM((n, cells, own), F32),
                pltpu.VMEM((2, own, co), BF16),
                pltpu.VMEM((images * rows, width, own), F32),
            ],
        ),
        out_shape=jax.ShapeDtypeStruct(shape, BF16),
        compiler_params=pltpu.CompilerParams(vmem_limit_bytes=18 * MIB),
        cost_estimate=pl.CostEstimate(
            flops=2 * n * cells * channels * co,
            bytes_accessed=4 * cells * channels,
            transcendentals=0,
        ),
        name="feature_grads",
    )(idx, k, *args)


def turn_kernel(slabs, grain, count, has_out, cot_ref, centre_ref, *refs):
    received, refs = refs[:count], refs[count + has_out :]
    g_ref, out_ref, flat, wide = refs
    n, rows = cot_ref.shape[:2]
    size = n * rows * grain
    for g in range(n * rows):
        line = cot_ref[g // rows, g % rows].astype(F32)
        for q in range(slabs):
            at = q * size + g * grain
            flat[at : at + grain, :] = line[q * grain : (q + 1) * grain, :]
    for q in range(slabs):
        here = slice(q * size, (q + 1) * size)
        pre = centre_ref[here, :]
        for ref in received:
            pre = pre + ref[here, :].astype(F32)
        sig = jax.nn.sigmoid(pre)
        g_ref[here, :] = (flat[here, :] * sig * (1.0 + pre * (1.0 - sig))).astype(BF16)
        out = pre * sig
        for g in range(n * rows):
            wide[g, q * grain : (q + 1) * grain, :] = out[g * grain : (g + 1) * grain, :]
    for g in range(n * rows):
        out_ref[g // rows, g % rows] = wide[g].astype(BF16)


def turn(slabs, grain, branch, cotangent, centre, received, outputs):
    n, rows, width, _ = cotangent.shape
    cells, co = centre.shape
    natural = pl.BlockSpec((n, rows, width, co), lambda i: (0, 0, 0, branch))
    has_out = outputs is not None
    args = [cotangent, centre, *received] + ([outputs] if has_out else [])
    specs = [natural] + [WHOLE] * (1 + len(received))
    return pl.pallas_call(
        functools.partial(turn_kernel, slabs, grain, len(received), has_out),
        grid=(1,),
        in_specs=specs + [pl.BlockSpec(memory_space=pl.ANY)] * has_out,
        out_specs=[WHOLE, natural],
        out_shape=[
            jax.ShapeDtypeStruct((cells, co), BF16),
            jax.ShapeDtypeStruct(cotangent.shape, BF16),
        ],
        scratch_shapes=[
            pltpu.VMEM((cells, co), F32),
            pltpu.VMEM((n * rows, width, co), F32),
        ],
        input_output_aliases={len(args) - 1: 1} if has_out else {},
        compiler_params=pltpu.CompilerParams(vmem_limit_bytes=8 * MIB),
        cost_estimate=pl.CostEstimate(
            flops=12 * cells * co, bytes_accessed=8 * cells * co, transcendentals=2 * cells * co
        ),
        name="turn",
    )(*args)


def finish_kernel(factor, halves, quarters, idx_ref, *refs):
    ins, (w_ref, k_ref, wide, taps_of) = refs[:halves], refs[halves:]
    co = w_ref.shape[2]
    per, taps = co // quarters, TAP_ROWS // quarters
    lanes = ins[0].shape[3]
    for branch in range(2):
        for q in range(quarters):
            at = q ^ idx_ref[1] if quarters > 1 else 0
            blocks = [ref[at, branch].astype(F32) * factor for ref in ins]
            if halves == 2:
                low = idx_ref[0] == 0
                blocks = [jnp.where(low, *blocks), jnp.where(low, *blocks[::-1])]
            for h, block in enumerate(blocks):
                cols = slice(h * lanes, (h + 1) * lanes)
                wide[q * per : (q + 1) * per, cols] = block[:per]
                taps_of[q * taps : (q + 1) * taps, cols] = block[per:]
        w_ref[branch] = wide[...].T
        for t in range(k_ref.shape[0]):
            k_ref[t, branch : branch + 1, :] = taps_of[t : t + 1, :]


def finish(idx, pieces, own, factor):
    halves = len(pieces)
    quarters, _, rows, _ = pieces[0].shape
    co = rows * quarters - TAP_ROWS
    w, k = pl.pallas_call(
        functools.partial(finish_kernel, factor, halves, quarters),
        in_specs=[pl.BlockSpec(memory_space=pltpu.SMEM)] + [WHOLE] * halves,
        out_specs=[WHOLE] * 2,
        out_shape=[
            jax.ShapeDtypeStruct((2, own, co), F32),
            jax.ShapeDtypeStruct((9, 2, own), F32),
        ],
        scratch_shapes=[pltpu.VMEM((co, own), F32), pltpu.VMEM((TAP_ROWS, own), F32)],
        name="finish_grads",
    )(idx, *pieces)
    return w, k.transpose(1, 0, 2)


def pyramid(features, pointwise, depthwise, cotangent):
    n, rows, width, _ = features.shape
    own, co = pointwise.shape[1:]
    space, dp = lax.axis_size("space"), lax.axis_size("dp")
    me, row = lax.axis_index("space"), lax.axis_index("dp")
    chips = space // 2
    halves = 2 if space % 2 == 0 and own % 256 == 0 and dp % 2 == 0 else 1
    part_c = own // halves
    even = chips & (chips - 1) == 0 and TAP_ROWS % (8 * chips) == 0 and co % (16 * chips) == 0
    quarters = chips if halves == 2 and even else 1
    core, chip = me % 2, me // 2

    grain = math.gcd(*RATES)
    slabs = width // grain

    terms, moves = [], []
    for branch, rate in enumerate(RATES):
        offset, reach = rate // rows, rate // grain
        terms.append((branch, 0, reach))
        moves.append(0)
        if 2 * offset == space:
            terms.append((branch, None, reach))
            moves.append(offset)
        elif offset < space:
            for u in (-1, 1):
                terms.append((branch, u, reach))
                moves.append(u * offset)
    middle = [t for t, m in enumerate(moves) if m == 0]
    outer = [t for t, m in enumerate(moves) if m != 0]
    half_way = next((moves[t] for t in outer if terms[t][1] is None), space)
    upper = (me >= half_way).astype(jnp.int32)

    def send(value, t, direction):
        if terms[t][1] is None:
            return cycle(value, "space", moves[t])
        return shift(value, "space", direction * moves[t])

    idx = jnp.concatenate(
        [
            jnp.stack([core, chip, upper]).astype(jnp.int32),
            (row + dp - jnp.arange(dp)).astype(jnp.int32) % dp,
        ]
    )

    taps = depthwise.transpose(1, 0, 2)
    k_all = [taps] + [cycle(taps, "dp", d) for d in range(1, dp)]
    mine = pointwise
    if halves == 2:
        mine = lax.dynamic_slice_in_dim(pointwise, core * part_c, part_c, axis=1)
    gathered = [None] * 2
    order = (1, 0)
    for b in order:
        gathered[b] = [mine[b]] + [cycle(mine[b], "dp", d) for d in range(1, dp)]

    k_rows = jnp.stack(k_all).astype(F32).transpose(0, 2, 1, 3).reshape(dp, 18, own)
    k_terms = []
    for branch, u, _ in terms:
        at = branch * 9
        if u is None:
            k_terms.append(
                jnp.where(upper > 0, k_rows[:, at + 6 : at + 9], k_rows[:, at : at + 3])
            )
        else:
            k_terms.append(k_rows[:, at + 3 * (u + 1) : at + 3 * (u + 1) + 3])

    taps_all = jnp.concatenate(k_terms, axis=1)
    taps_all = jnp.pad(taps_all, ((0, 0), (0, -taps_all.shape[1] % 8), (0, 0)))

    x, *sums = depthwise_sums(terms, slabs, grain, halves, idx, features, taps_all)
    held = lax.optimization_barrier
    pick = lambda values, chosen: [values[t] for t in chosen]
    mid = [[t for t in middle if terms[t][0] == b] for b in range(2)]
    out = [[t for t in outer if terms[t][0] == b] for b in range(2)]

    parts, received, outputs, gs = [None] * len(terms), {}, None, [None] * len(terms)
    ws = {h: [None] * 2 for h in range(halves)}
    before = (x, sums)
    for b in order:
        before, gathered[b] = held((before, gathered[b]))
        if b == order[0]:
            x, sums = before
        chosen = out[b]
        count, begun, last_part = len(chosen), None, 0
        ws[0][b] = jnp.concatenate(gathered[b], axis=0)
        if halves == 2:
            ws[1][b] = swap(ws[0][b], "space", 1)
            begun = forward([b] * count, [F32] * count, pick(sums, chosen), {0: ws[0]})
            last_part = 1
        ready = forward(
            [b] * count, [BF16] * count, pick(sums, chosen), {last_part: ws[last_part]}, begun
        )
        for t, part in zip(chosen, ready):
            parts[t] = part
        received[b] = [send(parts[t], t, -1) for t in chosen]
        before = ready
    w = [jnp.concatenate([ws[h][b] for h in range(halves)], axis=0) for b in range(2)]
    chosen = mid[1] + mid[0]
    centre = forward([terms[t][0] for t in chosen], [F32] * 2, pick(sums, chosen), ws)
    for t, part in zip(chosen, centre):
        parts[t] = part

    common = (slabs, halves, quarters, dp, idx, x)
    first = [None] * 2
    for b in order:
        t = mid[b][0]
        if b == order[1]:
            received[b], first[order[0]] = held((received[b], first[order[0]]))
        gs[t], outputs = turn(slabs, grain, b, cotangent, parts[t], received[b], outputs)
        for o in out[b]:
            gs[o] = send(gs[t], o, 1)
        first[b] = weight_grads(
            pick(terms, mid[b]), *common, w[b], pick(gs, mid[b]), pick(sums, mid[b])
        )
    grads = ()
    for b in order:
        grad_g = pick(gs, out[b])
        if b == order[0]:
            grad_g, first[order[1]] = held((grad_g, first[order[1]]))
        else:
            grad_g, grads = held((grad_g, grads))
        for t, field in zip(out[b], grad_g):
            gs[t] = field
        grads = weight_grads(
            pick(terms, out[b]), *common, w[b], grad_g, pick(sums, out[b]), first[b], grads
        )
    kept = grads[0]
    if halves == 2:
        kept = (kept.astype(F32) + swap(grads[1], "space", 1).astype(F32)).astype(BF16)
    pieces = [kept[e] for e in range(quarters)]
    gs, pieces = held((gs, pieces))
    summed = [pieces[0]] + [swap(pieces[e], "space", 2 * e) for e in range(1, quarters)]
    feature_grad = feature_grads(terms, slabs, grain, halves, idx, features.shape, taps_all, w, gs)

    factor = 1.0 / math.sqrt(dp * n * space * rows * width)
    total = sum(piece.astype(F32) for piece in summed).astype(BF16)
    mine = total[0].astype(F32)
    for d in range(1, dp):
        mine = mine + cycle(total[d], "dp", -d).astype(F32)
    if quarters > 1:
        mine = mine.astype(BF16)
        block = jnp.stack([mine] + [swap(mine, "space", 2 * e) for e in range(1, quarters)])
    else:
        peers = [[i for i in range(space) if i % halves == c] for c in range(halves)]
        block = lax.psum(mine, "space", axis_index_groups=peers)[None]
    block = [block, swap(block, "space", 1)] if halves == 2 else [block]
    pointwise_grad, depthwise_grad = finish(idx, block, own, factor)
    return outputs, feature_grad, pointwise_grad, depthwise_grad


def solution(mesh):
    return jax.shard_map(
        pyramid,
        mesh=mesh,
        in_specs=(
            P("dp", "space", None, None),
            P(None, "dp", None),
            P(None, None, "dp"),
            P("dp", "space", None, None),
        ),
        out_specs=(
            P("dp", "space", None, None),
            P("dp", "space", None, None),
            P(None, "dp", None),
            P(None, None, "dp"),
        ),
        check_vma=False,
    )
```

```python
import functools
import math

import jax
import jax.numpy as jnp
from jax import lax
from jax.experimental import pallas as pl
from jax.experimental.pallas import tpu as pltpu
from jax.sharding import PartitionSpec as P


RATES = (12, 24)
SIDES = (-1, 0, 1)
F32 = jnp.float32
BF16 = jnp.bfloat16
TAP_ROWS = 32
MIB = 1 << 20
FLAGS, FIRST = 2, 5
DYNAMIC = 10


def shift(value, axis, steps):
    count = lax.axis_size(axis)
    first, last = max(0, -steps), min(count, count - steps)
    return lax.ppermute(value, axis, [(i, i + steps) for i in range(first, last)])


def cycle(value, axis, steps):
    count = lax.axis_size(axis)
    return lax.ppermute(value, axis, [(i, (i + steps) % count) for i in range(count)])


def swap(value, axis, mask):
    count = lax.axis_size(axis)
    return lax.ppermute(value, axis, [(i, i ^ mask) for i in range(count)])


def span(slabs, q, side, reach):
    return 0 <= q + side * reach < slabs


WHOLE = pl.BlockSpec(memory_space=pltpu.VMEM)


def lanes_at(start, count):
    return pl.ds(start if isinstance(start, int) else pl.multiple_of(start, count), count)


def sums_kernel(terms, slabs, grain, halves, idx_ref, x_ref, k_ref, xs_ref, *refs):
    outs, wide = refs[: len(terms)], refs[len(terms)]
    n, rows = x_ref.shape[:2]
    size = n * rows * grain
    step, blocks = pl.program_id(0), pl.num_programs(0)
    lanes = x_ref.shape[3] // halves
    for g in range(n * rows):
        line = x_ref[g // rows, g % rows].astype(F32)
        for q in range(slabs):
            at = q * size + g * grain
            wide[at : at + grain, :] = line[q * grain : (q + 1) * grain, :]
    for h in range(halves):
        src = lanes_at((h ^ idx_ref[0]) * lanes if halves > 1 else 0, lanes)
        dst = lanes_at((h * blocks + step) * lanes, lanes)
        for q in range(slabs):
            here = slice(q * size, (q + 1) * size)
            xs_ref[here, dst] = wide[here, src].astype(BF16)
        for t, (_, _, reach) in enumerate(terms):
            taps = [k_ref[0, 3 * t + i : 3 * t + i + 1, src] for i in range(3)]
            for q in range(slabs):
                total = None
                for i, side in enumerate(SIDES):
                    if span(slabs, q, side, reach):
                        at = (q + side * reach) * size
                        term = wide[at : at + size, src] * taps[i]
                        total = term if total is None else total + term
                outs[t][q * size : (q + 1) * size, dst] = total.astype(BF16)


def depthwise_sums(terms, slabs, grain, halves, idx, x, k):
    n, rows, width, channels = x.shape
    cells, (blocks, _, own) = n * rows * width, k.shape
    return pl.pallas_call(
        functools.partial(sums_kernel, terms, slabs, grain, halves),
        grid_spec=pltpu.PrefetchScalarGridSpec(
            num_scalar_prefetch=1,
            grid=(blocks,),
            in_specs=[
                pl.BlockSpec((n, rows, width, own), lambda d, s: (0, 0, 0, s[FIRST + d])),
                pl.BlockSpec((1, k.shape[1], own), lambda d, s: (d, 0, 0)),
            ],
            out_specs=[WHOLE] * (1 + len(terms)),
            scratch_shapes=[pltpu.VMEM((cells, own), F32)],
        ),
        out_shape=[jax.ShapeDtypeStruct((cells, channels), BF16)] * (1 + len(terms)),
        compiler_params=pltpu.CompilerParams(vmem_limit_bytes=8 * MIB),
        cost_estimate=pl.CostEstimate(
            flops=6 * len(terms) * cells * channels,
            bytes_accessed=2 * (2 + len(terms)) * cells * channels,
            transcendentals=0,
        ),
        name="depthwise_sums",
    )(idx, x, k)


def forward_kernel(branches, parts, add, *refs):
    n = len(branches)
    count = len(parts) * len(set(branches))
    all_refs, refs = refs[:count], refs[count:]
    for t, branch in enumerate(branches):
        total = refs[n + t][...] if add else None
        at = sorted(set(branches)).index(branch) * len(parts)
        for w_ref, h in zip(all_refs[at : at + len(parts)], parts):
            depth = w_ref.shape[0]
            field = refs[t][:, h * depth : (h + 1) * depth]
            part = jnp.dot(field, w_ref[...], preferred_element_type=F32)
            total = part if total is None else total + part
        out = refs[len(refs) - n + t]
        out[...] = total.astype(out.dtype)


def forward(branches, dtypes, sums, ws, before=None):
    cells = sums[0].shape[0]
    used = [ws[h][b] for b in sorted(set(branches)) for h in ws]
    depth, co = used[0].shape
    args = [*used, *sums, *(before or [])]
    return pl.pallas_call(
        functools.partial(forward_kernel, branches, tuple(ws), before is not None),
        in_specs=[WHOLE] * len(args),
        out_specs=[WHOLE] * len(sums),
        out_shape=[jax.ShapeDtypeStruct((cells, co), dt) for dt in dtypes],
        compiler_params=pltpu.CompilerParams(vmem_limit_bytes=8 * MIB),
        cost_estimate=pl.CostEstimate(
            flops=2 * len(sums) * cells * depth * len(ws) * co,
            bytes_accessed=2 * len(sums) * cells * depth * len(ws),
            transcendentals=0,
        ),
        name="forward_terms",
    )(*args)


def back(g, weight):
    return lax.dot_general(g, weight, (((1,), (1,)), ((), ())), preferred_element_type=F32)


def weight_kernel(terms, slabs, halves, quarters, last, idx_ref, x_ref, w_ref, *refs):
    n = len(terms)
    g_refs, d_refs, refs = refs[:n], refs[n : 2 * n], refs[2 * n :]
    if last:
        w_before, k_before, *outs, gt, gd, kacc, pieces = refs
        outs = outs[-halves:]
    else:
        w_out, k_out, gt, gd, kacc = refs
    step, blocks = pl.program_id(0), pl.num_programs(0)
    own, co = kacc.shape[1], w_ref.shape[1]
    size = g_refs[0].shape[0] // slabs
    lanes = own // halves
    block = lanes_at(step * own, own)

    @pl.when(step == 0)
    def _():
        for t in range(n):
            gt[t] = g_refs[t][...].T

    for t in range(n):
        gd[t] = back(g_refs[t][...], w_ref[block, :])
    total = w_before[step] if last else None
    for t in range(n):
        part = jnp.dot(gt[t], d_refs[t][:, block], preferred_element_type=F32)
        total = part if total is None else total + part
    per = co // quarters
    if last:
        for h in range(halves):
            for q in range(quarters):
                rows = total[q * per : (q + 1) * per, h * lanes : (h + 1) * lanes]
                pieces[h, q, :per, :] = rows.astype(BF16)
    else:
        w_out[step] = total
    kacc[...] = k_before[step] if last else jnp.zeros_like(kacc)
    for h in range(halves):
        cols = slice(h * lanes, (h + 1) * lanes)
        there = lanes_at(step * own + h * lanes, lanes)
        sums = [None] * (3 * n)
        for q in range(slabs):
            xq = x_ref[q * size : (q + 1) * size, there].astype(F32)
            for t, (_, _, reach) in enumerate(terms):
                for i, side in enumerate(SIDES):
                    if not span(slabs, q, -side, reach):
                        continue
                    src = (q - side * reach) * size
                    part = xq * gd[t, src : src + size, cols]
                    part = jnp.sum(part.reshape(size // 8, 8, lanes), axis=0)
                    at = 3 * t + i
                    sums[at] = part if sums[at] is None else sums[at] + part
        for t, (_, u, _) in enumerate(terms):
            for i in range(3):
                total = jnp.sum(sums[3 * t + i], axis=0, keepdims=True)
                if u >= DYNAMIC:
                    upper = idx_ref[FLAGS + u - DYNAMIC] > 0
                    kacc[i : i + 1, cols] += jnp.where(upper, 0.0, total)
                    kacc[i + 6 : i + 7, cols] += jnp.where(upper, total, 0.0)
                else:
                    row = 3 * (u + 1) + i
                    kacc[row : row + 1, cols] += total
    if not last:
        k_out[step] = kacc[...]
        return
    taps = TAP_ROWS // quarters
    for h in range(halves):
        for q in range(quarters):
            rows = kacc[q * taps : (q + 1) * taps, h * lanes : (h + 1) * lanes]
            pieces[h, q, per:, :] = rows.astype(BF16)

    def put(out, which):
        for e in range(quarters):
            at = e ^ idx_ref[1] if quarters > 1 else 0
            for h in range(halves):
                out[e, (step - which * (blocks // halves)) * halves + h, terms[0][0]] = pieces[h, at]

    for which in range(halves):
        mine = step // (blocks // halves) == which
        pl.when(mine)(functools.partial(put, outs[which], which))


def weight_grads(terms, slabs, halves, quarters, blocks, idx, x, w, gs, ds, before=None, into=()):
    cells, channels = x.shape
    own, co = channels // blocks, w.shape[1]
    n = len(terms)
    last = before is not None
    args = [x, w, *gs, *ds, *(before or ()), *into]
    scratch = [
        pltpu.VMEM((n, co, cells), BF16),
        pltpu.VMEM((n, cells, own), F32),
        pltpu.VMEM((TAP_ROWS, own), F32),
    ]
    if last:
        piece = ((co + TAP_ROWS) // quarters, own // halves)
        out_shape = [jax.ShapeDtypeStruct((quarters, blocks, 2) + piece, BF16)] * halves
        scratch.append(pltpu.VMEM((halves, quarters) + piece, BF16))
    else:
        out_shape = [
            jax.ShapeDtypeStruct((blocks, co, own), F32),
            jax.ShapeDtypeStruct((blocks, TAP_ROWS, own), F32),
        ]
    return pl.pallas_call(
        functools.partial(weight_kernel, terms, slabs, halves, quarters, last),
        grid_spec=pltpu.PrefetchScalarGridSpec(
            num_scalar_prefetch=1,
            grid=(blocks,),
            in_specs=[WHOLE] * len(args),
            out_specs=[WHOLE] * len(out_shape),
            scratch_shapes=scratch,
        ),
        out_shape=out_shape,
        input_output_aliases={1 + len(args) - len(into) + i: i for i in range(len(into))},
        compiler_params=pltpu.CompilerParams(vmem_limit_bytes=10 * MIB),
        cost_estimate=pl.CostEstimate(
            flops=4 * n * cells * channels * co,
            bytes_accessed=2 * (n + 1) * cells * channels,
            transcendentals=0,
        ),
        name="weight_outer" if last else "weight_middle",
    )(idx, *args)


def feature_kernel(terms, slabs, grain, halves, idx_ref, k_ref, *refs):
    n = len(terms)
    w_refs, g_refs, (out_ref, gd, weight, wide) = refs[:2], refs[2 : 2 + n], refs[2 + n :]
    size = g_refs[0].shape[0] // slabs
    step, blocks = pl.program_id(0), pl.num_programs(0)
    own = weight.shape[1]
    lanes = own // halves
    for h in range(halves):
        at = ((h ^ idx_ref[0] if halves > 1 else 0) * blocks + step) * lanes
        for branch in range(2):
            rows = w_refs[branch][lanes_at(at, lanes), :]
            weight[branch, h * lanes : (h + 1) * lanes, :] = rows
    for t, (branch, _, _) in enumerate(terms):
        gd[t] = back(g_refs[t][...], weight[branch])
    for h in range(halves):
        cols = slice(h * lanes, (h + 1) * lanes)
        for q in range(slabs):
            acc = None
            for t, (_, _, reach) in enumerate(terms):
                for i, side in enumerate(SIDES):
                    if not span(slabs, q, -side, reach):
                        continue
                    src = (q - side * reach) * size
                    term = gd[t, src : src + size, cols] * k_ref[0, 3 * t + i : 3 * t + i + 1, cols]
                    acc = term if acc is None else acc + term
            for g in range(wide.shape[0]):
                wide[g, q * grain : (q + 1) * grain, cols] = acc[g * grain : (g + 1) * grain, :]
    rows = out_ref.shape[1]
    for g in range(wide.shape[0]):
        out_ref[g // rows, g % rows] = wide[g].astype(BF16)


def feature_grads(terms, slabs, grain, halves, idx, shape, k, w, gs):
    images, rows, width, channels = shape
    blocks, _, own = k.shape
    cells, co = gs[0].shape
    n = len(terms)
    args = [*w, *gs]
    return pl.pallas_call(
        functools.partial(feature_kernel, terms, slabs, grain, halves),
        grid_spec=pltpu.PrefetchScalarGridSpec(
            num_scalar_prefetch=1,
            grid=(blocks,),
            in_specs=[pl.BlockSpec((1,) + k.shape[1:], lambda d, s: (d, 0, 0))]
            + [WHOLE] * len(args),
            out_specs=pl.BlockSpec((images, rows, width, own), lambda d, s: (0, 0, 0, s[FIRST + d])),
            scratch_shapes=[
                pltpu.VMEM((n, cells, own), F32),
                pltpu.VMEM((2, own, co), BF16),
                pltpu.VMEM((images * rows, width, own), F32),
            ],
        ),
        out_shape=jax.ShapeDtypeStruct(shape, BF16),
        compiler_params=pltpu.CompilerParams(vmem_limit_bytes=18 * MIB),
        cost_estimate=pl.CostEstimate(
            flops=2 * n * cells * channels * co,
            bytes_accessed=4 * cells * channels,
            transcendentals=0,
        ),
        name="feature_grads",
    )(idx, k, *args)


def turn_kernel(slabs, grain, count, has_out, cot_ref, centre_ref, *refs):
    received, refs = refs[:count], refs[count + has_out :]
    g_ref, out_ref, flat, wide = refs
    n, rows = cot_ref.shape[:2]
    size = n * rows * grain
    for g in range(n * rows):
        line = cot_ref[g // rows, g % rows].astype(F32)
        for q in range(slabs):
            at = q * size + g * grain
            flat[at : at + grain, :] = line[q * grain : (q + 1) * grain, :]
    for q in range(slabs):
        here = slice(q * size, (q + 1) * size)
        pre = centre_ref[here, :]
        parts = [ref[here, :] for ref in received]
        halves = [part for part in parts if part.shape[1] < pre.shape[1]]
        parts = [part for part in parts if part.shape[1] == pre.shape[1]]
        if halves:
            parts.append(jnp.concatenate(halves, axis=1))
        for part in parts:
            pre = pre + part.astype(F32)
        sig = jax.nn.sigmoid(pre)
        g_ref[here, :] = (flat[here, :] * sig * (1.0 + pre * (1.0 - sig))).astype(BF16)
        out = pre * sig
        for g in range(n * rows):
            wide[g, q * grain : (q + 1) * grain, :] = out[g * grain : (g + 1) * grain, :]
    for g in range(n * rows):
        out_ref[g // rows, g % rows] = wide[g].astype(BF16)


def turn(slabs, grain, branch, cotangent, centre, received, outputs):
    n, rows, width, _ = cotangent.shape
    cells, co = centre.shape
    natural = pl.BlockSpec((n, rows, width, co), lambda i: (0, 0, 0, branch))
    has_out = outputs is not None
    args = [cotangent, centre, *received] + ([outputs] if has_out else [])
    specs = [natural] + [WHOLE] * (1 + len(received))
    return pl.pallas_call(
        functools.partial(turn_kernel, slabs, grain, len(received), has_out),
        grid=(1,),
        in_specs=specs + [pl.BlockSpec(memory_space=pl.ANY)] * has_out,
        out_specs=[WHOLE, natural],
        out_shape=[
            jax.ShapeDtypeStruct((cells, co), BF16),
            jax.ShapeDtypeStruct(cotangent.shape, BF16),
        ],
        scratch_shapes=[
            pltpu.VMEM((cells, co), F32),
            pltpu.VMEM((n * rows, width, co), F32),
        ],
        input_output_aliases={len(args) - 1: 1} if has_out else {},
        compiler_params=pltpu.CompilerParams(vmem_limit_bytes=8 * MIB),
        cost_estimate=pl.CostEstimate(
            flops=12 * cells * co, bytes_accessed=8 * cells * co, transcendentals=2 * cells * co
        ),
        name="turn",
    )(*args)


def finish_kernel(factor, halves, quarters, idx_ref, *refs):
    ins, (w_ref, k_ref, wide, taps_of) = refs[:halves], refs[halves:]
    co = w_ref.shape[2]
    per, taps = co // quarters, TAP_ROWS // quarters
    lanes = ins[0].shape[3]
    for branch in range(2):
        for q in range(quarters):
            at = q ^ idx_ref[1] if quarters > 1 else 0
            blocks = [ref[at, branch].astype(F32) * factor for ref in ins]
            if halves == 2:
                low = idx_ref[0] == 0
                blocks = [jnp.where(low, *blocks), jnp.where(low, *blocks[::-1])]
            for h, block in enumerate(blocks):
                cols = slice(h * lanes, (h + 1) * lanes)
                wide[q * per : (q + 1) * per, cols] = block[:per]
                taps_of[q * taps : (q + 1) * taps, cols] = block[per:]
        w_ref[branch] = wide[...].T
        for t in range(k_ref.shape[0]):
            k_ref[t, branch : branch + 1, :] = taps_of[t : t + 1, :]


def finish(idx, pieces, own, factor):
    halves = len(pieces)
    quarters, _, rows, _ = pieces[0].shape
    co = rows * quarters - TAP_ROWS
    w, k = pl.pallas_call(
        functools.partial(finish_kernel, factor, halves, quarters),
        in_specs=[pl.BlockSpec(memory_space=pltpu.SMEM)] + [WHOLE] * halves,
        out_specs=[WHOLE] * 2,
        out_shape=[
            jax.ShapeDtypeStruct((2, own, co), F32),
            jax.ShapeDtypeStruct((9, 2, own), F32),
        ],
        scratch_shapes=[pltpu.VMEM((co, own), F32), pltpu.VMEM((TAP_ROWS, own), F32)],
        name="finish_grads",
    )(idx, *pieces)
    return w, k.transpose(1, 0, 2)


def pyramid(features, pointwise, depthwise, cotangent):
    n, rows, width, _ = features.shape
    own, co = pointwise.shape[1:]
    space, dp = lax.axis_size("space"), lax.axis_size("dp")
    me, row = lax.axis_index("space"), lax.axis_index("dp")
    chips = space // 2
    halves = 2 if space % 2 == 0 and own % 256 == 0 and dp % 2 == 0 else 1
    part_c = own // halves
    even = chips & (chips - 1) == 0 and TAP_ROWS % (8 * chips) == 0 and co % (16 * chips) == 0
    quarters = chips if halves == 2 and even else 1
    core, chip = me % 2, me // 2

    grain = math.gcd(*RATES)
    slabs = width // grain

    terms, moves, modes = [], [], []
    flags = [jnp.zeros((), bool)] * (FIRST - FLAGS)
    for branch, rate in enumerate(RATES):
        offset, reach = rate // rows, rate // grain
        group = me // offset
        if 2 * offset == space:
            kinds = [(0, "none"), (DYNAMIC, "swap")]
            flags[0] = group == 1
        elif 4 * offset == space:
            kinds = [(0, "none"), (DYNAMIC + 1, "pair"), (DYNAMIC + 2, "relay")]
            flags[1] = group % 2 == 1
            flags[2] = group % 2 == 0
        else:
            kinds = [(0, "none")] + [(u, "shift") for u in (-1, 1) if offset < space]
        for u, mode in kinds:
            terms.append((branch, u, reach))
            modes.append(mode)
            moves.append(offset)
    middle = [t for t, mode in enumerate(modes) if mode == "none"]
    outer = [t for t, mode in enumerate(modes) if mode != "none"]

    def route(value, t, pairs):
        width_of = moves[t]
        return lax.ppermute(
            value,
            "space",
            [(a * width_of + i, b * width_of + i) for a, b in pairs for i in range(width_of)],
        )

    def send(value, t, direction):
        if modes[t] == "swap":
            return [route(value, t, [(0, 1), (1, 0)])]
        if modes[t] == "pair":
            return [route(value, t, [(0, 1), (1, 0), (2, 3), (3, 2)])]
        if modes[t] == "shift":
            return [shift(value, "space", direction * terms[t][1] * moves[t])]
        cut = value.shape[1] // 2
        one = route(value[:, :cut], t, [(1, 0), (2, 3)])
        two = route(value[:, cut:], t, [(1, 3), (2, 0)])
        one = route(one, t, [(0, 2), (3, 1)])
        two = route(two, t, [(3, 2), (0, 1)])
        return [one, two]

    idx = jnp.concatenate(
        [
            jnp.stack([core, chip, *flags]).astype(jnp.int32),
            (row + dp - jnp.arange(dp)).astype(jnp.int32) % dp,
        ]
    )

    taps = depthwise.transpose(1, 0, 2)
    k_all = [taps] + [cycle(taps, "dp", d) for d in range(1, dp)]
    mine = pointwise
    if halves == 2:
        mine = lax.dynamic_slice_in_dim(pointwise, core * part_c, part_c, axis=1)
    gathered = [None] * 2
    order = (1, 0)
    for b in order:
        gathered[b] = [mine[b]] + [cycle(mine[b], "dp", d) for d in range(1, dp)]

    k_rows = jnp.stack(k_all).astype(F32).transpose(0, 2, 1, 3).reshape(dp, 18, own)
    k_terms = []
    for branch, u, _ in terms:
        at = branch * 9
        if u >= DYNAMIC:
            upper = flags[u - DYNAMIC]
            k_terms.append(jnp.where(upper, k_rows[:, at + 6 : at + 9], k_rows[:, at : at + 3]))
        else:
            k_terms.append(k_rows[:, at + 3 * (u + 1) : at + 3 * (u + 1) + 3])

    taps_all = jnp.concatenate(k_terms, axis=1)
    taps_all = jnp.pad(taps_all, ((0, 0), (0, -taps_all.shape[1] % 8), (0, 0)))

    x, *sums = depthwise_sums(terms, slabs, grain, halves, idx, pltpu.with_memory_space_constraint(features, pltpu.HBM), taps_all)
    held = lax.optimization_barrier
    pick = lambda values, chosen: [values[t] for t in chosen]
    mid = [[t for t in middle if terms[t][0] == b] for b in range(2)]
    out = [[t for t in outer if terms[t][0] == b] for b in range(2)]

    parts, received, outputs, gs = [None] * len(terms), {}, None, [None] * len(terms)
    ws = {h: [None] * 2 for h in range(halves)}
    before = (x, sums)
    for b in order:
        before, gathered[b] = held((before, gathered[b]))
        if b == order[0]:
            x, sums = before
        chosen = out[b]
        count, begun, last_part = len(chosen), None, 0
        ws[0][b] = jnp.concatenate(gathered[b], axis=0)
        if halves == 2:
            ws[1][b] = swap(ws[0][b], "space", 1)
            begun = forward([b] * count, [F32] * count, pick(sums, chosen), {0: ws[0]})
            last_part = 1
        ready = forward(
            [b] * count, [BF16] * count, pick(sums, chosen), {last_part: ws[last_part]}, begun
        )
        for t, part in zip(chosen, ready):
            parts[t] = part
        received[b] = [piece for t in chosen for piece in send(parts[t], t, -1)]
        before = ready
    w = [jnp.concatenate([ws[h][b] for h in range(halves)], axis=0) for b in range(2)]
    chosen = mid[1] + mid[0]
    centre = forward([terms[t][0] for t in chosen], [F32] * 2, pick(sums, chosen), ws)
    for t, part in zip(chosen, centre):
        parts[t] = part

    common = (slabs, halves, quarters, dp, idx, x)
    first = [None] * 2
    for b in order:
        t = mid[b][0]
        if b == order[1]:
            received[b], first[order[0]] = held((received[b], first[order[0]]))
        gs[t], outputs = turn(slabs, grain, b, cotangent, parts[t], received[b], outputs)
        for o in out[b]:
            gs[o] = send(gs[t], o, 1)
        first[b] = weight_grads(
            pick(terms, mid[b]), *common, w[b], pick(gs, mid[b]), pick(sums, mid[b])
        )
    grads = ()
    for b in order:
        grad_g = [jnp.concatenate(gs[t], axis=1) for t in out[b]]
        if b == order[0]:
            grad_g, first[order[1]] = held((grad_g, first[order[1]]))
        else:
            grad_g, grads = held((grad_g, grads))
        for t, field in zip(out[b], grad_g):
            gs[t] = field
        grads = weight_grads(
            pick(terms, out[b]), *common, w[b], grad_g, pick(sums, out[b]), first[b], grads
        )
    kept = grads[0]
    if halves == 2:
        kept = (kept.astype(F32) + swap(grads[1], "space", 1).astype(F32)).astype(BF16)
    pieces = [kept[e] for e in range(quarters)]
    gs, pieces = held((gs, pieces))
    summed = [pieces[0]] + [swap(pieces[e], "space", 2 * e) for e in range(1, quarters)]
    feature_grad = feature_grads(terms, slabs, grain, halves, idx, features.shape, taps_all, w, gs)

    factor = 1.0 / math.sqrt(dp * n * space * rows * width)
    total = sum(piece.astype(F32) for piece in summed).astype(BF16)
    mine = total[0].astype(F32)
    for d in range(1, dp):
        mine = mine + cycle(total[d], "dp", -d).astype(F32)
    if quarters > 1:
        mine = mine.astype(BF16)
        block = jnp.stack([mine] + [swap(mine, "space", 2 * e) for e in range(1, quarters)])
    else:
        peers = [[i for i in range(space) if i % halves == c] for c in range(halves)]
        block = lax.psum(mine, "space", axis_index_groups=peers)[None]
    block = [block, swap(block, "space", 1)] if halves == 2 else [block]
    pointwise_grad, depthwise_grad = finish(idx, block, own, factor)
    return outputs, feature_grad, pointwise_grad, depthwise_grad


def solution(mesh):
    return jax.shard_map(
        pyramid,
        mesh=mesh,
        in_specs=(
            P("dp", "space", None, None),
            P(None, "dp", None),
            P(None, None, "dp"),
            P("dp", "space", None, None),
        ),
        out_specs=(
            P("dp", "space", None, None),
            P("dp", "space", None, None),
            P(None, "dp", None),
            P(None, None, "dp"),
        ),
        check_vma=False,
    )
```

```python
import functools
import math

import jax
import jax.numpy as jnp
from jax import lax
from jax.experimental import pallas as pl
from jax.experimental.pallas import tpu as pltpu
from jax.sharding import PartitionSpec as P


RATES = (12, 24)
SIDES = (-1, 0, 1)
F32 = jnp.float32
BF16 = jnp.bfloat16
TAP_ROWS = 32
MIB = 1 << 20
FLAGS, FIRST = 2, 5
DYNAMIC = 10


def shift(value, axis, steps):
    count = lax.axis_size(axis)
    first, last = max(0, -steps), min(count, count - steps)
    return lax.ppermute(value, axis, [(i, i + steps) for i in range(first, last)])


def cycle(value, axis, steps):
    count = lax.axis_size(axis)
    return lax.ppermute(value, axis, [(i, (i + steps) % count) for i in range(count)])


def swap(value, axis, mask):
    count = lax.axis_size(axis)
    return lax.ppermute(value, axis, [(i, i ^ mask) for i in range(count)])


def span(slabs, q, side, reach):
    return 0 <= q + side * reach < slabs


WHOLE = pl.BlockSpec(memory_space=pltpu.VMEM)


def lanes_at(start, count):
    return pl.ds(start if isinstance(start, int) else pl.multiple_of(start, count), count)


def sums_kernel(terms, slabs, grain, halves, idx_ref, x_ref, k_ref, xs_ref, *refs):
    outs, wide = refs[: len(terms)], refs[len(terms)]
    n, rows = x_ref.shape[:2]
    size = n * rows * grain
    step, blocks = pl.program_id(0), pl.num_programs(0)
    lanes = x_ref.shape[3] // halves
    for g in range(n * rows):
        line = x_ref[g // rows, g % rows].astype(F32)
        for q in range(slabs):
            at = q * size + g * grain
            wide[at : at + grain, :] = line[q * grain : (q + 1) * grain, :]
    for h in range(halves):
        src = lanes_at((h ^ idx_ref[0]) * lanes if halves > 1 else 0, lanes)
        dst = lanes_at((h * blocks + step) * lanes, lanes)
        for q in range(slabs):
            here = slice(q * size, (q + 1) * size)
            xs_ref[here, dst] = wide[here, src].astype(BF16)
        for t, (_, _, reach) in enumerate(terms):
            taps = [k_ref[0, 3 * t + i : 3 * t + i + 1, src] for i in range(3)]
            for q in range(slabs):
                total = None
                for i, side in enumerate(SIDES):
                    if span(slabs, q, side, reach):
                        at = (q + side * reach) * size
                        term = wide[at : at + size, src] * taps[i]
                        total = term if total is None else total + term
                outs[t][q * size : (q + 1) * size, dst] = total.astype(BF16)


def depthwise_sums(terms, slabs, grain, halves, idx, x, k):
    n, rows, width, channels = x.shape
    cells, (blocks, _, own) = n * rows * width, k.shape
    return pl.pallas_call(
        functools.partial(sums_kernel, terms, slabs, grain, halves),
        grid_spec=pltpu.PrefetchScalarGridSpec(
            num_scalar_prefetch=1,
            grid=(blocks,),
            in_specs=[
                pl.BlockSpec((n, rows, width, own), lambda d, s: (0, 0, 0, s[FIRST + d])),
                pl.BlockSpec((1, k.shape[1], own), lambda d, s: (d, 0, 0)),
            ],
            out_specs=[WHOLE] * (1 + len(terms)),
            scratch_shapes=[pltpu.VMEM((cells, own), F32)],
        ),
        out_shape=[jax.ShapeDtypeStruct((cells, channels), BF16)] * (1 + len(terms)),
        compiler_params=pltpu.CompilerParams(vmem_limit_bytes=8 * MIB),
        cost_estimate=pl.CostEstimate(
            flops=6 * len(terms) * cells * channels,
            bytes_accessed=2 * (2 + len(terms)) * cells * channels,
            transcendentals=0,
        ),
        name="depthwise_sums",
    )(idx, x, k)


def forward_kernel(branches, parts, add, *refs):
    n = len(branches)
    count = len(parts) * len(set(branches))
    all_refs, refs = refs[:count], refs[count:]
    for t, branch in enumerate(branches):
        total = refs[n + t][...] if add else None
        at = sorted(set(branches)).index(branch) * len(parts)
        for w_ref, h in zip(all_refs[at : at + len(parts)], parts):
            depth = w_ref.shape[0]
            field = refs[t][:, h * depth : (h + 1) * depth]
            part = jnp.dot(field, w_ref[...], preferred_element_type=F32)
            total = part if total is None else total + part
        out = refs[len(refs) - n + t]
        out[...] = total.astype(out.dtype)


def forward(branches, dtypes, sums, ws, before=None):
    cells = sums[0].shape[0]
    used = [ws[h][b] for b in sorted(set(branches)) for h in ws]
    depth, co = used[0].shape
    args = [*used, *sums, *(before or [])]
    return pl.pallas_call(
        functools.partial(forward_kernel, branches, tuple(ws), before is not None),
        in_specs=[WHOLE] * len(args),
        out_specs=[WHOLE] * len(sums),
        out_shape=[jax.ShapeDtypeStruct((cells, co), dt) for dt in dtypes],
        compiler_params=pltpu.CompilerParams(vmem_limit_bytes=8 * MIB),
        cost_estimate=pl.CostEstimate(
            flops=2 * len(sums) * cells * depth * len(ws) * co,
            bytes_accessed=2 * len(sums) * cells * depth * len(ws),
            transcendentals=0,
        ),
        name="forward_terms",
    )(*args)


def back(g, weight):
    return lax.dot_general(g, weight, (((1,), (1,)), ((), ())), preferred_element_type=F32)


def weight_kernel(terms, slabs, halves, quarters, last, idx_ref, x_ref, w_ref, *refs):
    n = len(terms)
    g_refs, d_refs, refs = refs[:n], refs[n : 2 * n], refs[2 * n :]
    if last:
        w_before, k_before, *outs, gt, gd, kacc, pieces = refs
        outs = outs[-halves:]
    else:
        w_out, k_out, gt, gd, kacc = refs
    step, blocks = pl.program_id(0), pl.num_programs(0)
    own, co = kacc.shape[1], w_ref.shape[1]
    size = g_refs[0].shape[0] // slabs
    lanes = own // halves
    block = lanes_at(step * own, own)

    @pl.when(step == 0)
    def _():
        for t in range(n):
            gt[t] = g_refs[t][...].T

    for t in range(n):
        gd[t] = back(g_refs[t][...], w_ref[block, :])
    total = w_before[step] if last else None
    for t in range(n):
        part = jnp.dot(gt[t], d_refs[t][:, block], preferred_element_type=F32)
        total = part if total is None else total + part
    per = co // quarters
    if last:
        for h in range(halves):
            for q in range(quarters):
                rows = total[q * per : (q + 1) * per, h * lanes : (h + 1) * lanes]
                pieces[h, q, :per, :] = rows.astype(BF16)
    else:
        w_out[step] = total
    kacc[...] = k_before[step] if last else jnp.zeros_like(kacc)
    for h in range(halves):
        cols = slice(h * lanes, (h + 1) * lanes)
        there = lanes_at(step * own + h * lanes, lanes)
        sums = [None] * (3 * n)
        for q in range(slabs):
            xq = x_ref[q * size : (q + 1) * size, there].astype(F32)
            for t, (_, _, reach) in enumerate(terms):
                for i, side in enumerate(SIDES):
                    if not span(slabs, q, -side, reach):
                        continue
                    src = (q - side * reach) * size
                    part = xq * gd[t, src : src + size, cols]
                    part = jnp.sum(part.reshape(size // 8, 8, lanes), axis=0)
                    at = 3 * t + i
                    sums[at] = part if sums[at] is None else sums[at] + part
        for t, (_, u, _) in enumerate(terms):
            for i in range(3):
                total = jnp.sum(sums[3 * t + i], axis=0, keepdims=True)
                if u >= DYNAMIC:
                    upper = idx_ref[FLAGS + u - DYNAMIC] > 0
                    kacc[i : i + 1, cols] += jnp.where(upper, 0.0, total)
                    kacc[i + 6 : i + 7, cols] += jnp.where(upper, total, 0.0)
                else:
                    row = 3 * (u + 1) + i
                    kacc[row : row + 1, cols] += total
    if not last:
        k_out[step] = kacc[...]
        return
    taps = TAP_ROWS // quarters
    for h in range(halves):
        for q in range(quarters):
            rows = kacc[q * taps : (q + 1) * taps, h * lanes : (h + 1) * lanes]
            pieces[h, q, per:, :] = rows.astype(BF16)

    def put(out, which):
        for e in range(quarters):
            at = e ^ idx_ref[1] if quarters > 1 else 0
            for h in range(halves):
                out[e, (step - which * (blocks // halves)) * halves + h, terms[0][0]] = pieces[h, at]

    for which in range(halves):
        mine = step // (blocks // halves) == which
        pl.when(mine)(functools.partial(put, outs[which], which))


def weight_grads(terms, slabs, halves, quarters, blocks, idx, x, w, gs, ds, before=None, into=()):
    cells, channels = x.shape
    own, co = channels // blocks, w.shape[1]
    n = len(terms)
    last = before is not None
    args = [x, w, *gs, *ds, *(before or ()), *into]
    scratch = [
        pltpu.VMEM((n, co, cells), BF16),
        pltpu.VMEM((n, cells, own), F32),
        pltpu.VMEM((TAP_ROWS, own), F32),
    ]
    if last:
        piece = ((co + TAP_ROWS) // quarters, own // halves)
        out_shape = [jax.ShapeDtypeStruct((quarters, blocks, 2) + piece, BF16)] * halves
        scratch.append(pltpu.VMEM((halves, quarters) + piece, BF16))
    else:
        out_shape = [
            jax.ShapeDtypeStruct((blocks, co, own), F32),
            jax.ShapeDtypeStruct((blocks, TAP_ROWS, own), F32),
        ]
    return pl.pallas_call(
        functools.partial(weight_kernel, terms, slabs, halves, quarters, last),
        grid_spec=pltpu.PrefetchScalarGridSpec(
            num_scalar_prefetch=1,
            grid=(blocks,),
            in_specs=[WHOLE] * len(args),
            out_specs=[WHOLE] * len(out_shape),
            scratch_shapes=scratch,
        ),
        out_shape=out_shape,
        input_output_aliases={1 + len(args) - len(into) + i: i for i in range(len(into))},
        compiler_params=pltpu.CompilerParams(vmem_limit_bytes=10 * MIB),
        cost_estimate=pl.CostEstimate(
            flops=4 * n * cells * channels * co,
            bytes_accessed=2 * (n + 1) * cells * channels,
            transcendentals=0,
        ),
        name="weight_outer" if last else "weight_middle",
    )(idx, *args)


def feature_kernel(terms, slabs, grain, halves, idx_ref, k_ref, *refs):
    n = len(terms)
    w_refs, g_refs, (out_ref, gd, weight, wide) = refs[:2], refs[2 : 2 + n], refs[2 + n :]
    size = g_refs[0].shape[0] // slabs
    step, blocks = pl.program_id(0), pl.num_programs(0)
    own = weight.shape[1]
    lanes = own // halves
    for h in range(halves):
        at = ((h ^ idx_ref[0] if halves > 1 else 0) * blocks + step) * lanes
        for branch in range(2):
            rows = w_refs[branch][lanes_at(at, lanes), :]
            weight[branch, h * lanes : (h + 1) * lanes, :] = rows
    for t, (branch, _, _) in enumerate(terms):
        gd[t] = back(g_refs[t][...], weight[branch])
    for h in range(halves):
        cols = slice(h * lanes, (h + 1) * lanes)
        for q in range(slabs):
            acc = None
            for t, (_, _, reach) in enumerate(terms):
                for i, side in enumerate(SIDES):
                    if not span(slabs, q, -side, reach):
                        continue
                    src = (q - side * reach) * size
                    term = gd[t, src : src + size, cols] * k_ref[0, 3 * t + i : 3 * t + i + 1, cols]
                    acc = term if acc is None else acc + term
            for g in range(wide.shape[0]):
                wide[g, q * grain : (q + 1) * grain, cols] = acc[g * grain : (g + 1) * grain, :]
    rows = out_ref.shape[1]
    for g in range(wide.shape[0]):
        out_ref[g // rows, g % rows] = wide[g].astype(BF16)


def feature_grads(terms, slabs, grain, halves, idx, shape, k, w, gs):
    images, rows, width, channels = shape
    blocks, _, own = k.shape
    cells, co = gs[0].shape
    n = len(terms)
    args = [*w, *gs]
    return pl.pallas_call(
        functools.partial(feature_kernel, terms, slabs, grain, halves),
        grid_spec=pltpu.PrefetchScalarGridSpec(
            num_scalar_prefetch=1,
            grid=(blocks,),
            in_specs=[pl.BlockSpec((1,) + k.shape[1:], lambda d, s: (d, 0, 0))]
            + [WHOLE] * len(args),
            out_specs=pl.BlockSpec((images, rows, width, own), lambda d, s: (0, 0, 0, s[FIRST + d])),
            scratch_shapes=[
                pltpu.VMEM((n, cells, own), F32),
                pltpu.VMEM((2, own, co), BF16),
                pltpu.VMEM((images * rows, width, own), F32),
            ],
        ),
        out_shape=jax.ShapeDtypeStruct(shape, BF16),
        compiler_params=pltpu.CompilerParams(vmem_limit_bytes=18 * MIB),
        cost_estimate=pl.CostEstimate(
            flops=2 * n * cells * channels * co,
            bytes_accessed=4 * cells * channels,
            transcendentals=0,
        ),
        name="feature_grads",
    )(idx, k, *args)


def turn_kernel(slabs, grain, count, has_out, cot_ref, centre_ref, *refs):
    received, refs = refs[:count], refs[count + has_out :]
    g_ref, out_ref, flat, wide = refs
    n, rows = cot_ref.shape[:2]
    size = n * rows * grain
    for g in range(n * rows):
        line = cot_ref[g // rows, g % rows].astype(F32)
        for q in range(slabs):
            at = q * size + g * grain
            flat[at : at + grain, :] = line[q * grain : (q + 1) * grain, :]
    for q in range(slabs):
        here = slice(q * size, (q + 1) * size)
        pre = centre_ref[here, :]
        parts = [ref[here, :] for ref in received]
        halves = [part for part in parts if part.shape[1] < pre.shape[1]]
        parts = [part for part in parts if part.shape[1] == pre.shape[1]]
        if halves:
            parts.append(jnp.concatenate(halves, axis=1))
        for part in parts:
            pre = pre + part.astype(F32)
        sig = jax.nn.sigmoid(pre)
        g_ref[here, :] = (flat[here, :] * sig * (1.0 + pre * (1.0 - sig))).astype(BF16)
        out = pre * sig
        for g in range(n * rows):
            wide[g, q * grain : (q + 1) * grain, :] = out[g * grain : (g + 1) * grain, :]
    for g in range(n * rows):
        out_ref[g // rows, g % rows] = wide[g].astype(BF16)


def turn(slabs, grain, branch, cotangent, centre, received, outputs):
    n, rows, width, _ = cotangent.shape
    cells, co = centre.shape
    natural = pl.BlockSpec((n, rows, width, co), lambda i: (0, 0, 0, branch))
    has_out = outputs is not None
    args = [cotangent, centre, *received] + ([outputs] if has_out else [])
    specs = [natural] + [WHOLE] * (1 + len(received))
    return pl.pallas_call(
        functools.partial(turn_kernel, slabs, grain, len(received), has_out),
        grid=(1,),
        in_specs=specs + [pl.BlockSpec(memory_space=pl.ANY)] * has_out,
        out_specs=[WHOLE, natural],
        out_shape=[
            jax.ShapeDtypeStruct((cells, co), BF16),
            jax.ShapeDtypeStruct(cotangent.shape, BF16),
        ],
        scratch_shapes=[
            pltpu.VMEM((cells, co), F32),
            pltpu.VMEM((n * rows, width, co), F32),
        ],
        input_output_aliases={len(args) - 1: 1} if has_out else {},
        compiler_params=pltpu.CompilerParams(vmem_limit_bytes=8 * MIB),
        cost_estimate=pl.CostEstimate(
            flops=12 * cells * co, bytes_accessed=8 * cells * co, transcendentals=2 * cells * co
        ),
        name="turn",
    )(*args)


def finish_kernel(factor, quarters, idx_ref, in_ref, *refs):
    w_ref, k_ref, wide, taps_of = refs[-4:]
    co = w_ref.shape[2]
    per, taps = co // quarters, TAP_ROWS // quarters
    for branch in range(2):
        for q in range(quarters):
            at = q ^ idx_ref[1] if quarters > 1 else 0
            block = in_ref[at, branch].astype(F32) * factor
            wide[q * per : (q + 1) * per, :] = block[:per]
            taps_of[q * taps : (q + 1) * taps, :] = block[per:]
        w_ref[branch] = wide[...].T
        for t in range(k_ref.shape[0]):
            k_ref[t, branch : branch + 1, :] = taps_of[t : t + 1, :]


def finish(idx, block, half, halves, own, factor, into=()):
    quarters, _, rows, lanes = block.shape
    co = rows * quarters - TAP_ROWS

    def place(s):
        return s[0] ^ half if halves > 1 else 0

    return pl.pallas_call(
        functools.partial(finish_kernel, factor, quarters),
        grid_spec=pltpu.PrefetchScalarGridSpec(
            num_scalar_prefetch=1,
            grid=(1,),
            in_specs=[pl.BlockSpec(block.shape, lambda i, s: (0, 0, 0, 0))]
            + [pl.BlockSpec(memory_space=pl.ANY)] * len(into),
            out_specs=[
                pl.BlockSpec((2, lanes, co), lambda i, s: (0, place(s), 0)),
                pl.BlockSpec((9, 2, lanes), lambda i, s: (0, 0, place(s))),
            ],
            scratch_shapes=[pltpu.VMEM((co, lanes), F32), pltpu.VMEM((TAP_ROWS, lanes), F32)],
        ),
        out_shape=[
            jax.ShapeDtypeStruct((2, own, co), F32),
            jax.ShapeDtypeStruct((9, 2, own), F32),
        ],
        input_output_aliases={2 + i: i for i in range(len(into))},
        compiler_params=pltpu.CompilerParams(vmem_limit_bytes=8 * MIB),
        name="finish_grads",
    )(idx, block, *into)


def pyramid(features, pointwise, depthwise, cotangent):
    n, rows, width, _ = features.shape
    own, co = pointwise.shape[1:]
    space, dp = lax.axis_size("space"), lax.axis_size("dp")
    me, row = lax.axis_index("space"), lax.axis_index("dp")
    chips = space // 2
    halves = 2 if space % 2 == 0 and own % 256 == 0 and dp % 2 == 0 else 1
    part_c = own // halves
    even = chips & (chips - 1) == 0 and TAP_ROWS % (8 * chips) == 0 and co % (16 * chips) == 0
    quarters = chips if halves == 2 and even else 1
    core, chip = me % 2, me // 2

    grain = math.gcd(*RATES)
    slabs = width // grain

    terms, moves, modes = [], [], []
    flags = [jnp.zeros((), bool)] * (FIRST - FLAGS)
    for branch, rate in enumerate(RATES):
        offset, reach = rate // rows, rate // grain
        group = me // offset
        if 2 * offset == space:
            kinds = [(0, "none"), (DYNAMIC, "swap")]
            flags[0] = group == 1
        elif 4 * offset == space:
            kinds = [(0, "none"), (DYNAMIC + 1, "pair"), (DYNAMIC + 2, "relay")]
            flags[1] = group % 2 == 1
            flags[2] = group % 2 == 0
        else:
            kinds = [(0, "none")] + [(u, "shift") for u in (-1, 1) if offset < space]
        for u, mode in kinds:
            terms.append((branch, u, reach))
            modes.append(mode)
            moves.append(offset)
    middle = [t for t, mode in enumerate(modes) if mode == "none"]
    outer = [t for t, mode in enumerate(modes) if mode != "none"]

    def route(value, t, pairs):
        width_of = moves[t]
        return lax.ppermute(
            value,
            "space",
            [(a * width_of + i, b * width_of + i) for a, b in pairs for i in range(width_of)],
        )

    def send(value, t, direction):
        if modes[t] == "swap":
            return [route(value, t, [(0, 1), (1, 0)])]
        if modes[t] == "pair":
            return [route(value, t, [(0, 1), (1, 0), (2, 3), (3, 2)])]
        if modes[t] == "shift":
            return [shift(value, "space", direction * terms[t][1] * moves[t])]
        cut = value.shape[1] // 2
        one = route(value[:, :cut], t, [(1, 0), (2, 3)])
        two = route(value[:, cut:], t, [(1, 3), (2, 0)])
        one = route(one, t, [(0, 2), (3, 1)])
        two = route(two, t, [(3, 2), (0, 1)])
        return [one, two]

    idx = jnp.concatenate(
        [
            jnp.stack([core, chip, *flags]).astype(jnp.int32),
            (row + dp - jnp.arange(dp)).astype(jnp.int32) % dp,
        ]
    )

    taps = depthwise.transpose(1, 0, 2)
    k_all = [taps] + [cycle(taps, "dp", d) for d in range(1, dp)]
    mine = pointwise
    if halves == 2:
        mine = lax.dynamic_slice_in_dim(pointwise, core * part_c, part_c, axis=1)
    gathered = [None] * 2
    order = (1, 0)
    for b in order:
        gathered[b] = [mine[b]] + [cycle(mine[b], "dp", d) for d in range(1, dp)]

    k_rows = jnp.stack(k_all).astype(F32).transpose(0, 2, 1, 3).reshape(dp, 18, own)
    k_terms = []
    for branch, u, _ in terms:
        at = branch * 9
        if u >= DYNAMIC:
            upper = flags[u - DYNAMIC]
            k_terms.append(jnp.where(upper, k_rows[:, at + 6 : at + 9], k_rows[:, at : at + 3]))
        else:
            k_terms.append(k_rows[:, at + 3 * (u + 1) : at + 3 * (u + 1) + 3])

    taps_all = jnp.concatenate(k_terms, axis=1)
    taps_all = jnp.pad(taps_all, ((0, 0), (0, -taps_all.shape[1] % 8), (0, 0)))

    x, *sums = depthwise_sums(terms, slabs, grain, halves, idx, pltpu.with_memory_space_constraint(features, pltpu.HBM), taps_all)
    held = lax.optimization_barrier
    pick = lambda values, chosen: [values[t] for t in chosen]
    mid = [[t for t in middle if terms[t][0] == b] for b in range(2)]
    out = [[t for t in outer if terms[t][0] == b] for b in range(2)]

    parts, received, outputs, gs = [None] * len(terms), {}, None, [None] * len(terms)
    ws = {h: [None] * 2 for h in range(halves)}
    before = (x, sums)
    for b in order:
        before, gathered[b] = held((before, gathered[b]))
        if b == order[0]:
            x, sums = before
        chosen = out[b]
        count, begun, last_part = len(chosen), None, 0
        ws[0][b] = jnp.concatenate(gathered[b], axis=0)
        if halves == 2:
            ws[1][b] = swap(ws[0][b], "space", 1)
            begun = forward([b] * count, [F32] * count, pick(sums, chosen), {0: ws[0]})
            last_part = 1
        ready = forward(
            [b] * count, [BF16] * count, pick(sums, chosen), {last_part: ws[last_part]}, begun
        )
        for t, part in zip(chosen, ready):
            parts[t] = part
        received[b] = [piece for t in chosen for piece in send(parts[t], t, -1)]
        before = ready
    w = [jnp.concatenate([ws[h][b] for h in range(halves)], axis=0) for b in range(2)]
    chosen = mid[1] + mid[0]
    centre = forward([terms[t][0] for t in chosen], [F32] * 2, pick(sums, chosen), ws)
    for t, part in zip(chosen, centre):
        parts[t] = part

    common = (slabs, halves, quarters, dp, idx, x)
    first = [None] * 2
    for b in order:
        t = mid[b][0]
        if b == order[1]:
            received[b], first[order[0]] = held((received[b], first[order[0]]))
        gs[t], outputs = turn(slabs, grain, b, cotangent, parts[t], received[b], outputs)
        for o in out[b]:
            gs[o] = send(gs[t], o, 1)
        first[b] = weight_grads(
            pick(terms, mid[b]), *common, w[b], pick(gs, mid[b]), pick(sums, mid[b])
        )
    grads = ()
    for b in order:
        grad_g = [jnp.concatenate(gs[t], axis=1) for t in out[b]]
        if b == order[0]:
            grad_g, first[order[1]] = held((grad_g, first[order[1]]))
        else:
            grad_g, grads = held((grad_g, grads))
        for t, field in zip(out[b], grad_g):
            gs[t] = field
        grads = weight_grads(
            pick(terms, out[b]), *common, w[b], grad_g, pick(sums, out[b]), first[b], grads
        )
    kept = grads[0]
    if halves == 2:
        kept = (kept.astype(F32) + swap(grads[1], "space", 1).astype(F32)).astype(BF16)
    pieces = [kept[e] for e in range(quarters)]
    gs, pieces = held((gs, pieces))
    summed = [pieces[0]] + [swap(pieces[e], "space", 2 * e) for e in range(1, quarters)]
    feature_grad = feature_grads(terms, slabs, grain, halves, idx, features.shape, taps_all, w, gs)

    factor = 1.0 / math.sqrt(dp * n * space * rows * width)
    total = sum(piece.astype(F32) for piece in summed).astype(BF16)
    mine = total[0].astype(F32)
    for d in range(1, dp):
        mine = mine + cycle(total[d], "dp", -d).astype(F32)
    if quarters > 1:
        mine = mine.astype(BF16)
        block = jnp.stack([mine] + [swap(mine, "space", 2 * e) for e in range(1, quarters)])
    else:
        peers = [[i for i in range(space) if i % halves == c] for c in range(halves)]
        block = lax.psum(mine, "space", axis_index_groups=peers)[None]
    if halves == 2:
        other = swap(block, "space", 1)
    done = finish(idx, block, 0, halves, own, factor)
    if halves == 2:
        done = finish(idx, other, 1, halves, own, factor, done)
    pointwise_grad, depthwise_grad = done[0], done[1].transpose(1, 0, 2)
    return outputs, feature_grad, pointwise_grad, depthwise_grad


def solution(mesh):
    return jax.shard_map(
        pyramid,
        mesh=mesh,
        in_specs=(
            P("dp", "space", None, None),
            P(None, "dp", None),
            P(None, None, "dp"),
            P("dp", "space", None, None),
        ),
        out_specs=(
            P("dp", "space", None, None),
            P("dp", "space", None, None),
            P(None, "dp", None),
            P(None, None, "dp"),
        ),
        check_vma=False,
    )
```

```python
import functools
import math

import jax
import jax.numpy as jnp
from jax import lax
from jax.experimental import pallas as pl
from jax.experimental.pallas import tpu as pltpu
from jax.sharding import PartitionSpec as P


RATES = (12, 24)
SIDES = (-1, 0, 1)
F32 = jnp.float32
BF16 = jnp.bfloat16
TAP_ROWS = 32
MIB = 1 << 20
FLAGS, FIRST = 2, 5
DYNAMIC = 10


def shift(value, axis, steps):
    count = lax.axis_size(axis)
    first, last = max(0, -steps), min(count, count - steps)
    return lax.ppermute(value, axis, [(i, i + steps) for i in range(first, last)])


def cycle(value, axis, steps):
    count = lax.axis_size(axis)
    return lax.ppermute(value, axis, [(i, (i + steps) % count) for i in range(count)])


def swap(value, axis, mask):
    count = lax.axis_size(axis)
    return lax.ppermute(value, axis, [(i, i ^ mask) for i in range(count)])


def span(slabs, q, side, reach):
    return 0 <= q + side * reach < slabs


WHOLE = pl.BlockSpec(memory_space=pltpu.VMEM)


def lanes_at(start, count):
    return pl.ds(start if isinstance(start, int) else pl.multiple_of(start, count), count)


def sums_kernel(terms, slabs, grain, halves, idx_ref, x_ref, k_ref, xs_ref, *refs):
    outs, wide = refs[: len(terms)], refs[len(terms)]
    n, rows = x_ref.shape[:2]
    size = n * rows * grain
    step, blocks = pl.program_id(0), pl.num_programs(0)
    lanes = x_ref.shape[3] // halves
    for g in range(n * rows):
        line = x_ref[g // rows, g % rows].astype(F32)
        for q in range(slabs):
            at = q * size + g * grain
            wide[at : at + grain, :] = line[q * grain : (q + 1) * grain, :]
    tile = 16 if size % 16 == 0 else 8
    for h in range(halves):
        start = (h ^ idx_ref[0]) * lanes if halves > 1 else 0
        for strip in range(lanes // 128):
            src = lanes_at(start + strip * 128, 128)
            dst = lanes_at((h * blocks + step) * lanes + strip * 128, 128)
            taps = [k_ref[0, r : r + 1, src] for r in range(3 * len(terms))]
            for q in range(slabs):
                for row in range(0, size, tile):
                    here = slice(q * size + row, q * size + row + tile)
                    near = {}
                    for t, (_, _, reach) in enumerate(terms):
                        total = None
                        for i, side in enumerate(SIDES):
                            if not span(slabs, q, side, reach):
                                continue
                            far = side * reach
                            if far not in near:
                                at = (q + far) * size + row
                                near[far] = wide[at : at + tile, src]
                            term = near[far] * taps[3 * t + i]
                            total = term if total is None else total + term
                        outs[t][here, dst] = total.astype(BF16)
                    xs_ref[here, dst] = near[0].astype(BF16)


def depthwise_sums(terms, slabs, grain, halves, idx, x, k):
    n, rows, width, channels = x.shape
    cells, (blocks, _, own) = n * rows * width, k.shape
    return pl.pallas_call(
        functools.partial(sums_kernel, terms, slabs, grain, halves),
        grid_spec=pltpu.PrefetchScalarGridSpec(
            num_scalar_prefetch=1,
            grid=(blocks,),
            in_specs=[
                pl.BlockSpec((n, rows, width, own), lambda d, s: (0, 0, 0, s[FIRST + d])),
                pl.BlockSpec((1, k.shape[1], own), lambda d, s: (d, 0, 0)),
            ],
            out_specs=[WHOLE] * (1 + len(terms)),
            scratch_shapes=[pltpu.VMEM((cells, own), F32)],
        ),
        out_shape=[jax.ShapeDtypeStruct((cells, channels), BF16)] * (1 + len(terms)),
        compiler_params=pltpu.CompilerParams(vmem_limit_bytes=8 * MIB),
        cost_estimate=pl.CostEstimate(
            flops=6 * len(terms) * cells * channels,
            bytes_accessed=2 * (2 + len(terms)) * cells * channels,
            transcendentals=0,
        ),
        name="depthwise_sums",
    )(idx, x, k)


def forward_kernel(branches, parts, add, *refs):
    n = len(branches)
    count = len(parts) * len(set(branches))
    all_refs, refs = refs[:count], refs[count:]
    for t, branch in enumerate(branches):
        total = refs[n + t][...] if add else None
        at = sorted(set(branches)).index(branch) * len(parts)
        for w_ref, h in zip(all_refs[at : at + len(parts)], parts):
            depth = w_ref.shape[0]
            field = refs[t][:, h * depth : (h + 1) * depth]
            part = jnp.dot(field, w_ref[...], preferred_element_type=F32)
            total = part if total is None else total + part
        out = refs[len(refs) - n + t]
        out[...] = total.astype(out.dtype)


def forward(branches, dtypes, sums, ws, before=None):
    cells = sums[0].shape[0]
    used = [ws[h][b] for b in sorted(set(branches)) for h in ws]
    depth, co = used[0].shape
    args = [*used, *sums, *(before or [])]
    return pl.pallas_call(
        functools.partial(forward_kernel, branches, tuple(ws), before is not None),
        in_specs=[WHOLE] * len(args),
        out_specs=[WHOLE] * len(sums),
        out_shape=[jax.ShapeDtypeStruct((cells, co), dt) for dt in dtypes],
        compiler_params=pltpu.CompilerParams(vmem_limit_bytes=8 * MIB),
        cost_estimate=pl.CostEstimate(
            flops=2 * len(sums) * cells * depth * len(ws) * co,
            bytes_accessed=2 * len(sums) * cells * depth * len(ws),
            transcendentals=0,
        ),
        name="forward_terms",
    )(*args)


def back(g, weight):
    return lax.dot_general(g, weight, (((1,), (1,)), ((), ())), preferred_element_type=F32)


def weight_kernel(terms, slabs, halves, quarters, last, idx_ref, x_ref, w_ref, *refs):
    n = len(terms)
    g_refs, d_refs, refs = refs[:n], refs[n : 2 * n], refs[2 * n :]
    if last:
        w_before, k_before, *outs, gt, gd, kacc, pieces = refs
        outs = outs[-halves:]
    else:
        w_out, k_out, gt, gd, kacc = refs
    step, blocks = pl.program_id(0), pl.num_programs(0)
    own, co = kacc.shape[1], w_ref.shape[1]
    size = g_refs[0].shape[0] // slabs
    lanes = own // halves
    block = lanes_at(step * own, own)

    @pl.when(step == 0)
    def _():
        for t in range(n):
            gt[t] = g_refs[t][...].T

    for t in range(n):
        gd[t] = back(g_refs[t][...], w_ref[block, :])
    total = w_before[step] if last else None
    for t in range(n):
        part = jnp.dot(gt[t], d_refs[t][:, block], preferred_element_type=F32)
        total = part if total is None else total + part
    per = co // quarters
    if last:
        for h in range(halves):
            for q in range(quarters):
                rows = total[q * per : (q + 1) * per, h * lanes : (h + 1) * lanes]
                pieces[h, q, :per, :] = rows.astype(BF16)
    else:
        w_out[step] = total
    kacc[...] = k_before[step] if last else jnp.zeros_like(kacc)
    for h in range(halves):
        cols = slice(h * lanes, (h + 1) * lanes)
        there = lanes_at(step * own + h * lanes, lanes)
        sums = [None] * (3 * n)
        for q in range(slabs):
            xq = x_ref[q * size : (q + 1) * size, there].astype(F32)
            for t, (_, _, reach) in enumerate(terms):
                for i, side in enumerate(SIDES):
                    if not span(slabs, q, -side, reach):
                        continue
                    src = (q - side * reach) * size
                    part = xq * gd[t, src : src + size, cols]
                    part = jnp.sum(part.reshape(size // 8, 8, lanes), axis=0)
                    at = 3 * t + i
                    sums[at] = part if sums[at] is None else sums[at] + part
        for t, (_, u, _) in enumerate(terms):
            for i in range(3):
                total = jnp.sum(sums[3 * t + i], axis=0, keepdims=True)
                if u >= DYNAMIC:
                    upper = idx_ref[FLAGS + u - DYNAMIC] > 0
                    kacc[i : i + 1, cols] += jnp.where(upper, 0.0, total)
                    kacc[i + 6 : i + 7, cols] += jnp.where(upper, total, 0.0)
                else:
                    row = 3 * (u + 1) + i
                    kacc[row : row + 1, cols] += total
    if not last:
        k_out[step] = kacc[...]
        return
    taps = TAP_ROWS // quarters
    for h in range(halves):
        for q in range(quarters):
            rows = kacc[q * taps : (q + 1) * taps, h * lanes : (h + 1) * lanes]
            pieces[h, q, per:, :] = rows.astype(BF16)

    def put(out, which):
        for e in range(quarters):
            at = e ^ idx_ref[1] if quarters > 1 else 0
            for h in range(halves):
                out[e, (step - which * (blocks // halves)) * halves + h, terms[0][0]] = pieces[h, at]

    for which in range(halves):
        mine = step // (blocks // halves) == which
        pl.when(mine)(functools.partial(put, outs[which], which))


def weight_grads(terms, slabs, halves, quarters, blocks, idx, x, w, gs, ds, before=None, into=()):
    cells, channels = x.shape
    own, co = channels // blocks, w.shape[1]
    n = len(terms)
    last = before is not None
    args = [x, w, *gs, *ds, *(before or ()), *into]
    scratch = [
        pltpu.VMEM((n, co, cells), BF16),
        pltpu.VMEM((n, cells, own), F32),
        pltpu.VMEM((TAP_ROWS, own), F32),
    ]
    if last:
        piece = ((co + TAP_ROWS) // quarters, own // halves)
        out_shape = [jax.ShapeDtypeStruct((quarters, blocks, 2) + piece, BF16)] * halves
        scratch.append(pltpu.VMEM((halves, quarters) + piece, BF16))
    else:
        out_shape = [
            jax.ShapeDtypeStruct((blocks, co, own), F32),
            jax.ShapeDtypeStruct((blocks, TAP_ROWS, own), F32),
        ]
    return pl.pallas_call(
        functools.partial(weight_kernel, terms, slabs, halves, quarters, last),
        grid_spec=pltpu.PrefetchScalarGridSpec(
            num_scalar_prefetch=1,
            grid=(blocks,),
            in_specs=[WHOLE] * len(args),
            out_specs=[WHOLE] * len(out_shape),
            scratch_shapes=scratch,
        ),
        out_shape=out_shape,
        input_output_aliases={1 + len(args) - len(into) + i: i for i in range(len(into))},
        compiler_params=pltpu.CompilerParams(vmem_limit_bytes=10 * MIB),
        cost_estimate=pl.CostEstimate(
            flops=4 * n * cells * channels * co,
            bytes_accessed=2 * (n + 1) * cells * channels,
            transcendentals=0,
        ),
        name="weight_outer" if last else "weight_middle",
    )(idx, *args)


def feature_kernel(terms, slabs, grain, halves, idx_ref, k_ref, *refs):
    n = len(terms)
    w_refs, g_refs, (out_ref, gd, weight, wide) = refs[:2], refs[2 : 2 + n], refs[2 + n :]
    size = g_refs[0].shape[0] // slabs
    step, blocks = pl.program_id(0), pl.num_programs(0)
    own = weight.shape[1]
    lanes = own // halves
    for h in range(halves):
        at = ((h ^ idx_ref[0] if halves > 1 else 0) * blocks + step) * lanes
        for branch in range(2):
            rows = w_refs[branch][lanes_at(at, lanes), :]
            weight[branch, h * lanes : (h + 1) * lanes, :] = rows
    for t, (branch, _, _) in enumerate(terms):
        gd[t] = back(g_refs[t][...], weight[branch])
    for h in range(halves):
        cols = slice(h * lanes, (h + 1) * lanes)
        for q in range(slabs):
            acc = None
            for t, (_, _, reach) in enumerate(terms):
                for i, side in enumerate(SIDES):
                    if not span(slabs, q, -side, reach):
                        continue
                    src = (q - side * reach) * size
                    term = gd[t, src : src + size, cols] * k_ref[0, 3 * t + i : 3 * t + i + 1, cols]
                    acc = term if acc is None else acc + term
            for g in range(wide.shape[0]):
                wide[g, q * grain : (q + 1) * grain, cols] = acc[g * grain : (g + 1) * grain, :]
    rows = out_ref.shape[1]
    for g in range(wide.shape[0]):
        out_ref[g // rows, g % rows] = wide[g].astype(BF16)


def feature_grads(terms, slabs, grain, halves, idx, shape, k, w, gs):
    images, rows, width, channels = shape
    blocks, _, own = k.shape
    cells, co = gs[0].shape
    n = len(terms)
    args = [*w, *gs]
    return pl.pallas_call(
        functools.partial(feature_kernel, terms, slabs, grain, halves),
        grid_spec=pltpu.PrefetchScalarGridSpec(
            num_scalar_prefetch=1,
            grid=(blocks,),
            in_specs=[pl.BlockSpec((1,) + k.shape[1:], lambda d, s: (d, 0, 0))]
            + [WHOLE] * len(args),
            out_specs=pl.BlockSpec((images, rows, width, own), lambda d, s: (0, 0, 0, s[FIRST + d])),
            scratch_shapes=[
                pltpu.VMEM((n, cells, own), F32),
                pltpu.VMEM((2, own, co), BF16),
                pltpu.VMEM((images * rows, width, own), F32),
            ],
        ),
        out_shape=jax.ShapeDtypeStruct(shape, BF16),
        compiler_params=pltpu.CompilerParams(vmem_limit_bytes=18 * MIB),
        cost_estimate=pl.CostEstimate(
            flops=2 * n * cells * channels * co,
            bytes_accessed=4 * cells * channels,
            transcendentals=0,
        ),
        name="feature_grads",
    )(idx, k, *args)


def turn_kernel(slabs, grain, count, has_out, cot_ref, centre_ref, *refs):
    received, refs = refs[:count], refs[count + has_out :]
    g_ref, out_ref, flat, wide = refs
    n, rows = cot_ref.shape[:2]
    size = n * rows * grain
    for g in range(n * rows):
        line = cot_ref[g // rows, g % rows].astype(F32)
        for q in range(slabs):
            at = q * size + g * grain
            flat[at : at + grain, :] = line[q * grain : (q + 1) * grain, :]
    for q in range(slabs):
        here = slice(q * size, (q + 1) * size)
        pre = centre_ref[here, :]
        parts = [ref[here, :] for ref in received]
        halves = [part for part in parts if part.shape[1] < pre.shape[1]]
        parts = [part for part in parts if part.shape[1] == pre.shape[1]]
        if halves:
            parts.append(jnp.concatenate(halves, axis=1))
        for part in parts:
            pre = pre + part.astype(F32)
        sig = jax.nn.sigmoid(pre)
        g_ref[here, :] = (flat[here, :] * sig * (1.0 + pre * (1.0 - sig))).astype(BF16)
        out = pre * sig
        for g in range(n * rows):
            wide[g, q * grain : (q + 1) * grain, :] = out[g * grain : (g + 1) * grain, :]
    for g in range(n * rows):
        out_ref[g // rows, g % rows] = wide[g].astype(BF16)


def turn(slabs, grain, branch, cotangent, centre, received, outputs):
    n, rows, width, _ = cotangent.shape
    cells, co = centre.shape
    natural = pl.BlockSpec((n, rows, width, co), lambda i: (0, 0, 0, branch))
    has_out = outputs is not None
    args = [cotangent, centre, *received] + ([outputs] if has_out else [])
    specs = [natural] + [WHOLE] * (1 + len(received))
    return pl.pallas_call(
        functools.partial(turn_kernel, slabs, grain, len(received), has_out),
        grid=(1,),
        in_specs=specs + [pl.BlockSpec(memory_space=pl.ANY)] * has_out,
        out_specs=[WHOLE, natural],
        out_shape=[
            jax.ShapeDtypeStruct((cells, co), BF16),
            jax.ShapeDtypeStruct(cotangent.shape, BF16),
        ],
        scratch_shapes=[
            pltpu.VMEM((cells, co), F32),
            pltpu.VMEM((n * rows, width, co), F32),
        ],
        input_output_aliases={len(args) - 1: 1} if has_out else {},
        compiler_params=pltpu.CompilerParams(vmem_limit_bytes=8 * MIB),
        cost_estimate=pl.CostEstimate(
            flops=12 * cells * co, bytes_accessed=8 * cells * co, transcendentals=2 * cells * co
        ),
        name="turn",
    )(*args)


def finish_kernel(factor, quarters, idx_ref, in_ref, *refs):
    w_ref, k_ref, wide, taps_of = refs[-4:]
    co = w_ref.shape[2]
    per, taps = co // quarters, TAP_ROWS // quarters
    for branch in range(2):
        for q in range(quarters):
            at = q ^ idx_ref[1] if quarters > 1 else 0
            block = in_ref[at, branch].astype(F32) * factor
            wide[q * per : (q + 1) * per, :] = block[:per]
            taps_of[q * taps : (q + 1) * taps, :] = block[per:]
        w_ref[branch] = wide[...].T
        for t in range(k_ref.shape[0]):
            k_ref[t, branch : branch + 1, :] = taps_of[t : t + 1, :]


def finish(idx, block, half, halves, own, factor, into=()):
    quarters, _, rows, lanes = block.shape
    co = rows * quarters - TAP_ROWS

    def place(s):
        return s[0] ^ half if halves > 1 else 0

    return pl.pallas_call(
        functools.partial(finish_kernel, factor, quarters),
        grid_spec=pltpu.PrefetchScalarGridSpec(
            num_scalar_prefetch=1,
            grid=(1,),
            in_specs=[pl.BlockSpec(block.shape, lambda i, s: (0, 0, 0, 0))]
            + [pl.BlockSpec(memory_space=pl.ANY)] * len(into),
            out_specs=[
                pl.BlockSpec((2, lanes, co), lambda i, s: (0, place(s), 0)),
                pl.BlockSpec((9, 2, lanes), lambda i, s: (0, 0, place(s))),
            ],
            scratch_shapes=[pltpu.VMEM((co, lanes), F32), pltpu.VMEM((TAP_ROWS, lanes), F32)],
        ),
        out_shape=[
            jax.ShapeDtypeStruct((2, own, co), F32),
            jax.ShapeDtypeStruct((9, 2, own), F32),
        ],
        input_output_aliases={2 + i: i for i in range(len(into))},
        compiler_params=pltpu.CompilerParams(vmem_limit_bytes=8 * MIB),
        name="finish_grads",
    )(idx, block, *into)


def pyramid(features, pointwise, depthwise, cotangent):
    n, rows, width, _ = features.shape
    own, co = pointwise.shape[1:]
    space, dp = lax.axis_size("space"), lax.axis_size("dp")
    me, row = lax.axis_index("space"), lax.axis_index("dp")
    chips = space // 2
    halves = 2 if space % 2 == 0 and own % 256 == 0 and dp % 2 == 0 else 1
    part_c = own // halves
    even = chips & (chips - 1) == 0 and TAP_ROWS % (8 * chips) == 0 and co % (16 * chips) == 0
    quarters = chips if halves == 2 and even else 1
    core, chip = me % 2, me // 2

    grain = math.gcd(*RATES)
    slabs = width // grain

    terms, moves, modes = [], [], []
    flags = [jnp.zeros((), bool)] * (FIRST - FLAGS)
    for branch, rate in enumerate(RATES):
        offset, reach = rate // rows, rate // grain
        group = me // offset
        if 2 * offset == space:
            kinds = [(0, "none"), (DYNAMIC, "swap")]
            flags[0] = group == 1
        elif 4 * offset == space:
            kinds = [(0, "none"), (DYNAMIC + 1, "pair"), (DYNAMIC + 2, "relay")]
            flags[1] = group % 2 == 1
            flags[2] = group % 2 == 0
        else:
            kinds = [(0, "none")] + [(u, "shift") for u in (-1, 1) if offset < space]
        for u, mode in kinds:
            terms.append((branch, u, reach))
            modes.append(mode)
            moves.append(offset)
    middle = [t for t, mode in enumerate(modes) if mode == "none"]
    outer = [t for t, mode in enumerate(modes) if mode != "none"]

    def route(value, t, pairs):
        width_of = moves[t]
        return lax.ppermute(
            value,
            "space",
            [(a * width_of + i, b * width_of + i) for a, b in pairs for i in range(width_of)],
        )

    def send(value, t, direction):
        if modes[t] == "swap":
            return [route(value, t, [(0, 1), (1, 0)])]
        if modes[t] == "pair":
            return [route(value, t, [(0, 1), (1, 0), (2, 3), (3, 2)])]
        if modes[t] == "shift":
            return [shift(value, "space", direction * terms[t][1] * moves[t])]
        cut = value.shape[1] // 2
        one = route(value[:, :cut], t, [(1, 0), (2, 3)])
        two = route(value[:, cut:], t, [(1, 3), (2, 0)])
        one = route(one, t, [(0, 2), (3, 1)])
        two = route(two, t, [(3, 2), (0, 1)])
        return [one, two]

    idx = jnp.concatenate(
        [
            jnp.stack([core, chip, *flags]).astype(jnp.int32),
            (row + dp - jnp.arange(dp)).astype(jnp.int32) % dp,
        ]
    )

    taps = depthwise.transpose(1, 0, 2)
    k_all = [taps] + [cycle(taps, "dp", d) for d in range(1, dp)]
    mine = pointwise
    if halves == 2:
        mine = lax.dynamic_slice_in_dim(pointwise, core * part_c, part_c, axis=1)
    gathered = [None] * 2
    order = (1, 0)
    for b in order:
        gathered[b] = [mine[b]] + [cycle(mine[b], "dp", d) for d in range(1, dp)]

    k_rows = jnp.stack(k_all).astype(F32).transpose(0, 2, 1, 3).reshape(dp, 18, own)
    k_terms = []
    for branch, u, _ in terms:
        at = branch * 9
        if u >= DYNAMIC:
            upper = flags[u - DYNAMIC]
            k_terms.append(jnp.where(upper, k_rows[:, at + 6 : at + 9], k_rows[:, at : at + 3]))
        else:
            k_terms.append(k_rows[:, at + 3 * (u + 1) : at + 3 * (u + 1) + 3])

    taps_all = jnp.concatenate(k_terms, axis=1)
    taps_all = jnp.pad(taps_all, ((0, 0), (0, -taps_all.shape[1] % 8), (0, 0)))

    x, *sums = depthwise_sums(terms, slabs, grain, halves, idx, pltpu.with_memory_space_constraint(features, pltpu.HBM), taps_all)
    held = lax.optimization_barrier
    pick = lambda values, chosen: [values[t] for t in chosen]
    mid = [[t for t in middle if terms[t][0] == b] for b in range(2)]
    out = [[t for t in outer if terms[t][0] == b] for b in range(2)]

    parts, received, outputs, gs = [None] * len(terms), {}, None, [None] * len(terms)
    ws = {h: [None] * 2 for h in range(halves)}
    before = (x, sums)
    for b in order:
        before, gathered[b] = held((before, gathered[b]))
        if b == order[0]:
            x, sums = before
        chosen = out[b]
        count, begun, last_part = len(chosen), None, 0
        ws[0][b] = jnp.concatenate(gathered[b], axis=0)
        if halves == 2:
            ws[1][b] = swap(ws[0][b], "space", 1)
            begun = forward([b] * count, [F32] * count, pick(sums, chosen), {0: ws[0]})
            last_part = 1
        ready = forward(
            [b] * count, [BF16] * count, pick(sums, chosen), {last_part: ws[last_part]}, begun
        )
        for t, part in zip(chosen, ready):
            parts[t] = part
        received[b] = [piece for t in chosen for piece in send(parts[t], t, -1)]
        before = ready
    w = [jnp.concatenate([ws[h][b] for h in range(halves)], axis=0) for b in range(2)]
    chosen = mid[1] + mid[0]
    centre = forward([terms[t][0] for t in chosen], [F32] * 2, pick(sums, chosen), ws)
    for t, part in zip(chosen, centre):
        parts[t] = part

    common = (slabs, halves, quarters, dp, idx, x)
    first = [None] * 2
    for b in order:
        t = mid[b][0]
        if b == order[1]:
            received[b], first[order[0]] = held((received[b], first[order[0]]))
        gs[t], outputs = turn(slabs, grain, b, cotangent, parts[t], received[b], outputs)
        for o in out[b]:
            gs[o] = send(gs[t], o, 1)
        first[b] = weight_grads(
            pick(terms, mid[b]), *common, w[b], pick(gs, mid[b]), pick(sums, mid[b])
        )
    grads = ()
    for b in order:
        grad_g = [jnp.concatenate(gs[t], axis=1) for t in out[b]]
        if b == order[0]:
            grad_g, first[order[1]] = held((grad_g, first[order[1]]))
        else:
            grad_g, grads = held((grad_g, grads))
        for t, field in zip(out[b], grad_g):
            gs[t] = field
        grads = weight_grads(
            pick(terms, out[b]), *common, w[b], grad_g, pick(sums, out[b]), first[b], grads
        )
    kept = grads[0]
    if halves == 2:
        kept = (kept.astype(F32) + swap(grads[1], "space", 1).astype(F32)).astype(BF16)
    pieces = [kept[e] for e in range(quarters)]
    gs, pieces = held((gs, pieces))
    summed = [pieces[0]] + [swap(pieces[e], "space", 2 * e) for e in range(1, quarters)]
    feature_grad = feature_grads(terms, slabs, grain, halves, idx, features.shape, taps_all, w, gs)

    factor = 1.0 / math.sqrt(dp * n * space * rows * width)
    total = sum(piece.astype(F32) for piece in summed).astype(BF16)
    mine = total[0].astype(F32)
    for d in range(1, dp):
        mine = mine + cycle(total[d], "dp", -d).astype(F32)
    if quarters > 1:
        mine = mine.astype(BF16)
        block = jnp.stack([mine] + [swap(mine, "space", 2 * e) for e in range(1, quarters)])
    else:
        peers = [[i for i in range(space) if i % halves == c] for c in range(halves)]
        block = lax.psum(mine, "space", axis_index_groups=peers)[None]
    if halves == 2:
        other = swap(block, "space", 1)
    done = finish(idx, block, 0, halves, own, factor)
    if halves == 2:
        done = finish(idx, other, 1, halves, own, factor, done)
    pointwise_grad, depthwise_grad = done[0], done[1].transpose(1, 0, 2)
    return outputs, feature_grad, pointwise_grad, depthwise_grad


def solution(mesh):
    return jax.shard_map(
        pyramid,
        mesh=mesh,
        in_specs=(
            P("dp", "space", None, None),
            P(None, "dp", None),
            P(None, None, "dp"),
            P("dp", "space", None, None),
        ),
        out_specs=(
            P("dp", "space", None, None),
            P("dp", "space", None, None),
            P(None, "dp", None),
            P(None, None, "dp"),
        ),
        check_vma=False,
    )
```

```python
import functools
import math

import jax
import jax.numpy as jnp
from jax import lax
from jax.experimental import pallas as pl
from jax.experimental.pallas import tpu as pltpu
from jax.sharding import PartitionSpec as P


RATES = (12, 24)
SIDES = (-1, 0, 1)
F32 = jnp.float32
BF16 = jnp.bfloat16
TAP_ROWS = 32
MIB = 1 << 20
FLAGS, FIRST = 2, 5
DYNAMIC = 10


def shift(value, axis, steps):
    count = lax.axis_size(axis)
    first, last = max(0, -steps), min(count, count - steps)
    return lax.ppermute(value, axis, [(i, i + steps) for i in range(first, last)])


def cycle(value, axis, steps):
    count = lax.axis_size(axis)
    return lax.ppermute(value, axis, [(i, (i + steps) % count) for i in range(count)])


def swap(value, axis, mask):
    count = lax.axis_size(axis)
    return lax.ppermute(value, axis, [(i, i ^ mask) for i in range(count)])


def span(slabs, q, side, reach):
    return 0 <= q + side * reach < slabs


WHOLE = pl.BlockSpec(memory_space=pltpu.VMEM)


def lanes_at(start, count):
    return pl.ds(start if isinstance(start, int) else pl.multiple_of(start, count), count)


def sums_kernel(terms, slabs, grain, halves, idx_ref, x_ref, k_ref, xs_ref, *refs):
    outs, wide = refs[: len(terms)], refs[len(terms)]
    n, rows = x_ref.shape[:2]
    size = n * rows * grain
    step, blocks = pl.program_id(0), pl.num_programs(0)
    lanes = x_ref.shape[3] // halves
    for g in range(n * rows):
        line = x_ref[g // rows, g % rows].astype(F32)
        for q in range(slabs):
            at = q * size + g * grain
            wide[at : at + grain, :] = line[q * grain : (q + 1) * grain, :]
    tile = 16 if size % 16 == 0 else 8
    for h in range(halves):
        start = (h ^ idx_ref[0]) * lanes if halves > 1 else 0
        for strip in range(lanes // 128):
            src = lanes_at(start + strip * 128, 128)
            dst = lanes_at((h * blocks + step) * lanes + strip * 128, 128)
            taps = [k_ref[0, r : r + 1, src] for r in range(3 * len(terms))]
            for q in range(slabs):
                for row in range(0, size, tile):
                    here = slice(q * size + row, q * size + row + tile)
                    near = {}
                    for t, (_, _, reach) in enumerate(terms):
                        total = None
                        for i, side in enumerate(SIDES):
                            if not span(slabs, q, side, reach):
                                continue
                            far = side * reach
                            if far not in near:
                                at = (q + far) * size + row
                                near[far] = wide[at : at + tile, src]
                            term = near[far] * taps[3 * t + i]
                            total = term if total is None else total + term
                        outs[t][here, dst] = total.astype(BF16)
                    xs_ref[here, dst] = near[0].astype(BF16)


def depthwise_sums(terms, slabs, grain, halves, idx, x, k):
    n, rows, width, channels = x.shape
    cells, (blocks, _, own) = n * rows * width, k.shape
    return pl.pallas_call(
        functools.partial(sums_kernel, terms, slabs, grain, halves),
        grid_spec=pltpu.PrefetchScalarGridSpec(
            num_scalar_prefetch=1,
            grid=(blocks,),
            in_specs=[
                pl.BlockSpec((n, rows, width, own), lambda d, s: (0, 0, 0, s[FIRST + d])),
                pl.BlockSpec((1, k.shape[1], own), lambda d, s: (d, 0, 0)),
            ],
            out_specs=[WHOLE] * (1 + len(terms)),
            scratch_shapes=[pltpu.VMEM((cells, own), F32)],
        ),
        out_shape=[jax.ShapeDtypeStruct((cells, channels), BF16)] * (1 + len(terms)),
        compiler_params=pltpu.CompilerParams(vmem_limit_bytes=8 * MIB),
        cost_estimate=pl.CostEstimate(
            flops=6 * len(terms) * cells * channels,
            bytes_accessed=2 * (2 + len(terms)) * cells * channels,
            transcendentals=0,
        ),
        name="depthwise_sums",
    )(idx, x, k)


def forward_kernel(branches, parts, add, *refs):
    n = len(branches)
    count = len(parts) * len(set(branches))
    all_refs, refs = refs[:count], refs[count:]
    for t, branch in enumerate(branches):
        total = refs[n + t][...] if add else None
        at = sorted(set(branches)).index(branch) * len(parts)
        for w_ref, h in zip(all_refs[at : at + len(parts)], parts):
            depth = w_ref.shape[0]
            field = refs[t][:, h * depth : (h + 1) * depth]
            part = jnp.dot(field, w_ref[...], preferred_element_type=F32)
            total = part if total is None else total + part
        out = refs[len(refs) - n + t]
        out[...] = total.astype(out.dtype)


def forward(branches, dtypes, sums, ws, before=None):
    cells = sums[0].shape[0]
    used = [ws[h][b] for b in sorted(set(branches)) for h in ws]
    depth, co = used[0].shape
    args = [*used, *sums, *(before or [])]
    return pl.pallas_call(
        functools.partial(forward_kernel, branches, tuple(ws), before is not None),
        in_specs=[WHOLE] * len(args),
        out_specs=[WHOLE] * len(sums),
        out_shape=[jax.ShapeDtypeStruct((cells, co), dt) for dt in dtypes],
        compiler_params=pltpu.CompilerParams(vmem_limit_bytes=8 * MIB),
        cost_estimate=pl.CostEstimate(
            flops=2 * len(sums) * cells * depth * len(ws) * co,
            bytes_accessed=2 * len(sums) * cells * depth * len(ws),
            transcendentals=0,
        ),
        name="forward_terms",
    )(*args)


def back(g, weight):
    return lax.dot_general(g, weight, (((1,), (1,)), ((), ())), preferred_element_type=F32)


def weight_kernel(terms, slabs, halves, quarters, last, idx_ref, x_ref, w_ref, *refs):
    n = len(terms)
    g_refs, d_refs, refs = refs[:n], refs[n : 2 * n], refs[2 * n :]
    if last:
        w_before, k_before, *outs, gt, gd, kacc, pieces = refs
        outs = outs[-halves:]
    else:
        w_out, k_out, gt, gd, kacc = refs
    step, blocks = pl.program_id(0), pl.num_programs(0)
    own, co = kacc.shape[1], w_ref.shape[1]
    size = g_refs[0].shape[0] // slabs
    lanes = own // halves
    block = lanes_at(step * own, own)

    @pl.when(step == 0)
    def _():
        for t in range(n):
            gt[t] = g_refs[t][...].T

    for t in range(n):
        gd[t] = back(g_refs[t][...], w_ref[block, :]).astype(gd.dtype)
    total = w_before[step] if last else None
    for t in range(n):
        part = jnp.dot(gt[t], d_refs[t][:, block], preferred_element_type=F32)
        total = part if total is None else total + part
    per = co // quarters
    if last:
        for h in range(halves):
            for q in range(quarters):
                rows = total[q * per : (q + 1) * per, h * lanes : (h + 1) * lanes]
                pieces[h, q, :per, :] = rows.astype(BF16)
    else:
        w_out[step] = total
    kacc[...] = k_before[step] if last else jnp.zeros_like(kacc)
    for h in range(halves):
        cols = slice(h * lanes, (h + 1) * lanes)
        there = lanes_at(step * own + h * lanes, lanes)
        sums = [None] * (3 * n)
        for q in range(slabs):
            xq = x_ref[q * size : (q + 1) * size, there].astype(F32)
            for t, (_, _, reach) in enumerate(terms):
                for i, side in enumerate(SIDES):
                    if not span(slabs, q, -side, reach):
                        continue
                    src = (q - side * reach) * size
                    part = xq * gd[t, src : src + size, cols].astype(F32)
                    part = jnp.sum(part.reshape(size // 8, 8, lanes), axis=0)
                    at = 3 * t + i
                    sums[at] = part if sums[at] is None else sums[at] + part
        for t, (_, u, _) in enumerate(terms):
            for i in range(3):
                total = jnp.sum(sums[3 * t + i], axis=0, keepdims=True)
                if u >= DYNAMIC:
                    upper = idx_ref[FLAGS + u - DYNAMIC] > 0
                    kacc[i : i + 1, cols] += jnp.where(upper, 0.0, total)
                    kacc[i + 6 : i + 7, cols] += jnp.where(upper, total, 0.0)
                else:
                    row = 3 * (u + 1) + i
                    kacc[row : row + 1, cols] += total
    if not last:
        k_out[step] = kacc[...]
        return
    taps = TAP_ROWS // quarters
    for h in range(halves):
        for q in range(quarters):
            rows = kacc[q * taps : (q + 1) * taps, h * lanes : (h + 1) * lanes]
            pieces[h, q, per:, :] = rows.astype(BF16)

    def put(out, which):
        for e in range(quarters):
            at = e ^ idx_ref[1] if quarters > 1 else 0
            for h in range(halves):
                out[e, (step - which * (blocks // halves)) * halves + h, terms[0][0]] = pieces[h, at]

    for which in range(halves):
        mine = step // (blocks // halves) == which
        pl.when(mine)(functools.partial(put, outs[which], which))


def weight_grads(terms, slabs, halves, quarters, blocks, idx, x, w, gs, ds, before=None, into=()):
    cells, channels = x.shape
    own, co = channels // blocks, w.shape[1]
    n = len(terms)
    last = before is not None
    args = [x, w, *gs, *ds, *(before or ()), *into]
    held_as = BF16 if cells // slabs % 16 == 0 else F32
    scratch = [
        pltpu.VMEM((n, co, cells), BF16),
        pltpu.VMEM((n, cells, own), held_as),
        pltpu.VMEM((TAP_ROWS, own), F32),
    ]
    if last:
        piece = ((co + TAP_ROWS) // quarters, own // halves)
        out_shape = [jax.ShapeDtypeStruct((quarters, blocks, 2) + piece, BF16)] * halves
        scratch.append(pltpu.VMEM((halves, quarters) + piece, BF16))
    else:
        out_shape = [
            jax.ShapeDtypeStruct((blocks, co, own), F32),
            jax.ShapeDtypeStruct((blocks, TAP_ROWS, own), F32),
        ]
    return pl.pallas_call(
        functools.partial(weight_kernel, terms, slabs, halves, quarters, last),
        grid_spec=pltpu.PrefetchScalarGridSpec(
            num_scalar_prefetch=1,
            grid=(blocks,),
            in_specs=[WHOLE] * len(args),
            out_specs=[WHOLE] * len(out_shape),
            scratch_shapes=scratch,
        ),
        out_shape=out_shape,
        input_output_aliases={1 + len(args) - len(into) + i: i for i in range(len(into))},
        compiler_params=pltpu.CompilerParams(vmem_limit_bytes=10 * MIB),
        cost_estimate=pl.CostEstimate(
            flops=4 * n * cells * channels * co,
            bytes_accessed=2 * (n + 1) * cells * channels,
            transcendentals=0,
        ),
        name="weight_outer" if last else "weight_middle",
    )(idx, *args)


def feature_kernel(terms, slabs, grain, halves, idx_ref, k_ref, *refs):
    n = len(terms)
    w_refs, g_refs, (out_ref, gd, weight, wide) = refs[:2], refs[2 : 2 + n], refs[2 + n :]
    size = g_refs[0].shape[0] // slabs
    step, blocks = pl.program_id(0), pl.num_programs(0)
    own = weight.shape[1]
    lanes = own // halves
    for h in range(halves):
        at = ((h ^ idx_ref[0] if halves > 1 else 0) * blocks + step) * lanes
        for branch in range(2):
            rows = w_refs[branch][lanes_at(at, lanes), :]
            weight[branch, h * lanes : (h + 1) * lanes, :] = rows
    for t, (branch, _, _) in enumerate(terms):
        gd[t] = back(g_refs[t][...], weight[branch])
    for h in range(halves):
        cols = slice(h * lanes, (h + 1) * lanes)
        for q in range(slabs):
            acc = None
            for t, (_, _, reach) in enumerate(terms):
                for i, side in enumerate(SIDES):
                    if not span(slabs, q, -side, reach):
                        continue
                    src = (q - side * reach) * size
                    term = gd[t, src : src + size, cols] * k_ref[0, 3 * t + i : 3 * t + i + 1, cols]
                    acc = term if acc is None else acc + term
            for g in range(wide.shape[0]):
                wide[g, q * grain : (q + 1) * grain, cols] = acc[g * grain : (g + 1) * grain, :]
    rows = out_ref.shape[1]
    for g in range(wide.shape[0]):
        out_ref[g // rows, g % rows] = wide[g].astype(BF16)


def feature_grads(terms, slabs, grain, halves, idx, shape, k, w, gs):
    images, rows, width, channels = shape
    blocks, _, own = k.shape
    cells, co = gs[0].shape
    n = len(terms)
    args = [*w, *gs]
    return pl.pallas_call(
        functools.partial(feature_kernel, terms, slabs, grain, halves),
        grid_spec=pltpu.PrefetchScalarGridSpec(
            num_scalar_prefetch=1,
            grid=(blocks,),
            in_specs=[pl.BlockSpec((1,) + k.shape[1:], lambda d, s: (d, 0, 0))]
            + [WHOLE] * len(args),
            out_specs=pl.BlockSpec((images, rows, width, own), lambda d, s: (0, 0, 0, s[FIRST + d])),
            scratch_shapes=[
                pltpu.VMEM((n, cells, own), F32),
                pltpu.VMEM((2, own, co), BF16),
                pltpu.VMEM((images * rows, width, own), F32),
            ],
        ),
        out_shape=jax.ShapeDtypeStruct(shape, BF16),
        compiler_params=pltpu.CompilerParams(vmem_limit_bytes=18 * MIB),
        cost_estimate=pl.CostEstimate(
            flops=2 * n * cells * channels * co,
            bytes_accessed=4 * cells * channels,
            transcendentals=0,
        ),
        name="feature_grads",
    )(idx, k, *args)


def turn_kernel(slabs, grain, count, has_out, cot_ref, centre_ref, *refs):
    received, refs = refs[:count], refs[count + has_out :]
    g_ref, out_ref, flat, wide = refs
    n, rows = cot_ref.shape[:2]
    size = n * rows * grain
    for g in range(n * rows):
        line = cot_ref[g // rows, g % rows].astype(F32)
        for q in range(slabs):
            at = q * size + g * grain
            flat[at : at + grain, :] = line[q * grain : (q + 1) * grain, :]
    for q in range(slabs):
        here = slice(q * size, (q + 1) * size)
        pre = centre_ref[here, :]
        parts = [ref[here, :] for ref in received]
        halves = [part for part in parts if part.shape[1] < pre.shape[1]]
        parts = [part for part in parts if part.shape[1] == pre.shape[1]]
        if halves:
            parts.append(jnp.concatenate(halves, axis=1))
        for part in parts:
            pre = pre + part.astype(F32)
        sig = jax.nn.sigmoid(pre)
        g_ref[here, :] = (flat[here, :] * sig * (1.0 + pre * (1.0 - sig))).astype(BF16)
        out = pre * sig
        for g in range(n * rows):
            wide[g, q * grain : (q + 1) * grain, :] = out[g * grain : (g + 1) * grain, :]
    for g in range(n * rows):
        out_ref[g // rows, g % rows] = wide[g].astype(BF16)


def turn(slabs, grain, branch, cotangent, centre, received, outputs):
    n, rows, width, _ = cotangent.shape
    cells, co = centre.shape
    natural = pl.BlockSpec((n, rows, width, co), lambda i: (0, 0, 0, branch))
    has_out = outputs is not None
    args = [cotangent, centre, *received] + ([outputs] if has_out else [])
    specs = [natural] + [WHOLE] * (1 + len(received))
    return pl.pallas_call(
        functools.partial(turn_kernel, slabs, grain, len(received), has_out),
        grid=(1,),
        in_specs=specs + [pl.BlockSpec(memory_space=pl.ANY)] * has_out,
        out_specs=[WHOLE, natural],
        out_shape=[
            jax.ShapeDtypeStruct((cells, co), BF16),
            jax.ShapeDtypeStruct(cotangent.shape, BF16),
        ],
        scratch_shapes=[
            pltpu.VMEM((cells, co), F32),
            pltpu.VMEM((n * rows, width, co), F32),
        ],
        input_output_aliases={len(args) - 1: 1} if has_out else {},
        compiler_params=pltpu.CompilerParams(vmem_limit_bytes=8 * MIB),
        cost_estimate=pl.CostEstimate(
            flops=12 * cells * co, bytes_accessed=8 * cells * co, transcendentals=2 * cells * co
        ),
        name="turn",
    )(*args)


def finish_kernel(factor, quarters, idx_ref, in_ref, *refs):
    w_ref, k_ref, wide, taps_of = refs[-4:]
    co = w_ref.shape[2]
    per, taps = co // quarters, TAP_ROWS // quarters
    for branch in range(2):
        for q in range(quarters):
            at = q ^ idx_ref[1] if quarters > 1 else 0
            block = in_ref[at, branch].astype(F32) * factor
            wide[q * per : (q + 1) * per, :] = block[:per]
            taps_of[q * taps : (q + 1) * taps, :] = block[per:]
        w_ref[branch] = wide[...].T
        for t in range(k_ref.shape[0]):
            k_ref[t, branch : branch + 1, :] = taps_of[t : t + 1, :]


def finish(idx, block, half, halves, own, factor, into=()):
    quarters, _, rows, lanes = block.shape
    co = rows * quarters - TAP_ROWS

    def place(s):
        return s[0] ^ half if halves > 1 else 0

    return pl.pallas_call(
        functools.partial(finish_kernel, factor, quarters),
        grid_spec=pltpu.PrefetchScalarGridSpec(
            num_scalar_prefetch=1,
            grid=(1,),
            in_specs=[pl.BlockSpec(block.shape, lambda i, s: (0, 0, 0, 0))]
            + [pl.BlockSpec(memory_space=pl.ANY)] * len(into),
            out_specs=[
                pl.BlockSpec((2, lanes, co), lambda i, s: (0, place(s), 0)),
                pl.BlockSpec((9, 2, lanes), lambda i, s: (0, 0, place(s))),
            ],
            scratch_shapes=[pltpu.VMEM((co, lanes), F32), pltpu.VMEM((TAP_ROWS, lanes), F32)],
        ),
        out_shape=[
            jax.ShapeDtypeStruct((2, own, co), F32),
            jax.ShapeDtypeStruct((9, 2, own), F32),
        ],
        input_output_aliases={2 + i: i for i in range(len(into))},
        compiler_params=pltpu.CompilerParams(vmem_limit_bytes=8 * MIB),
        name="finish_grads",
    )(idx, block, *into)


def pyramid(features, pointwise, depthwise, cotangent):
    n, rows, width, _ = features.shape
    own, co = pointwise.shape[1:]
    space, dp = lax.axis_size("space"), lax.axis_size("dp")
    me, row = lax.axis_index("space"), lax.axis_index("dp")
    chips = space // 2
    halves = 2 if space % 2 == 0 and own % 256 == 0 and dp % 2 == 0 else 1
    part_c = own // halves
    even = chips & (chips - 1) == 0 and TAP_ROWS % (8 * chips) == 0 and co % (16 * chips) == 0
    quarters = chips if halves == 2 and even else 1
    core, chip = me % 2, me // 2

    grain = math.gcd(*RATES)
    slabs = width // grain

    terms, moves, modes = [], [], []
    flags = [jnp.zeros((), bool)] * (FIRST - FLAGS)
    for branch, rate in enumerate(RATES):
        offset, reach = rate // rows, rate // grain
        group = me // offset
        if 2 * offset == space:
            kinds = [(0, "none"), (DYNAMIC, "swap")]
            flags[0] = group == 1
        elif 4 * offset == space:
            kinds = [(0, "none"), (DYNAMIC + 1, "pair"), (DYNAMIC + 2, "relay")]
            flags[1] = group % 2 == 1
            flags[2] = group % 2 == 0
        else:
            kinds = [(0, "none")] + [(u, "shift") for u in (-1, 1) if offset < space]
        for u, mode in kinds:
            terms.append((branch, u, reach))
            modes.append(mode)
            moves.append(offset)
    middle = [t for t, mode in enumerate(modes) if mode == "none"]
    outer = [t for t, mode in enumerate(modes) if mode != "none"]

    def route(value, t, pairs):
        width_of = moves[t]
        return lax.ppermute(
            value,
            "space",
            [(a * width_of + i, b * width_of + i) for a, b in pairs for i in range(width_of)],
        )

    def send(value, t, direction):
        if modes[t] == "swap":
            return [route(value, t, [(0, 1), (1, 0)])]
        if modes[t] == "pair":
            return [route(value, t, [(0, 1), (1, 0), (2, 3), (3, 2)])]
        if modes[t] == "shift":
            return [shift(value, "space", direction * terms[t][1] * moves[t])]
        cut = value.shape[1] // 2
        one = route(value[:, :cut], t, [(1, 0), (2, 3)])
        two = route(value[:, cut:], t, [(1, 3), (2, 0)])
        one = route(one, t, [(0, 2), (3, 1)])
        two = route(two, t, [(3, 2), (0, 1)])
        return [one, two]

    idx = jnp.concatenate(
        [
            jnp.stack([core, chip, *flags]).astype(jnp.int32),
            (row + dp - jnp.arange(dp)).astype(jnp.int32) % dp,
        ]
    )

    taps = depthwise.transpose(1, 0, 2)
    k_all = [taps] + [cycle(taps, "dp", d) for d in range(1, dp)]
    mine = pointwise
    if halves == 2:
        mine = lax.dynamic_slice_in_dim(pointwise, core * part_c, part_c, axis=1)
    gathered = [None] * 2
    order = (1, 0)
    for b in order:
        gathered[b] = [mine[b]] + [cycle(mine[b], "dp", d) for d in range(1, dp)]

    k_rows = jnp.stack(k_all).astype(F32).transpose(0, 2, 1, 3).reshape(dp, 18, own)
    k_terms = []
    for branch, u, _ in terms:
        at = branch * 9
        if u >= DYNAMIC:
            upper = flags[u - DYNAMIC]
            k_terms.append(jnp.where(upper, k_rows[:, at + 6 : at + 9], k_rows[:, at : at + 3]))
        else:
            k_terms.append(k_rows[:, at + 3 * (u + 1) : at + 3 * (u + 1) + 3])

    taps_all = jnp.concatenate(k_terms, axis=1)
    taps_all = jnp.pad(taps_all, ((0, 0), (0, -taps_all.shape[1] % 8), (0, 0)))

    x, *sums = depthwise_sums(terms, slabs, grain, halves, idx, pltpu.with_memory_space_constraint(features, pltpu.HBM), taps_all)
    held = lax.optimization_barrier
    pick = lambda values, chosen: [values[t] for t in chosen]
    mid = [[t for t in middle if terms[t][0] == b] for b in range(2)]
    out = [[t for t in outer if terms[t][0] == b] for b in range(2)]

    parts, received, outputs, gs = [None] * len(terms), {}, None, [None] * len(terms)
    ws = {h: [None] * 2 for h in range(halves)}
    before = (x, sums)
    for b in order:
        before, gathered[b] = held((before, gathered[b]))
        if b == order[0]:
            x, sums = before
        chosen = out[b]
        count, begun, last_part = len(chosen), None, 0
        ws[0][b] = jnp.concatenate(gathered[b], axis=0)
        if halves == 2:
            ws[1][b] = swap(ws[0][b], "space", 1)
            begun = forward([b] * count, [F32] * count, pick(sums, chosen), {0: ws[0]})
            last_part = 1
        ready = forward(
            [b] * count, [BF16] * count, pick(sums, chosen), {last_part: ws[last_part]}, begun
        )
        for t, part in zip(chosen, ready):
            parts[t] = part
        received[b] = [piece for t in chosen for piece in send(parts[t], t, -1)]
        before = ready
    w = [jnp.concatenate([ws[h][b] for h in range(halves)], axis=0) for b in range(2)]
    chosen = mid[1] + mid[0]
    centre = forward([terms[t][0] for t in chosen], [F32] * 2, pick(sums, chosen), ws)
    for t, part in zip(chosen, centre):
        parts[t] = part

    common = (slabs, halves, quarters, dp, idx, x)
    first = [None] * 2
    for b in order:
        t = mid[b][0]
        if b == order[1]:
            received[b], first[order[0]] = held((received[b], first[order[0]]))
        gs[t], outputs = turn(slabs, grain, b, cotangent, parts[t], received[b], outputs)
        for o in out[b]:
            gs[o] = send(gs[t], o, 1)
        first[b] = weight_grads(
            pick(terms, mid[b]), *common, w[b], pick(gs, mid[b]), pick(sums, mid[b])
        )
    grads = ()
    for b in order:
        grad_g = [jnp.concatenate(gs[t], axis=1) for t in out[b]]
        if b == order[0]:
            grad_g, first[order[1]] = held((grad_g, first[order[1]]))
        else:
            grad_g, grads = held((grad_g, grads))
        for t, field in zip(out[b], grad_g):
            gs[t] = field
        grads = weight_grads(
            pick(terms, out[b]), *common, w[b], grad_g, pick(sums, out[b]), first[b], grads
        )
    kept = grads[0]
    if halves == 2:
        kept = (kept.astype(F32) + swap(grads[1], "space", 1).astype(F32)).astype(BF16)
    pieces = [kept[e] for e in range(quarters)]
    gs, pieces = held((gs, pieces))
    summed = [pieces[0]] + [swap(pieces[e], "space", 2 * e) for e in range(1, quarters)]
    feature_grad = feature_grads(terms, slabs, grain, halves, idx, features.shape, taps_all, w, gs)

    factor = 1.0 / math.sqrt(dp * n * space * rows * width)
    total = sum(piece.astype(F32) for piece in summed).astype(BF16)
    mine = total[0].astype(F32)
    for d in range(1, dp):
        mine = mine + cycle(total[d], "dp", -d).astype(F32)
    if quarters > 1:
        mine = mine.astype(BF16)
        block = jnp.stack([mine] + [swap(mine, "space", 2 * e) for e in range(1, quarters)])
    else:
        peers = [[i for i in range(space) if i % halves == c] for c in range(halves)]
        block = lax.psum(mine, "space", axis_index_groups=peers)[None]
    if halves == 2:
        other = swap(block, "space", 1)
    done = finish(idx, block, 0, halves, own, factor)
    if halves == 2:
        done = finish(idx, other, 1, halves, own, factor, done)
    pointwise_grad, depthwise_grad = done[0], done[1].transpose(1, 0, 2)
    return outputs, feature_grad, pointwise_grad, depthwise_grad


def solution(mesh):
    return jax.shard_map(
        pyramid,
        mesh=mesh,
        in_specs=(
            P("dp", "space", None, None),
            P(None, "dp", None),
            P(None, None, "dp"),
            P("dp", "space", None, None),
        ),
        out_specs=(
            P("dp", "space", None, None),
            P("dp", "space", None, None),
            P(None, "dp", None),
            P(None, None, "dp"),
        ),
        check_vma=False,
    )
```
